32 devices in a mesh: groups: 2 (over y), context: 4 (over x, core), tensor: 4 (over z).
Axes of the slice: x: 2, y: 2, z: 4, core: 2. Of those that a mesh axis runs over, the one named last changes fastest.
Arguments:
- tokens: bfloat16 [4096, 4096], P(('groups', 'context', 'tensor')), parts along dimension 0, may hold values from -1000 to 1000
- norm_gain: bfloat16 [4096], replicated, may hold values from 0.099609375 to 1.8984375
- w_in: bfloat16 [4096, 3, 4096], P('context', None, 'tensor'), may hold values from -0.09375 to 0.09375
- short_filter: float32 [3, 3, 4096], P(None, None, 'tensor'), may hold values from -3.6 to 3.6
- medium_filter: float32 [128, 4096], P(None, 'tensor'), may hold values from -0.9 to 0.9
- decay: float32 [4096], P('tensor'), may hold values from 0.004 to 0.12
- w_out: bfloat16 [4096, 4096], P('context', 'tensor'), may hold values from -0.09375 to 0.09375
Outputs:
- mixer_out: bfloat16 [4096, 4096], P(('groups', 'context', 'tensor')), parts along dimension 0
The draws below stay inside these ranges and needn't reach their ends.
There are 2 independent parts, one for each index of `groups`. The reference program is written for one: setup_inputs(seed, part) draws one part's arguments, and reference() takes and returns one part's arrays. A program takes and returns all parts, laid end to end along the dimension named above; an argument that names none is the same for every part. Nothing has to cross between parts.
All inputs are finite; a program needn't handle non-finite values.
Results may differ from the reference program's by a relative error of at most 0.01.
Values may be sent and summed in bfloat16 or wider, within the bound.
No kernel may reach another device: no remote copies, remote signals or barrier semaphores. Data moves between devices by JAX's collectives and lax.ppermute only.
A program may use at most 128 MiB of HBM per device.

```python
import math
import jax
import jax.numpy as jnp
from jax import lax

D = 4096
CH = 4096
SHORT = 3
MEDIUM = 128
TOKENS = 2048
N_TENSOR = 4


def draw_tokens(key, part):
    first, second, third = jax.random.split(key, 3)
    base = jax.random.truncated_normal(first, -4.0, 4.0, (TOKENS, D), jnp.float32)
    row_scale = jnp.exp(jax.random.uniform(second, (TOKENS, 1), jnp.float32, 0.0, math.log(10.0)))
    col_scale = jnp.exp(jax.random.uniform(third, (1, D), jnp.float32, 0.0, math.log(10.0)))
    return (base * row_scale * col_scale).astype(jnp.bfloat16)


def shard_levels(stream_key, shape, pieces, low, top_value):
    def one(axis_at, shards_of):
        steps = jax.random.uniform(jax.random.fold_in(jax.random.fold_in(stream_key, 6), axis_at), (shards_of,), jnp.float32, low / len(pieces), top_value / len(pieces))
        return jnp.repeat(jnp.exp(steps), shape[axis_at] // shards_of).reshape((-1,) + (1,) * (len(shape) - axis_at - 1))

    loudness = one(*pieces[0])
    for cut in pieces[1:]:
        loudness = loudness * one(*cut)
    return loudness


def noise(stream_key, shape, deviation, limit, cuts=(), kind=jnp.bfloat16):
    values = jax.random.normal(stream_key, shape, jnp.float32) * deviation
    if len(cuts) > 0:
        values = shard_levels(stream_key, shape, cuts, -0.22, 0.18) * values
    return jnp.clip(values, min=-limit, max=limit).astype(kind)


def setup_inputs(seed: int = 0, part: int = 0) -> dict:
    splits = jax.random.split(jax.random.key(seed), 8)
    part_splits = jax.random.split(jax.random.fold_in(splits[7], part), 8)
    tokens = draw_tokens(jax.random.fold_in(jax.random.fold_in(splits[7], part), 71), part)
    norm_gain = jnp.clip(1.0 + 0.18 * jax.random.normal(splits[1], (D,), jnp.float32), 0.099609375, 1.8984375).astype(jnp.bfloat16)
    w_in = noise(splits[2], (D, 3, CH), D ** -0.5, 0.09375, ((0, 4), (2, 4)))
    short_filter = noise(splits[3], (SHORT, 3, CH), 0.6, 3.6, ((2, 4),), jnp.float32)
    medium_filter = noise(splits[4], (MEDIUM, CH), 0.15, 0.9, ((1, 4),), jnp.float32)
    decay = jnp.clip(jnp.exp(math.log(0.12) - 3.4011973 * jax.random.uniform(splits[5], (CH,), jnp.float32) ** shard_levels(splits[5], (CH,), ((0, 4),), -0.2, 0.2)), 0.004, 0.12)
    w_out = noise(splits[6], (D, CH), CH ** -0.5, 0.09375, ((0, 4), (1, 4)))
    return dict(tokens=tokens, norm_gain=norm_gain, w_in=w_in, short_filter=short_filter, medium_filter=medium_filter, decay=decay, w_out=w_out)


norm_epsilon = 1e-06

def reference(tokens, norm_gain, w_in, short_filter, medium_filter, decay, w_out):
    values = tokens.astype(jnp.float32)
    inverse_rms = lax.rsqrt(lax.optimization_barrier(jnp.mean(values * values, axis=1, keepdims=True)) + norm_epsilon)
    normed = (values * inverse_rms * norm_gain.astype(jnp.float32)[None, :]).astype(jnp.bfloat16)
    projected = jnp.dot(normed, w_in.reshape(D, 3 * CH), preferred_element_type=jnp.float32)
    projected = projected.astype(jnp.bfloat16).reshape(TOKENS, 3, CH)
    padded = jnp.concatenate([jnp.zeros((SHORT - 1, 3, CH), jnp.float32), projected.astype(jnp.float32)], axis=0)
    featured = jnp.zeros((TOKENS, 3, CH), jnp.float32)
    for lag in range(SHORT):
        featured = featured + short_filter[lag][None] * padded[SHORT - 1 - lag:SHORT - 1 - lag + TOKENS]
    gated = (featured[:, 1] * featured[:, 2]).astype(jnp.bfloat16)
    lag_index = jnp.arange(MEDIUM, dtype=jnp.float32)
    medium_taps = (medium_filter * jnp.exp(-decay[None, :] * lag_index[:, None])).astype(jnp.bfloat16)
    taps_wide = medium_taps.astype(jnp.float32)
    gated_pad = jnp.concatenate([jnp.zeros((MEDIUM - 1, CH), jnp.float32), gated.astype(jnp.float32)], axis=0)

    def add_tap(lag, total):
        shifted = lax.dynamic_slice_in_dim(gated_pad, (MEDIUM - 1 - lag).astype(jnp.int32), TOKENS, 0)
        weights = lax.dynamic_slice_in_dim(taps_wide, lag.astype(jnp.int32), 1, 0)
        return total + weights * shifted
    mixed = lax.fori_loop(0, MEDIUM, add_tap, jnp.zeros((TOKENS, CH), jnp.float32))
    combined = (featured[:, 0] * mixed).astype(jnp.bfloat16)
    group_width = CH // N_TENSOR
    combined_groups = combined.reshape(TOKENS, N_TENSOR, group_width)
    out_groups = w_out.reshape(D, N_TENSOR, group_width)

    def add_group(group, total):
        left = lax.dynamic_index_in_dim(combined_groups, group.astype(jnp.int32), 1, keepdims=False)
        right = lax.dynamic_index_in_dim(out_groups, group.astype(jnp.int32), 1, keepdims=False)
        term = lax.dot_general(left, right, (((1,), (1,)), ((), ())), preferred_element_type=jnp.float32)
        return total + lax.optimization_barrier(term.astype(jnp.bfloat16)).astype(jnp.float32)
    summed = lax.fori_loop(0, N_TENSOR, add_group, jnp.zeros((TOKENS, D), jnp.float32))
    return summed.astype(jnp.bfloat16)
```

```python
import functools
import jax
import jax.numpy as jnp
import ml_dtypes
import numpy as np
from jax import lax
from jax.experimental import pallas as pl
from jax.experimental.pallas import tpu as pltpu
from jax.sharding import PartitionSpec as P

norm_epsilon = 1e-06
axes = ("groups", "context", "tensor")
edge = 16
f32 = jnp.float32
bf16 = jnp.bfloat16


def split_parts(matrix):
    high = matrix.astype(ml_dtypes.bfloat16)
    low = (matrix - high.astype(np.float64)).astype(ml_dtypes.bfloat16)
    return high, low


def fourier_tables(taps):
    size = 2 * taps
    freq = np.arange(taps)[:, None]
    time = np.arange(size)[None, :]
    angle = 2 * np.pi * ((freq * time) % size) / size
    cosine, sine = np.cos(angle), np.sin(angle)
    sine[0] = 1.0 - 2.0 * (np.arange(size) % 2)
    forward = np.concatenate([cosine, sine], axis=0)
    weight = np.full((2 * taps, 1), 2.0 / size)
    weight[0] = weight[taps] = 1.0 / size
    inverse = (forward * weight)[:, taps:].T
    fh, fl = split_parts(forward[:, :taps])
    ih, il = split_parts(inverse)
    return np.concatenate([fh, fl], axis=0), np.concatenate([ih, ih, il], axis=1)


def gate_kernel(z_ref, a1_ref, a2_ref, taps_ref, gated_ref, head_ref, tail_ref, s1, s2):
    count, length, _ = a1_ref.shape
    slab = count * length
    z = z_ref[0]
    feats = []
    for k, (a_ref, s) in enumerate(((a1_ref, s1), (a2_ref, s2))):
        s[0:edge] = jnp.zeros_like(s[0:edge])
        for n in range(count):
            block = a_ref[lax.rem(z - n + count, count)].astype(bf16)
            s[edge + n * length : edge + (n + 1) * length] = block.astype(f32)
        head_ref[k] = s[edge : 2 * edge].astype(bf16)
        tail_ref[k] = s[slab : slab + edge].astype(bf16)
        total = None
        for lag in range(taps_ref.shape[0]):
            term = taps_ref[lag, k + 1][None] * s[edge - lag : edge - lag + slab]
            total = term if total is None else total + term
        feats.append(total)
    gated_ref[...] = (feats[0] * feats[1]).astype(bf16)


def gate(z, acc1, acc2, short_filter, width):
    count, length, channels = acc1.shape
    slab = count * length
    grid_spec = pltpu.PrefetchScalarGridSpec(
        num_scalar_prefetch=1,
        grid=(channels // width,),
        in_specs=[
            pl.BlockSpec((count, length, width), lambda i, z: (0, 0, i)),
            pl.BlockSpec((count, length, width), lambda i, z: (0, 0, i)),
            pl.BlockSpec(short_filter.shape[:2] + (width,), lambda i, z: (0, 0, i)),
        ],
        out_specs=[
            pl.BlockSpec((slab, width), lambda i, z: (0, i)),
            pl.BlockSpec((2, edge, width), lambda i, z: (0, 0, i)),
            pl.BlockSpec((2, edge, width), lambda i, z: (0, 0, i)),
        ],
        scratch_shapes=[pltpu.VMEM((slab + edge, width), f32)] * 2,
    )
    return pl.pallas_call(
        gate_kernel,
        grid_spec=grid_spec,
        out_shape=[
            jax.ShapeDtypeStruct((slab, channels), bf16),
            jax.ShapeDtypeStruct((2, edge, channels), bf16),
            jax.ShapeDtypeStruct((2, edge, channels), bf16),
        ],
        compiler_params=pltpu.CompilerParams(vmem_limit_bytes=40 << 20),
        name="gate",
    )(z, acc1, acc2, short_filter)


def mix_kernel(
    gated_ref, before_ref, head_ref, edge_ref, short_ref, taps_ref, fwd_ref, inv_ref, mixed_ref, s
):
    taps = taps_ref.shape[0]
    blocks = gated_ref.shape[0] // taps
    feats = []
    for k in range(2):
        s[0:edge] = edge_ref[k].astype(f32)
        s[edge : 2 * edge] = head_ref[k].astype(f32)
        total = None
        for lag in range(short_ref.shape[0]):
            term = short_ref[lag, k + 1][None] * s[edge - lag : 2 * edge - lag]
            total = term if total is None else total + term
        feats.append(total)
    first = (feats[0] * feats[1]).astype(bf16)

    def transform(block):
        both = jnp.dot(fwd_ref[...], block, preferred_element_type=f32)
        return both[: 2 * taps] + both[2 * taps :]

    row = lax.broadcasted_iota(jnp.int32, (2 * taps, 1), 0)
    sign = jnp.where(row % 2 == 0, 1.0, -1.0).astype(f32)
    is_zero = lax.broadcasted_iota(jnp.int32, (taps, 1), 0) == 0
    response = transform(taps_ref[...])
    h_cos, h_sin = response[:taps], response[taps:]
    h_low = jnp.where(is_zero, h_sin, h_cos)
    h_sin = jnp.where(is_zero, 0.0, h_sin)
    last = transform(before_ref[...])
    for b in range(blocks):
        if b == 0:
            block = jnp.concatenate([first, gated_ref[edge:taps]], axis=0)
        else:
            block = gated_ref[b * taps : (b + 1) * taps]
        now = transform(block)
        x = last + sign * now
        last = now
        x_cos, x_sin = x[:taps], x[taps:]
        y = jnp.concatenate([x_cos * h_cos - x_sin * h_sin, x_sin * h_low + x_cos * h_sin], axis=0)
        high = y.astype(bf16)
        low = (y - high.astype(f32)).astype(bf16)
        mixed_ref[b * taps : (b + 1) * taps] = jnp.dot(
            inv_ref[...], jnp.concatenate([high, low, high], axis=0), preferred_element_type=f32
        )


def mix(gated, before, head, edge_rows, short_filter, taps, width):
    slab, channels = gated.shape
    count = taps.shape[0]
    forward, inverse = fourier_tables(count)
    col = lambda rows: pl.BlockSpec((rows, width), lambda i: (0, i))
    cube = lambda a, b: pl.BlockSpec((a, b, width), lambda i: (0, 0, i))
    return pl.pallas_call(
        mix_kernel,
        grid=(channels // width,),
        in_specs=[
            col(slab),
            col(count),
            cube(2, edge),
            cube(2, edge),
            cube(*short_filter.shape[:2]),
            col(count),
            pl.BlockSpec(forward.shape, lambda i: (0, 0)),
            pl.BlockSpec(inverse.shape, lambda i: (0, 0)),
        ],
        out_specs=col(slab),
        out_shape=jax.ShapeDtypeStruct((slab, channels), f32),
        scratch_shapes=[pltpu.VMEM((2 * edge, width), f32)],
        compiler_params=pltpu.CompilerParams(vmem_limit_bytes=40 << 20),
        name="mix",
    )(gated, before, head, edge_rows, short_filter, taps, forward, inverse)


def combine_kernel(z_ref, a_ref, edge_ref, short_ref, mixed_ref, out_ref, s):
    count, length, _ = a_ref.shape
    slab = count * length
    z = z_ref[0]
    s[0:edge] = edge_ref[...].astype(f32)
    for n in range(count):
        block = a_ref[lax.rem(z - n + count, count)].astype(bf16)
        s[edge + n * length : edge + (n + 1) * length] = block.astype(f32)
    total = None
    for lag in range(short_ref.shape[0]):
        term = short_ref[lag, 0][None] * s[edge - lag : edge - lag + slab]
        total = term if total is None else total + term
    out_ref[...] = (total * mixed_ref[...]).astype(bf16)


def combine(z, acc, edge_rows, short_filter, mixed, width):
    count, length, channels = acc.shape
    slab = count * length
    grid_spec = pltpu.PrefetchScalarGridSpec(
        num_scalar_prefetch=1,
        grid=(channels // width,),
        in_specs=[
            pl.BlockSpec((count, length, width), lambda i, z: (0, 0, i)),
            pl.BlockSpec((edge, width), lambda i, z: (0, i)),
            pl.BlockSpec(short_filter.shape[:2] + (width,), lambda i, z: (0, 0, i)),
            pl.BlockSpec((slab, width), lambda i, z: (0, i)),
        ],
        out_specs=pl.BlockSpec((slab, width), lambda i, z: (0, i)),
        scratch_shapes=[pltpu.VMEM((slab + edge, width), f32)],
    )
    return pl.pallas_call(
        combine_kernel,
        grid_spec=grid_spec,
        out_shape=jax.ShapeDtypeStruct((slab, channels), bf16),
        compiler_params=pltpu.CompilerParams(vmem_limit_bytes=40 << 20),
        name="combine",
    )(z, acc, edge_rows, short_filter, mixed)


def local(tokens, norm_gain, w_in, short_filter, medium_filter, decay, w_out):
    groups, contexts, count = (lax.axis_size(a) for a in axes)
    g, c, z = (lax.axis_index(a) for a in axes)
    length, features = tokens.shape
    rows, branches, channels = w_in.shape
    slab = length * count
    width = min(channels, 256)
    z_ref = z.astype(jnp.int32).reshape(1)
    paired = contexts == 4 and groups == 2

    def move(value, target):
        pairs = []
        for i in range(groups):
            for j in range(contexts):
                for k in range(count):
                    to = target(i, j, k)
                    if 0 <= to[1] < contexts and 0 <= to[2] < count:
                        pairs.append(
                            ((i * contexts + j) * count + k, (to[0] * contexts + to[1]) * count + to[2])
                        )
        return lax.ppermute(value, axes, pairs)

    to_chip = lambda v: move(v, lambda i, j, k: (i, j ^ 2, k))
    to_core = lambda v: move(v, lambda i, j, k: (i, j ^ 1, k))
    to_group = lambda v: move(v, lambda i, j, k: (1 - i, j, k))
    to_next = lambda v: move(v, lambda i, j, k: (i, j + 1, k))
    to_up = lambda v: move(v, lambda i, j, k: (i, j, k + 1))
    to_down = lambda v: move(v, lambda i, j, k: (i, j, k - 1))

    values = tokens.astype(f32)
    inverse_rms = lax.rsqrt(jnp.mean(values * values, axis=1, keepdims=True) + norm_epsilon)
    normed = (values * inverse_rms * norm_gain.astype(f32)[None, :]).astype(bf16)

    weights = jnp.transpose(w_in, (1, 0, 2))
    half = rows // 2
    fine = half // 2
    pieces = {}
    order = (1, 2, 0)
    if paired:
        first_half, other_half = g * half, (1 - g) * half
        for b in order:
            pieces[b] = [(c * rows, weights[b]), ((c ^ 1) * rows, to_core(weights[b]))]
        for b in order:
            for u in range(half // fine):
                mine = lax.dynamic_slice(weights[b], (first_half + u * fine, 0), (fine, channels))
                near = to_chip(mine)
                far = to_group(near)
                pieces[b] += [
                    ((c ^ 2) * rows + first_half + u * fine, near),
                    ((c ^ 3) * rows + first_half + u * fine, to_core(near)),
                    ((c ^ 2) * rows + other_half + u * fine, far),
                    ((c ^ 3) * rows + other_half + u * fine, to_core(far)),
                ]
    else:
        full = lax.all_gather(weights, "context", axis=1, tiled=True)
        for b in order:
            pieces[b] = [(i * rows, full[b, i * rows : (i + 1) * rows]) for i in range(contexts)]

    def spread(chunk):
        up, down = [chunk], [chunk]
        for _ in range(count - 1):
            up.append(to_up(up[-1]))
            down.append(to_down(down[-1]))
        blocks = [chunk]
        for s in range(1, count):
            blocks.append(jnp.where(z >= s, up[s], down[count - s]))
        return jnp.concatenate(blocks, axis=0)

    chunk_of = {}
    if paired:
        starts = [c * rows, (c ^ 1) * rows, (c ^ 2) * rows, (c ^ 3) * rows]
    else:
        starts = [i * rows for i in range(contexts)]
    gathered = []
    for i, start in enumerate(starts):
        chunk = lax.dynamic_slice(normed, (0, start), (length, rows))
        if paired and i >= 2:
            chunk = jnp.where(g == 0, chunk, jnp.concatenate([chunk[:, half:], chunk[:, :half]], 1))
        gathered.append(spread(chunk))

    def columns(b, index):
        if not paired or index < 2:
            return gathered[index]
        u, kind = divmod(index - 2, 4)
        part = gathered[2 + kind % 2]
        at = (kind // 2) * half + u * fine
        return part[:, at : at + fine]

    acc = {}
    for b in order:
        total = None
        for index, (_, weight) in enumerate(pieces[b]):
            term = jnp.dot(columns(b, index), weight, preferred_element_type=f32)
            total = term if total is None else total + term
        acc[b] = total.reshape(count, length, channels)

    medium_count = medium_filter.shape[0]
    lag_index = jnp.arange(medium_count, dtype=f32)
    taps = (medium_filter * jnp.exp(-decay[None, :] * lag_index[:, None])).astype(bf16)
    gated, head, tail = gate(z_ref, acc[1], acc[2], short_filter, width)
    before = to_next(gated[slab - medium_count :])
    mixed = mix(gated, before, head, to_next(tail), short_filter, taps, width)
    last = lax.dynamic_index_in_dim(acc[0], lax.rem(z + 1, count), 0, keepdims=False)
    query_edge = to_next(last[length - edge :].astype(bf16))
    combined = combine(z_ref, acc[0], query_edge, short_filter, mixed, width)

    out_rows = w_out.shape[0]
    if paired:
        out_half = out_rows // 2
        mine = lax.dynamic_slice(w_out, (g * out_half, 0), (out_half, channels))
        near = to_chip(mine)
        far = to_group(near)
        sets = [[w_out, to_core(w_out)], [near, far, to_core(near), to_core(far)]]
    else:
        full_out = lax.all_gather(w_out, "context", axis=0, tiled=True)
        sets = [[full_out]]

    results = []
    for parts in sets:
        partial = [
            lax.dot_general(
                combined, part, (((1,), (1,)), ((), ())), preferred_element_type=f32
            ).astype(bf16)
            for part in parts
        ]

        def block(index):
            index = jnp.clip(index, 0, count - 1)
            return jnp.concatenate(
                [lax.dynamic_slice(p, (index * length, 0), (length, p.shape[1])) for p in partial], 1
            )

        up = down = None
        for s in range(1, count):
            rising = block(count + z - s)
            falling = block(z - count + s)
            if up is not None:
                rising = (rising.astype(f32) + up.astype(f32)).astype(bf16)
                falling = (falling.astype(f32) + down.astype(f32)).astype(bf16)
            up, down = to_up(rising), to_down(falling)
        results.append(block(z).astype(f32) + up.astype(f32) + down.astype(f32))
    if not paired:
        return results[0].astype(bf16)
    own, other = results
    e0, e1 = own[:, :out_rows], own[:, out_rows:]
    quarter = [other[:, i * out_half : (i + 1) * out_half] for i in range(4)]
    swap = lambda test, a, b: (jnp.where(test, b, a), jnp.where(test, a, b))
    e2 = jnp.concatenate(swap(g == 1, quarter[0], quarter[1]), 1)
    e3 = jnp.concatenate(swap(g == 1, quarter[2], quarter[3]), 1)
    odd = c % 2 == 1
    low = jnp.concatenate(swap(odd, e0, e1), 1)
    high = jnp.concatenate(swap(odd, e2, e3), 1)
    return jnp.concatenate(swap(c >= 2, low, high), 1).astype(bf16)


def solution(mesh):
    in_specs = (
        P(axes, None),
        P(),
        P("context", None, "tensor"),
        P(None, None, "tensor"),
        P(None, "tensor"),
        P("tensor"),
        P("context", "tensor"),
    )
    return jax.shard_map(
        local, mesh=mesh, in_specs=in_specs, out_specs=P(axes, None), check_vma=False
    )
```

```python
import functools
import jax
import jax.numpy as jnp
import ml_dtypes
import numpy as np
from jax import lax
from jax.experimental import pallas as pl
from jax.experimental.pallas import tpu as pltpu
from jax.sharding import PartitionSpec as P

norm_epsilon = 1e-06
axes = ("groups", "context", "tensor")
edge = 16
f32 = jnp.float32
bf16 = jnp.bfloat16


def split_parts(matrix):
    high = matrix.astype(ml_dtypes.bfloat16)
    low = (matrix - high.astype(np.float64)).astype(ml_dtypes.bfloat16)
    return high, low


def fourier_tables(taps):
    size = 2 * taps
    freq = np.arange(taps)[:, None]
    time = np.arange(size)[None, :]
    angle = 2 * np.pi * ((freq * time) % size) / size
    cosine, sine = np.cos(angle), np.sin(angle)
    sine[0] = 1.0 - 2.0 * (np.arange(size) % 2)
    forward = np.concatenate([cosine, sine], axis=0)
    weight = np.full((2 * taps, 1), 2.0 / size)
    weight[0] = weight[taps] = 1.0 / size
    inverse = (forward * weight)[:, taps:].T
    fh, fl = split_parts(forward[:, :taps])
    ih, il = split_parts(inverse)
    return np.concatenate([fh, fl], axis=0), np.concatenate([ih, ih, il], axis=1)


def short_sum(s, taps_ref, branch, slab):
    total = None
    for lag in range(taps_ref.shape[0]):
        term = taps_ref[lag, branch][None] * s[edge - lag : edge - lag + slab]
        total = term if total is None else total + term
    return total


def product(at_ref, x_ref, pieces):
    total = None
    for n, piece in enumerate(pieces):
        depth = piece.shape[-2]
        step = min(depth, 256)
        part = x_ref[:, pl.ds(pl.multiple_of(at_ref[n], step), depth)]
        term = jnp.dot(part, piece[...], preferred_element_type=f32)
        total = term if total is None else total + term
    return total.astype(bf16).astype(f32)


def gate_kernel(counts, at_ref, x_ref, taps_ref, *rest):
    slab = x_ref.shape[0]
    pieces = [rest[: counts[0]], rest[counts[0] : sum(counts)]]
    gated_ref, head_ref, tail_ref, s = rest[sum(counts) :]
    feats = []
    for k in range(2):
        s[0:edge] = jnp.zeros((edge, s.shape[1]), f32)
        s[edge : edge + slab] = product(at_ref, x_ref, pieces[k])
        head_ref[k] = s[edge : 2 * edge].astype(bf16)
        tail_ref[k] = s[slab : slab + edge].astype(bf16)
        feats.append(short_sum(s, taps_ref, k + 1, slab))
    gated_ref[...] = (feats[0] * feats[1]).astype(bf16)


def piece_specs(pieces, width):
    specs = []
    for array, branch, _ in pieces:
        if branch is None:
            specs.append(pl.BlockSpec((array.shape[0], width), lambda i, at: (0, i)))
        else:
            specs.append(
                pl.BlockSpec((None, array.shape[1], width), lambda i, at, b=branch: (b, 0, i))
            )
    return specs


def offsets(pieces):
    return jnp.stack([jnp.asarray(p[2], jnp.int32) for p in pieces])


def gate(x, one, two, short_filter, width):
    slab = x.shape[0]
    channels = short_filter.shape[-1]
    grid_spec = pltpu.PrefetchScalarGridSpec(
        num_scalar_prefetch=1,
        grid=(channels // width,),
        in_specs=[
            pl.BlockSpec(x.shape, lambda i, at: (0, 0)),
            pl.BlockSpec(short_filter.shape[:2] + (width,), lambda i, at: (0, 0, i)),
        ]
        + piece_specs(one, width)
        + piece_specs(two, width),
        out_specs=[
            pl.BlockSpec((slab, width), lambda i, at: (0, i)),
            pl.BlockSpec((2, edge, width), lambda i, at: (0, 0, i)),
            pl.BlockSpec((2, edge, width), lambda i, at: (0, 0, i)),
        ],
        scratch_shapes=[pltpu.VMEM((slab + edge, width), f32)],
    )
    return pl.pallas_call(
        functools.partial(gate_kernel, (len(one), len(two))),
        grid_spec=grid_spec,
        out_shape=[
            jax.ShapeDtypeStruct((slab, channels), bf16),
            jax.ShapeDtypeStruct((2, edge, channels), bf16),
            jax.ShapeDtypeStruct((2, edge, channels), bf16),
        ],
        compiler_params=pltpu.CompilerParams(vmem_limit_bytes=50 << 20),
        name="gate",
    )(offsets(one), x, short_filter, *[p[0] for p in one + two])


def query_kernel(at_ref, x_ref, before_ref, taps_ref, *rest):
    slab = x_ref.shape[0]
    *pieces, out_ref, s = rest
    s[0:edge] = product(at_ref, before_ref, pieces)
    s[edge : edge + slab] = product(at_ref, x_ref, pieces)
    out_ref[...] = short_sum(s, taps_ref, 0, slab)


def query(x, before, pieces, short_filter, width):
    slab = x.shape[0]
    channels = short_filter.shape[-1]
    grid_spec = pltpu.PrefetchScalarGridSpec(
        num_scalar_prefetch=1,
        grid=(channels // width,),
        in_specs=[
            pl.BlockSpec(x.shape, lambda i, at: (0, 0)),
            pl.BlockSpec(before.shape, lambda i, at: (0, 0)),
            pl.BlockSpec(short_filter.shape[:2] + (width,), lambda i, at: (0, 0, i)),
        ]
        + piece_specs(pieces, width),
        out_specs=pl.BlockSpec((slab, width), lambda i, at: (0, i)),
        scratch_shapes=[pltpu.VMEM((slab + edge, width), f32)],
    )
    return pl.pallas_call(
        query_kernel,
        grid_spec=grid_spec,
        out_shape=jax.ShapeDtypeStruct((slab, channels), f32),
        compiler_params=pltpu.CompilerParams(vmem_limit_bytes=50 << 20),
        name="query",
    )(offsets(pieces), x, before, short_filter, *[p[0] for p in pieces])


def mix_kernel(
    gated_ref, before_ref, head_ref, edge_ref, short_ref, taps_ref, query_ref, fwd_ref, inv_ref, out_ref, s
):
    taps = taps_ref.shape[0]
    blocks = gated_ref.shape[0] // taps
    feats = []
    for k in range(2):
        s[0:edge] = edge_ref[k].astype(f32)
        s[edge : 2 * edge] = head_ref[k].astype(f32)
        total = None
        for lag in range(short_ref.shape[0]):
            term = short_ref[lag, k + 1][None] * s[edge - lag : 2 * edge - lag]
            total = term if total is None else total + term
        feats.append(total)
    first = (feats[0] * feats[1]).astype(bf16)

    def transform(block):
        both = jnp.dot(fwd_ref[...], block, preferred_element_type=f32)
        return both[: 2 * taps] + both[2 * taps :]

    row = lax.broadcasted_iota(jnp.int32, (2 * taps, 1), 0)
    sign = jnp.where(row % 2 == 0, 1.0, -1.0).astype(f32)
    is_zero = lax.broadcasted_iota(jnp.int32, (taps, 1), 0) == 0
    response = transform(taps_ref[...])
    h_cos, h_sin = response[:taps], response[taps:]
    h_low = jnp.where(is_zero, h_sin, h_cos)
    h_sin = jnp.where(is_zero, 0.0, h_sin)
    last = transform(before_ref[...])
    for b in range(blocks):
        if b == 0:
            block = jnp.concatenate([first, gated_ref[edge:taps]], axis=0)
        else:
            block = gated_ref[b * taps : (b + 1) * taps]
        now = transform(block)
        x = last + sign * now
        last = now
        x_cos, x_sin = x[:taps], x[taps:]
        y = jnp.concatenate([x_cos * h_cos - x_sin * h_sin, x_sin * h_low + x_cos * h_sin], axis=0)
        high = y.astype(bf16)
        low = (y - high.astype(f32)).astype(bf16)
        mixed = jnp.dot(
            inv_ref[...], jnp.concatenate([high, low, high], axis=0), preferred_element_type=f32
        )
        at = slice(b * taps, (b + 1) * taps)
        out_ref[at] = (query_ref[at] * mixed).astype(bf16)


def mix(gated, before, head, edge_rows, short_filter, taps, query_rows, width):
    slab, channels = gated.shape
    count = taps.shape[0]
    forward, inverse = fourier_tables(count)
    col = lambda rows: pl.BlockSpec((rows, width), lambda i: (0, i))
    cube = lambda a, b: pl.BlockSpec((a, b, width), lambda i: (0, 0, i))
    return pl.pallas_call(
        mix_kernel,
        grid=(channels // width,),
        in_specs=[
            col(slab),
            col(count),
            cube(2, edge),
            cube(2, edge),
            cube(*short_filter.shape[:2]),
            col(count),
            col(slab),
            pl.BlockSpec(forward.shape, lambda i: (0, 0)),
            pl.BlockSpec(inverse.shape, lambda i: (0, 0)),
        ],
        out_specs=col(slab),
        out_shape=jax.ShapeDtypeStruct((slab, channels), bf16),
        scratch_shapes=[pltpu.VMEM((2 * edge, width), f32)],
        compiler_params=pltpu.CompilerParams(vmem_limit_bytes=40 << 20),
        name="mix",
    )(gated, before, head, edge_rows, short_filter, taps, query_rows, forward, inverse)


def local(tokens, norm_gain, w_in, short_filter, medium_filter, decay, w_out):
    groups, contexts, count = (lax.axis_size(a) for a in axes)
    g, c, z = (lax.axis_index(a) for a in axes)
    length, features = tokens.shape
    rows, branches, channels = w_in.shape
    slab = length * count
    width = min(channels, 256)
    paired = contexts == 4 and groups == 2

    def move(value, target):
        pairs = []
        for i in range(groups):
            for j in range(contexts):
                for k in range(count):
                    to = target(i, j, k)
                    if 0 <= to[1] < contexts and 0 <= to[2] < count:
                        pairs.append(
                            ((i * contexts + j) * count + k, (to[0] * contexts + to[1]) * count + to[2])
                        )
        return lax.ppermute(value, axes, pairs)

    to_chip = lambda v: move(v, lambda i, j, k: (i, j ^ 2, k))
    to_core = lambda v: move(v, lambda i, j, k: (i, j ^ 1, k))
    to_group = lambda v: move(v, lambda i, j, k: (1 - i, j, k))
    to_next = lambda v: move(v, lambda i, j, k: (i, j + 1, k))
    send = lambda v, pairs: move(v, lambda i, j, k: (i, j, pairs.get(k, -1)))
    to_up = lambda v: move(v, lambda i, j, k: (i, j, k + 1))
    to_down = lambda v: move(v, lambda i, j, k: (i, j, k - 1))

    def after(value, *earlier):
        return lax.optimization_barrier((value, *earlier))[0]

    values = tokens.astype(f32)
    inverse_rms = lax.rsqrt(jnp.mean(values * values, axis=1, keepdims=True) + norm_epsilon)
    normed = (values * inverse_rms * norm_gain.astype(f32)[None, :]).astype(bf16)

    weights = jnp.transpose(w_in, (1, 0, 2))
    half = rows // 2
    fine = half // 2
    order = (1, 2, 0)
    out_rows = w_out.shape[0]
    out_half = out_rows // 2
    if paired:
        first_half, other_half = g * half, (1 - g) * half
        peer = to_core(weights)
        pieces = {b: [(weights, b, c * rows), (peer, b, (c ^ 1) * rows)] for b in order}
        nears = []
        for b in order:
            for u in range(half // fine):
                mine = lax.dynamic_slice(weights[b], (first_half + u * fine, 0), (fine, channels))
                if len(nears) >= 2:
                    mine = after(mine, nears[-2])
                near = to_chip(mine)
                far = to_group(near)
                nears.append(near)
                pieces[b] += [
                    (near, None, (c ^ 2) * rows + first_half + u * fine),
                    (to_core(near), None, (c ^ 3) * rows + first_half + u * fine),
                    (far, None, (c ^ 2) * rows + other_half + u * fine),
                    (to_core(far), None, (c ^ 3) * rows + other_half + u * fine),
                ]
        mine = lax.dynamic_slice(w_out, (g * out_half, 0), (out_half, channels))
        near = to_chip(after(mine, nears[-2]))
        far = to_group(near)
        out_peer = to_core(after(w_out, nears[-2]))
        sets = [[w_out], [out_peer], [near, far], [to_core(near), to_core(far)]]
    else:
        full = lax.all_gather(weights, "context", axis=1, tiled=True)
        pieces = {b: [(full, b, 0)] for b in order}
        sets = [[lax.all_gather(w_out, "context", axis=0, tiled=True)]]

    gathered = lax.all_gather(normed, "tensor", axis=0, tiled=True)
    before_rows = to_next(gathered[slab - edge :])

    medium_count = medium_filter.shape[0]
    lag_index = jnp.arange(medium_count, dtype=f32)
    taps = (medium_filter * jnp.exp(-decay[None, :] * lag_index[:, None])).astype(bf16)
    gated, head, tail = gate(gathered, pieces[1], pieces[2], short_filter, width)
    before = to_next(gated[slab - medium_count :])
    edge_rows = to_next(tail)
    query_rows = query(gathered, before_rows, pieces[0], short_filter, width)
    combined = mix(gated, before, head, edge_rows, short_filter, taps, query_rows, width)

    results = []
    for parts in sets:
        partial = [
            lax.dot_general(
                combined, part, (((1,), (1,)), ((), ())), preferred_element_type=f32
            ).astype(bf16)
            for part in parts
        ]

        def block(index, blocks=1):
            index = jnp.clip(index, 0, count - blocks)
            return jnp.concatenate(
                [
                    lax.dynamic_slice(p, (index * length, 0), (blocks * length, p.shape[1]))
                    for p in partial
                ],
                1,
            )

        def plus(*terms):
            total = terms[0].astype(f32)
            for term in terms[1:]:
                total = total + term.astype(f32)
            return total.astype(bf16)

        if count == 4:
            far_pair = block(jnp.where(z < 2, 2, 0), 2)
            got = send(far_pair, {0: 1, 3: 2})
            got = send(plus(far_pair, got), {1: 2, 2: 1})
            low, high = got[:length], got[length:]
            odd = z % 2 == 1
            got_own = jnp.where(odd, high, low)
            got_peer = jnp.where(odd, low, high)
            last = send(plus(block(z ^ 1), got_peer), {0: 1, 1: 0, 2: 3, 3: 2})
            results.append(plus(block(z), got_own, last))
        else:
            up = down = None
            for s in range(1, count):
                rising = block(count + z - s)
                falling = block(z - count + s)
                if up is not None:
                    rising, falling = plus(rising, up), plus(falling, down)
                up, down = to_up(rising), to_down(falling)
            results.append(plus(block(z), up, down))
    if not paired:
        return results[0]
    swap = lambda test, a, b: (jnp.where(test, b, a), jnp.where(test, a, b))
    e0, e1, e2, e3 = results
    e2 = jnp.concatenate(swap(g == 1, e2[:, :out_half], e2[:, out_half:]), 1)
    e3 = jnp.concatenate(swap(g == 1, e3[:, :out_half], e3[:, out_half:]), 1)
    odd = c % 2 == 1
    low = jnp.concatenate(swap(odd, e0, e1), 1)
    high = jnp.concatenate(swap(odd, e2, e3), 1)
    return jnp.concatenate(swap(c >= 2, low, high), 1)


def solution(mesh):
    in_specs = (
        P(axes, None),
        P(),
        P("context", None, "tensor"),
        P(None, None, "tensor"),
        P(None, "tensor"),
        P("tensor"),
        P("context", "tensor"),
    )
    return jax.shard_map(
        local, mesh=mesh, in_specs=in_specs, out_specs=P(axes, None), check_vma=False
    )
```

```python
import functools
import jax
import jax.numpy as jnp
import ml_dtypes
import numpy as np
from jax import lax
from jax.experimental import pallas as pl
from jax.experimental.pallas import tpu as pltpu
from jax.sharding import PartitionSpec as P

norm_epsilon = 1e-06
axes = ("groups", "context", "tensor")
edge = 16
f32 = jnp.float32
bf16 = jnp.bfloat16


def split_parts(matrix):
    high = matrix.astype(ml_dtypes.bfloat16)
    low = (matrix - high.astype(np.float64)).astype(ml_dtypes.bfloat16)
    return high, low


def fourier_tables(taps):
    size = 2 * taps
    freq = np.arange(taps)[:, None]
    time = np.arange(size)[None, :]
    angle = 2 * np.pi * ((freq * time) % size) / size
    cosine, sine = np.cos(angle), np.sin(angle)
    sine[0] = 1.0 - 2.0 * (np.arange(size) % 2)
    forward = np.concatenate([cosine, sine], axis=0)
    weight = np.full((2 * taps, 1), 2.0 / size)
    weight[0] = weight[taps] = 1.0 / size
    inverse = (forward * weight)[:, taps:].T
    fh, fl = split_parts(forward[:, :taps])
    ih, il = split_parts(inverse)
    return np.concatenate([fh, fl], axis=1), np.concatenate([ih, ih, il], axis=1)


def short_sum(s, taps_ref, branch, slab):
    total = None
    for lag in range(taps_ref.shape[0]):
        term = taps_ref[lag, branch][None] * s[edge - lag : edge - lag + slab]
        total = term if total is None else total + term
    return total


def norm_kernel(x_ref, gain_ref, out_ref):
    values = x_ref[...].astype(f32)
    mean = jnp.mean(values * values, axis=1, keepdims=True)
    scaled = values * lax.rsqrt(mean + norm_epsilon)
    out_ref[...] = (scaled * gain_ref[...].astype(f32)).astype(bf16)


def norm(tokens, gain):
    length, features = tokens.shape
    rows = min(length, 32)
    return pl.pallas_call(
        norm_kernel,
        grid=(length // rows,),
        in_specs=[
            pl.BlockSpec((rows, features), lambda i: (i, 0)),
            pl.BlockSpec((1, features), lambda i: (0, 0)),
        ],
        out_specs=pl.BlockSpec((rows, features), lambda i: (i, 0)),
        out_shape=jax.ShapeDtypeStruct((length, features), bf16),
        name="norm",
    )(tokens, gain.reshape(1, features))


def fetch(kinds, at_ref, arrays, buffer, sems, step, slot, width):
    copies = []
    columns = pl.ds(pl.multiple_of(step * width, width), width)
    for n, ((place, branch, depth), array) in enumerate(zip(kinds, arrays)):
        source = array.at[:, columns] if branch is None else array.at[branch, :, columns]
        at = at_ref[n % at_ref.shape[0]]
        rows = pl.ds(pl.multiple_of(at, min(depth, 256)), depth)
        copies.append(
            pltpu.make_async_copy(source, buffer.at[slot, place, rows], sems.at[slot, n])
        )
    return copies


def rotate(kinds, at_ref, arrays, buffer, sems, width):
    step, steps = pl.program_id(0), pl.num_programs(0)
    slot = lax.rem(step, 2)

    @pl.when(step == 0)
    def _():
        for copy in fetch(kinds, at_ref, arrays, buffer, sems, 0, 0, width):
            copy.start()

    @pl.when(step + 1 < steps)
    def _():
        for copy in fetch(kinds, at_ref, arrays, buffer, sems, step + 1, 1 - slot, width):
            copy.start()

    for copy in fetch(kinds, at_ref, arrays, buffer, sems, step, slot, width):
        copy.wait()
    return slot


def gate_kernel(kinds, width, at_ref, x_ref, taps_ref, *rest):
    slab = x_ref.shape[0]
    arrays = rest[: len(kinds)]
    gated_ref, head_ref, tail_ref, s, buffer, sems = rest[len(kinds) :]
    slot = rotate(kinds, at_ref, arrays, buffer, sems, width)
    feats = []
    for k in range(2):
        s[0:edge] = jnp.zeros((edge, width), f32)
        term = jnp.dot(x_ref[...], buffer[slot, k], preferred_element_type=f32)
        s[edge : edge + slab] = term.astype(bf16).astype(f32)
        head_ref[k] = s[edge : 2 * edge].astype(bf16)
        tail_ref[k] = s[slab : slab + edge].astype(bf16)
        feats.append(short_sum(s, taps_ref, k + 1, slab))
    gated_ref[...] = (feats[0] * feats[1]).astype(bf16)


def kinds_of(pieces, place):
    return tuple((place, branch, array.shape[-2]) for array, branch, _ in pieces)


def offsets(pieces):
    return jnp.stack([jnp.asarray(p[2], jnp.int32) for p in pieces])


def gate(x, one, two, short_filter, width):
    slab, features = x.shape
    channels = short_filter.shape[-1]
    kinds = kinds_of(one, 0) + kinds_of(two, 1)
    grid_spec = pltpu.PrefetchScalarGridSpec(
        num_scalar_prefetch=1,
        grid=(channels // width,),
        in_specs=[
            pl.BlockSpec(x.shape, lambda i, at: (0, 0), pipeline_mode=pl.Buffered(1)),
            pl.BlockSpec(short_filter.shape[:2] + (width,), lambda i, at: (0, 0, i)),
        ]
        + [pl.BlockSpec(memory_space=pl.ANY)] * len(kinds),
        out_specs=[
            pl.BlockSpec((slab, width), lambda i, at: (0, i)),
            pl.BlockSpec((2, edge, width), lambda i, at: (0, 0, i)),
            pl.BlockSpec((2, edge, width), lambda i, at: (0, 0, i)),
        ],
        scratch_shapes=[
            pltpu.VMEM((slab + edge, width), f32),
            pltpu.VMEM((2, 2, features, width), bf16),
            pltpu.SemaphoreType.DMA((2, len(kinds))),
        ],
    )
    return pl.pallas_call(
        functools.partial(gate_kernel, kinds, width),
        grid_spec=grid_spec,
        out_shape=[
            jax.ShapeDtypeStruct((slab, channels), bf16),
            jax.ShapeDtypeStruct((2, edge, channels), bf16),
            jax.ShapeDtypeStruct((2, edge, channels), bf16),
        ],
        compiler_params=pltpu.CompilerParams(vmem_limit_bytes=40 << 20),
        name="gate",
    )(offsets(one), x, short_filter, *[p[0] for p in one + two])


def query_kernel(kinds, width, at_ref, x_ref, before_ref, taps_ref, *rest):
    slab = x_ref.shape[0]
    arrays = rest[: len(kinds)]
    out_ref, s, full, buffer, sems = rest[len(kinds) :]

    @pl.when(pl.program_id(0) == 0)
    def _():
        full[0:edge] = before_ref[...]
        full[edge : edge + slab] = x_ref[...]

    slot = rotate(kinds, at_ref, arrays, buffer, sems, width)
    term = jnp.dot(full[...], buffer[slot, 0], preferred_element_type=f32)
    s[...] = term.astype(bf16).astype(f32)
    out_ref[...] = short_sum(s, taps_ref, 0, slab)


def query(x, before, pieces, short_filter, width):
    slab, features = x.shape
    channels = short_filter.shape[-1]
    kinds = kinds_of(pieces, 0)
    grid_spec = pltpu.PrefetchScalarGridSpec(
        num_scalar_prefetch=1,
        grid=(channels // width,),
        in_specs=[
            pl.BlockSpec(x.shape, lambda i, at: (0, 0), pipeline_mode=pl.Buffered(1)),
            pl.BlockSpec(before.shape, lambda i, at: (0, 0), pipeline_mode=pl.Buffered(1)),
            pl.BlockSpec(short_filter.shape[:2] + (width,), lambda i, at: (0, 0, i)),
        ]
        + [pl.BlockSpec(memory_space=pl.ANY)] * len(kinds),
        out_specs=pl.BlockSpec((slab, width), lambda i, at: (0, i)),
        scratch_shapes=[
            pltpu.VMEM((slab + edge, width), f32),
            pltpu.VMEM((slab + edge, features), bf16),
            pltpu.VMEM((2, 1, features, width), bf16),
            pltpu.SemaphoreType.DMA((2, len(kinds))),
        ],
    )
    return pl.pallas_call(
        functools.partial(query_kernel, kinds, width),
        grid_spec=grid_spec,
        out_shape=jax.ShapeDtypeStruct((slab, channels), f32),
        compiler_params=pltpu.CompilerParams(vmem_limit_bytes=40 << 20),
        name="query",
    )(offsets(pieces), x, before, short_filter, *[p[0] for p in pieces])


def transform(fwd_ref, block):
    return jnp.dot(fwd_ref[...], jnp.concatenate([block, block], axis=0), preferred_element_type=f32)


def respond_kernel(filter_ref, decay_ref, fwd_ref, out_ref):
    taps = filter_ref.shape[0]
    lag = lax.broadcasted_iota(jnp.int32, (taps, 1), 0)
    faded = filter_ref[...] * jnp.exp(-decay_ref[...] * lag.astype(f32))
    response = transform(fwd_ref, faded.astype(bf16))
    h_cos, h_sin = response[:taps], response[taps:]
    out_ref[0] = h_cos
    out_ref[1] = jnp.where(lag == 0, 0.0, h_sin)
    out_ref[2] = jnp.where(lag == 0, h_sin, h_cos)


def respond(medium_filter, decay, forward, width):
    taps, channels = medium_filter.shape
    return pl.pallas_call(
        respond_kernel,
        grid=(channels // width,),
        in_specs=[
            pl.BlockSpec((taps, width), lambda i: (0, i)),
            pl.BlockSpec((1, width), lambda i: (0, i)),
            pl.BlockSpec(forward.shape, lambda i: (0, 0)),
        ],
        out_specs=pl.BlockSpec((3, taps, width), lambda i: (0, 0, i)),
        out_shape=jax.ShapeDtypeStruct((3, taps, channels), f32),
        name="respond",
    )(medium_filter, decay.reshape(1, channels), forward)


def mix_kernel(
    gated_ref, before_ref, head_ref, edge_ref, short_ref, response_ref, query_ref, fwd_ref, inv_ref, out_ref, s
):
    taps = response_ref.shape[1]
    blocks = gated_ref.shape[0] // taps
    feats = []
    for k in range(2):
        s[0:edge] = edge_ref[k].astype(f32)
        s[edge : 2 * edge] = head_ref[k].astype(f32)
        total = None
        for lag in range(short_ref.shape[0]):
            term = short_ref[lag, k + 1][None] * s[edge - lag : 2 * edge - lag]
            total = term if total is None else total + term
        feats.append(total)
    first = (feats[0] * feats[1]).astype(bf16)

    row = lax.broadcasted_iota(jnp.int32, (2 * taps, 1), 0)
    sign = jnp.where(row % 2 == 0, 1.0, -1.0).astype(f32)
    h_cos, h_sin, h_low = response_ref[0], response_ref[1], response_ref[2]
    last = transform(fwd_ref, before_ref[...])
    for b in range(blocks):
        if b == 0:
            block = jnp.concatenate([first, gated_ref[edge:taps]], axis=0)
        else:
            block = gated_ref[b * taps : (b + 1) * taps]
        now = transform(fwd_ref, block)
        x = last + sign * now
        last = now
        x_cos, x_sin = x[:taps], x[taps:]
        y = jnp.concatenate([x_cos * h_cos - x_sin * h_sin, x_sin * h_low + x_cos * h_sin], axis=0)
        high = y.astype(bf16)
        low = (y - high.astype(f32)).astype(bf16)
        mixed = jnp.dot(
            inv_ref[...], jnp.concatenate([high, low, high], axis=0), preferred_element_type=f32
        )
        at = slice(b * taps, (b + 1) * taps)
        out_ref[at] = (query_ref[at] * mixed).astype(bf16)


def mix(gated, before, head, edge_rows, short_filter, response, query_rows, tables, width):
    slab, channels = gated.shape
    count = response.shape[1]
    forward, inverse = tables
    col = lambda rows: pl.BlockSpec((rows, width), lambda i: (0, i))
    cube = lambda a, b: pl.BlockSpec((a, b, width), lambda i: (0, 0, i))
    return pl.pallas_call(
        mix_kernel,
        grid=(channels // width,),
        in_specs=[
            col(slab),
            col(count),
            cube(2, edge),
            cube(2, edge),
            cube(*short_filter.shape[:2]),
            cube(3, count),
            col(slab),
            pl.BlockSpec(forward.shape, lambda i: (0, 0)),
            pl.BlockSpec(inverse.shape, lambda i: (0, 0)),
        ],
        out_specs=col(slab),
        out_shape=jax.ShapeDtypeStruct((slab, channels), bf16),
        scratch_shapes=[pltpu.VMEM((2 * edge, width), f32)],
        compiler_params=pltpu.CompilerParams(vmem_limit_bytes=40 << 20),
        name="mix",
    )(gated, before, head, edge_rows, short_filter, response, query_rows, forward, inverse)


def local(tokens, norm_gain, w_in, short_filter, medium_filter, decay, w_out):
    groups, contexts, count = (lax.axis_size(a) for a in axes)
    g, c, z = (lax.axis_index(a) for a in axes)
    length, features = tokens.shape
    rows, branches, channels = w_in.shape
    slab = length * count
    width = min(channels, 256)
    paired = contexts == 4 and groups == 2

    def move(value, target):
        pairs = []
        for i in range(groups):
            for j in range(contexts):
                for k in range(count):
                    to = target(i, j, k)
                    if 0 <= to[1] < contexts and 0 <= to[2] < count:
                        pairs.append(
                            ((i * contexts + j) * count + k, (to[0] * contexts + to[1]) * count + to[2])
                        )
        return lax.ppermute(value, axes, pairs)

    to_chip = lambda v: move(v, lambda i, j, k: (i, j ^ 2, k))
    to_core = lambda v: move(v, lambda i, j, k: (i, j ^ 1, k))
    to_group = lambda v: move(v, lambda i, j, k: (1 - i, j, k))
    to_next = lambda v: move(v, lambda i, j, k: (i, j + 1, k))
    send = lambda v, pairs: move(v, lambda i, j, k: (i, j, pairs.get(k, -1)))
    to_up = lambda v: move(v, lambda i, j, k: (i, j, k + 1))
    to_down = lambda v: move(v, lambda i, j, k: (i, j, k - 1))

    def after(value, *earlier):
        return lax.optimization_barrier((value, *earlier))[0]

    weights = jnp.transpose(w_in, (1, 0, 2))
    half = rows // 2
    fine = half // 2
    order = (1, 2, 0)
    out_rows = w_out.shape[0]
    out_half = out_rows // 2
    if paired:
        first_half, other_half = g * half, (1 - g) * half
        peer = to_core(weights)
        pieces = {b: [(weights, b, c * rows), (peer, b, (c ^ 1) * rows)] for b in order}
        nears, far_cores = [], {}
        for b in order:
            for u in range(half // fine):
                mine = lax.dynamic_slice(
                    weights, (b, first_half + u * fine, 0), (1, fine, channels)
                ).reshape(fine, channels)
                if len(nears) < 2:
                    tokens = after(tokens, mine)
                if len(nears) >= 2:
                    mine = after(mine, nears[-2])
                near = to_chip(mine)
                far = to_group(near)
                nears.append(near)
                pieces[b] += [
                    (near, None, (c ^ 2) * rows + first_half + u * fine),
                    (to_core(near), None, (c ^ 3) * rows + first_half + u * fine),
                    (far, None, (c ^ 2) * rows + other_half + u * fine),
                    (far if b == 0 else to_core(far), None, (c ^ 3) * rows + other_half + u * fine),
                ]
                if b == 0:
                    far_cores[len(pieces[b]) - 1] = far
        mine = lax.dynamic_slice(w_out, (g * out_half, 0), (out_half, channels))
        near_out = to_chip(after(mine, nears[-1]))
    else:
        full = lax.all_gather(weights, "context", axis=1, tiled=True)
        pieces = {b: [(full, b, 0)] for b in order}

    normed = norm(tokens, norm_gain)
    gathered = lax.all_gather(normed, "tensor", axis=0, tiled=True)
    before_rows = to_next(gathered[slab - edge :])

    medium_count = medium_filter.shape[0]
    tables = fourier_tables(medium_count)
    response = respond(medium_filter, decay, tables[0], width)
    gate_taps = after(short_filter, response)
    gated, head, tail = gate(gathered, pieces[1], pieces[2], gate_taps, width)
    if paired:
        near_out = after(near_out, gated)
        far_out = to_group(near_out)
        out_peer = to_core(after(w_out, gated))
        sets = [[w_out], [out_peer], [near_out, far_out], [to_core(near_out), to_core(far_out)]]
        for n, p in enumerate(pieces[0]):
            if n in far_cores:
                pieces[0][n] = (to_core(after(far_cores[n], gated)), p[1], p[2])
    else:
        sets = [[lax.all_gather(w_out, "context", axis=0, tiled=True)]]
    before = to_next(gated[slab - medium_count :])
    edge_rows = to_next(tail)
    query_rows = query(gathered, before_rows, pieces[0], short_filter, width)
    combined = mix(gated, before, head, edge_rows, short_filter, response, query_rows, tables, width)

    results, firsts = [], []
    for parts in sets:
        partial = [
            lax.dot_general(
                combined, part, (((1,), (1,)), ((), ())), preferred_element_type=f32
            ).astype(bf16)
            for part in parts
        ]

        def block(index, blocks=1):
            index = jnp.clip(index, 0, count - blocks)
            return jnp.concatenate(
                [
                    lax.dynamic_slice(p, (index * length, 0), (blocks * length, p.shape[1]))
                    for p in partial
                ],
                1,
            )

        def plus(*terms):
            total = terms[0].astype(f32)
            for term in terms[1:]:
                total = total + term.astype(f32)
            return total.astype(bf16)

        if count == 4:
            far_pair = block(jnp.where(z < 2, 2, 0), 2)
            if len(firsts) >= 2:
                far_pair = after(far_pair, firsts[-2])
            got = send(far_pair, {0: 1, 3: 2})
            firsts.append(got)
            got = send(plus(far_pair, got), {1: 2, 2: 1})
            low, high = got[:length], got[length:]
            odd = z % 2 == 1
            got_own = jnp.where(odd, high, low)
            got_peer = jnp.where(odd, low, high)
            last = send(plus(block(z ^ 1), got_peer), {0: 1, 1: 0, 2: 3, 3: 2})
            results.append(plus(block(z), got_own, last))
        else:
            up = down = None
            for s in range(1, count):
                rising = block(count + z - s)
                falling = block(z - count + s)
                if up is not None:
                    rising, falling = plus(rising, up), plus(falling, down)
                up, down = to_up(rising), to_down(falling)
            results.append(plus(block(z), up, down))
    if not paired:
        return results[0]
    swap = lambda test, a, b: (jnp.where(test, b, a), jnp.where(test, a, b))
    e0, e1, e2, e3 = results
    e2 = jnp.concatenate(swap(g == 1, e2[:, :out_half], e2[:, out_half:]), 1)
    e3 = jnp.concatenate(swap(g == 1, e3[:, :out_half], e3[:, out_half:]), 1)
    odd = c % 2 == 1
    low = jnp.concatenate(swap(odd, e0, e1), 1)
    high = jnp.concatenate(swap(odd, e2, e3), 1)
    return jnp.concatenate(swap(c >= 2, low, high), 1)


def solution(mesh):
    in_specs = (
        P(axes, None),
        P(),
        P("context", None, "tensor"),
        P(None, None, "tensor"),
        P(None, "tensor"),
        P("tensor"),
        P("context", "tensor"),
    )
    return jax.shard_map(
        local, mesh=mesh, in_specs=in_specs, out_specs=P(axes, None), check_vma=False
    )
```

```python
import functools
import jax
import jax.numpy as jnp
import ml_dtypes
import numpy as np
from jax import lax
from jax.experimental import pallas as pl
from jax.experimental.pallas import tpu as pltpu
from jax.sharding import PartitionSpec as P

norm_epsilon = 1e-06
axes = ("groups", "context", "tensor")
edge = 16
f32 = jnp.float32
bf16 = jnp.bfloat16


def split_parts(matrix):
    high = matrix.astype(ml_dtypes.bfloat16)
    low = (matrix - high.astype(np.float64)).astype(ml_dtypes.bfloat16)
    return high, low


def fourier_tables(taps):
    size = 2 * taps
    freq = np.arange(taps)[:, None]
    time = np.arange(size)[None, :]
    angle = 2 * np.pi * ((freq * time) % size) / size
    cosine, sine = np.cos(angle), np.sin(angle)
    sine[0] = 1.0 - 2.0 * (np.arange(size) % 2)
    forward = np.concatenate([cosine, sine], axis=0)
    weight = np.full((2 * taps, 1), 2.0 / size)
    weight[0] = weight[taps] = 1.0 / size
    inverse = (forward * weight)[:, taps:].T
    fh, fl = split_parts(forward[:, :taps])
    ih, il = split_parts(inverse)
    return np.concatenate([fh, fl], axis=1), np.concatenate([ih, ih, il], axis=1)


def short_sum(s, taps_ref, branch, slab):
    total = None
    for lag in range(taps_ref.shape[0]):
        term = taps_ref[lag, branch][None] * s[edge - lag : edge - lag + slab]
        total = term if total is None else total + term
    return total


def norm_kernel(x_ref, gain_ref, out_ref):
    values = x_ref[...].astype(f32)
    mean = jnp.mean(values * values, axis=1, keepdims=True)
    scaled = values * lax.rsqrt(mean + norm_epsilon)
    out_ref[...] = (scaled * gain_ref[...].astype(f32)).astype(bf16)


def norm(tokens, gain):
    length, features = tokens.shape
    rows = min(length, 32)
    return pl.pallas_call(
        norm_kernel,
        grid=(length // rows,),
        in_specs=[
            pl.BlockSpec((rows, features), lambda i: (i, 0)),
            pl.BlockSpec((1, features), lambda i: (0, 0)),
        ],
        out_specs=pl.BlockSpec((rows, features), lambda i: (i, 0)),
        out_shape=jax.ShapeDtypeStruct((length, features), bf16),
        name="norm",
    )(tokens, gain.reshape(1, features))


def fetch(kinds, at_ref, arrays, buffer, sems, step, slot, width):
    copies = []
    columns = pl.ds(pl.multiple_of(step * width, width), width)
    for n, ((place, branch, depth), array) in enumerate(zip(kinds, arrays)):
        source = array.at[:, columns] if branch is None else array.at[branch, :, columns]
        at = at_ref[n % at_ref.shape[0]]
        rows = pl.ds(pl.multiple_of(at, min(depth, 256)), depth)
        copies.append(
            pltpu.make_async_copy(source, buffer.at[slot, place, rows], sems.at[slot, n])
        )
    return copies


def rotate(kinds, at_ref, arrays, buffer, sems, width, more):
    step, steps = pl.program_id(0), pl.num_programs(0)
    slot = lax.rem(step, 2)

    @pl.when(step == 0)
    def _():
        for copy in more:
            copy.start()
        for copy in fetch(kinds, at_ref, arrays, buffer, sems, 0, 0, width):
            copy.start()

    @pl.when(step + 1 < steps)
    def _():
        for copy in fetch(kinds, at_ref, arrays, buffer, sems, step + 1, 1 - slot, width):
            copy.start()

    @pl.when(step == 0)
    def _():
        for copy in more:
            copy.wait()

    copies = fetch(kinds, at_ref, arrays, buffer, sems, step, slot, width)

    def ready(place):
        for kind, copy in zip(kinds, copies):
            if kind[0] == place:
                copy.wait()

    return slot, ready


def gate_kernel(kinds, width, at_ref, x_ref, taps_ref, *rest):
    slab = x_ref.shape[0]
    arrays = rest[: len(kinds)]
    gated_ref, head_ref, halo_ref, s, full, buffer, sems, x_sem = rest[len(kinds) :]
    count = halo_ref.shape[0] - 2 * edge
    load = [pltpu.make_async_copy(x_ref, full, x_sem.at[0])]
    slot, ready = rotate(kinds, at_ref, arrays, buffer, sems, width, load)
    feats = []
    for k in range(2):
        ready(k)
        s[0:edge] = jnp.zeros((edge, width), f32)
        term = jnp.dot(full[...], buffer[slot, k], preferred_element_type=f32)
        s[edge : edge + slab] = term.astype(bf16).astype(f32)
        head_ref[k] = s[edge : 2 * edge].astype(bf16)
        halo_ref[count + k * edge : count + (k + 1) * edge] = s[slab : slab + edge].astype(bf16)
        feats.append(short_sum(s, taps_ref, k + 1, slab))
    gated = (feats[0] * feats[1]).astype(bf16)
    gated_ref[...] = gated
    halo_ref[0:count] = gated[slab - count :]


def kinds_of(pieces, place):
    return tuple((place, branch, array.shape[-2]) for array, branch, _ in pieces)


def offsets(pieces):
    return jnp.stack([jnp.asarray(p[2], jnp.int32) for p in pieces])


def hold(array):
    return pltpu.with_memory_space_constraint(array, pltpu.MemorySpace.HBM)


in_hbm = pl.BlockSpec(memory_space=pltpu.MemorySpace.HBM)


def gate(x, one, two, short_filter, taps, width):
    slab, features = x.shape
    channels = short_filter.shape[-1]
    kinds = kinds_of(one, 0) + kinds_of(two, 1)
    grid_spec = pltpu.PrefetchScalarGridSpec(
        num_scalar_prefetch=1,
        grid=(channels // width,),
        in_specs=[
            in_hbm,
            pl.BlockSpec(short_filter.shape[:2] + (width,), lambda i, at: (0, 0, i)),
        ]
        + [in_hbm] * len(kinds),
        out_specs=[
            pl.BlockSpec((slab, width), lambda i, at: (0, i)),
            pl.BlockSpec((2, edge, width), lambda i, at: (0, 0, i)),
            pl.BlockSpec((taps + 2 * edge, width), lambda i, at: (0, i)),
        ],
        scratch_shapes=[
            pltpu.VMEM((slab + edge, width), f32),
            pltpu.VMEM((slab, features), bf16),
            pltpu.VMEM((2, 2, features, width), bf16),
            pltpu.SemaphoreType.DMA((2, len(kinds))),
            pltpu.SemaphoreType.DMA((1,)),
        ],
    )
    return pl.pallas_call(
        functools.partial(gate_kernel, kinds, width),
        grid_spec=grid_spec,
        out_shape=[
            jax.ShapeDtypeStruct((slab, channels), bf16),
            jax.ShapeDtypeStruct((2, edge, channels), bf16),
            jax.ShapeDtypeStruct((taps + 2 * edge, channels), bf16),
        ],
        compiler_params=pltpu.CompilerParams(vmem_limit_bytes=40 << 20),
        name="gate",
    )(offsets(one), hold(x), short_filter, *[hold(p[0]) for p in one + two])


def query_kernel(kinds, width, at_ref, x_ref, before_ref, taps_ref, *rest):
    slab = x_ref.shape[0]
    arrays = rest[: len(kinds)]
    out_ref, s, full, buffer, sems, x_sem = rest[len(kinds) :]
    load = [
        pltpu.make_async_copy(x_ref, full.at[edge : edge + slab], x_sem.at[0]),
        pltpu.make_async_copy(before_ref, full.at[0:edge], x_sem.at[1]),
    ]
    slot, ready = rotate(kinds, at_ref, arrays, buffer, sems, width, load)
    ready(0)
    term = jnp.dot(full[...], buffer[slot, 0], preferred_element_type=f32)
    s[...] = term.astype(bf16).astype(f32)
    out_ref[...] = short_sum(s, taps_ref, 0, slab)


def query(x, before, pieces, short_filter, width):
    slab, features = x.shape
    channels = short_filter.shape[-1]
    kinds = kinds_of(pieces, 0)
    grid_spec = pltpu.PrefetchScalarGridSpec(
        num_scalar_prefetch=1,
        grid=(channels // width,),
        in_specs=[
            in_hbm,
            in_hbm,
            pl.BlockSpec(short_filter.shape[:2] + (width,), lambda i, at: (0, 0, i)),
        ]
        + [in_hbm] * len(kinds),
        out_specs=pl.BlockSpec((slab, width), lambda i, at: (0, i)),
        scratch_shapes=[
            pltpu.VMEM((slab + edge, width), f32),
            pltpu.VMEM((slab + edge, features), bf16),
            pltpu.VMEM((2, 1, features, width), bf16),
            pltpu.SemaphoreType.DMA((2, len(kinds))),
            pltpu.SemaphoreType.DMA((2,)),
        ],
    )
    return pl.pallas_call(
        functools.partial(query_kernel, kinds, width),
        grid_spec=grid_spec,
        out_shape=jax.ShapeDtypeStruct((slab, channels), f32),
        compiler_params=pltpu.CompilerParams(vmem_limit_bytes=40 << 20),
        name="query",
    )(offsets(pieces), hold(x), hold(before), short_filter, *[hold(p[0]) for p in pieces])


def transform(fwd_ref, block):
    return jnp.dot(fwd_ref[...], jnp.concatenate([block, block], axis=0), preferred_element_type=f32)


def respond_kernel(filter_ref, decay_ref, fwd_ref, out_ref):
    taps = filter_ref.shape[0]
    lag = lax.broadcasted_iota(jnp.int32, (taps, 1), 0)
    faded = filter_ref[...] * jnp.exp(-decay_ref[...] * lag.astype(f32))
    response = transform(fwd_ref, faded.astype(bf16))
    h_cos, h_sin = response[:taps], response[taps:]
    out_ref[0] = h_cos
    out_ref[1] = jnp.where(lag == 0, 0.0, h_sin)
    out_ref[2] = jnp.where(lag == 0, h_sin, h_cos)


def respond(medium_filter, decay, forward, width):
    taps, channels = medium_filter.shape
    return pl.pallas_call(
        respond_kernel,
        grid=(channels // width,),
        in_specs=[
            pl.BlockSpec((taps, width), lambda i: (0, i)),
            pl.BlockSpec((1, width), lambda i: (0, i)),
            pl.BlockSpec(forward.shape, lambda i: (0, 0)),
        ],
        out_specs=pl.BlockSpec((3, taps, width), lambda i: (0, 0, i)),
        out_shape=jax.ShapeDtypeStruct((3, taps, channels), f32),
        name="respond",
    )(medium_filter, decay.reshape(1, channels), forward)


def mix_kernel(
    gated_ref, halo_ref, head_ref, short_ref, response_ref, query_ref, fwd_ref, inv_ref, out_ref, s
):
    taps = response_ref.shape[1]
    blocks = gated_ref.shape[0] // taps
    feats = []
    for k in range(2):
        s[0:edge] = halo_ref[taps + k * edge : taps + (k + 1) * edge].astype(f32)
        s[edge : 2 * edge] = head_ref[k].astype(f32)
        total = None
        for lag in range(short_ref.shape[0]):
            term = short_ref[lag, k + 1][None] * s[edge - lag : 2 * edge - lag]
            total = term if total is None else total + term
        feats.append(total)
    first = (feats[0] * feats[1]).astype(bf16)

    row = lax.broadcasted_iota(jnp.int32, (2 * taps, 1), 0)
    sign = jnp.where(row % 2 == 0, 1.0, -1.0).astype(f32)
    h_cos, h_sin, h_low = response_ref[0], response_ref[1], response_ref[2]
    last = transform(fwd_ref, halo_ref[0:taps])
    for b in range(blocks):
        if b == 0:
            block = jnp.concatenate([first, gated_ref[edge:taps]], axis=0)
        else:
            block = gated_ref[b * taps : (b + 1) * taps]
        now = transform(fwd_ref, block)
        x = last + sign * now
        last = now
        x_cos, x_sin = x[:taps], x[taps:]
        y = jnp.concatenate([x_cos * h_cos - x_sin * h_sin, x_sin * h_low + x_cos * h_sin], axis=0)
        high = y.astype(bf16)
        low = (y - high.astype(f32)).astype(bf16)
        mixed = jnp.dot(
            inv_ref[...], jnp.concatenate([high, low, high], axis=0), preferred_element_type=f32
        )
        at = slice(b * taps, (b + 1) * taps)
        out_ref[at] = (query_ref[at] * mixed).astype(bf16)


def mix(gated, halo, head, short_filter, response, query_rows, tables, width):
    slab, channels = gated.shape
    count = response.shape[1]
    forward, inverse = tables
    col = lambda rows: pl.BlockSpec((rows, width), lambda i: (0, i))
    cube = lambda a, b: pl.BlockSpec((a, b, width), lambda i: (0, 0, i))
    return pl.pallas_call(
        mix_kernel,
        grid=(channels // width,),
        in_specs=[
            col(slab),
            col(count + 2 * edge),
            cube(2, edge),
            cube(*short_filter.shape[:2]),
            cube(3, count),
            col(slab),
            pl.BlockSpec(forward.shape, lambda i: (0, 0)),
            pl.BlockSpec(inverse.shape, lambda i: (0, 0)),
        ],
        out_specs=col(slab),
        out_shape=jax.ShapeDtypeStruct((slab, channels), bf16),
        scratch_shapes=[pltpu.VMEM((2 * edge, width), f32)],
        compiler_params=pltpu.CompilerParams(vmem_limit_bytes=40 << 20),
        name="mix",
    )(gated, halo, head, short_filter, response, query_rows, forward, inverse)


def local(tokens, norm_gain, w_in, short_filter, medium_filter, decay, w_out):
    groups, contexts, count = (lax.axis_size(a) for a in axes)
    g, c, z = (lax.axis_index(a) for a in axes)
    length, features = tokens.shape
    rows, branches, channels = w_in.shape
    slab = length * count
    width = min(channels, 256)
    paired = contexts == 4 and groups == 2

    def move(value, target):
        pairs = []
        for i in range(groups):
            for j in range(contexts):
                for k in range(count):
                    to = target(i, j, k)
                    if 0 <= to[1] < contexts and 0 <= to[2] < count:
                        pairs.append(
                            ((i * contexts + j) * count + k, (to[0] * contexts + to[1]) * count + to[2])
                        )
        return lax.ppermute(value, axes, pairs)

    to_chip = lambda v: move(v, lambda i, j, k: (i, j ^ 2, k))
    to_core = lambda v: move(v, lambda i, j, k: (i, j ^ 1, k))
    to_group = lambda v: move(v, lambda i, j, k: (1 - i, j, k))
    to_next = lambda v: move(v, lambda i, j, k: (i, j + 1, k))
    send = lambda v, pairs: move(v, lambda i, j, k: (i, j, pairs.get(k, -1)))
    to_up = lambda v: move(v, lambda i, j, k: (i, j, k + 1))
    to_down = lambda v: move(v, lambda i, j, k: (i, j, k - 1))

    def after(value, *earlier):
        return lax.optimization_barrier((value, *earlier))[0]

    weights = jnp.transpose(w_in, (1, 0, 2))
    half = rows // 2
    fine = half
    order = (1, 2, 0)
    out_rows = w_out.shape[0]
    if paired:
        first_half, other_half = g * half, (1 - g) * half
        peer = to_core(weights)
        pieces = {b: [(weights, b, c * rows), (peer, b, (c ^ 1) * rows)] for b in order}
        nears, fars, far_cores = [], [], {}
        for b in order:
            for u in range(half // fine):
                source = after(weights, normed) if nears else weights
                mine = lax.dynamic_slice(
                    source, (b, first_half + u * fine, 0), (1, fine, channels)
                ).reshape(fine, channels)
                if not nears:
                    normed = norm(after(tokens, mine), norm_gain)
                if nears:
                    mine = after(mine, nears[-1])
                near = to_chip(mine)
                far = to_group(after(near, fars[-1]) if fars else near)
                fars.append(far)
                nears.append(near)
                pieces[b] += [
                    (near, None, (c ^ 2) * rows + first_half + u * fine),
                    (to_core(near), None, (c ^ 3) * rows + first_half + u * fine),
                    (far, None, (c ^ 2) * rows + other_half + u * fine),
                    (far if b == 0 else to_core(far), None, (c ^ 3) * rows + other_half + u * fine),
                ]
                if b == 0:
                    far_cores[len(pieces[b]) - 1] = far
    else:
        full = lax.all_gather(weights, "context", axis=1, tiled=True)
        pieces = {b: [(full, b, 0)] for b in order}
        normed = norm(tokens, norm_gain)

    gathered = lax.all_gather(normed, "tensor", axis=0, tiled=True)
    before_rows = to_next(gathered[slab - edge :])

    medium_count = medium_filter.shape[0]
    tables = fourier_tables(medium_count)
    response = respond(medium_filter, decay, tables[0], width)
    gate_taps = after(short_filter, response)
    gated, head, edges = gate(
        gathered, pieces[1], pieces[2], gate_taps, medium_count, width
    )
    halo = to_next(edges)
    if paired:
        for n, far in far_cores.items():
            pieces[0][n] = (to_core(after(far, gated)), *pieces[0][n][1:])
    query_rows = query(gathered, before_rows, pieces[0], short_filter, width)
    combined = mix(gated, halo, head, short_filter, response, query_rows, tables, width)
    if paired:
        out_full = lax.all_gather(after(w_out, nears[0]), "context", axis=0, tiled=True)
        out_peer = to_core(after(w_out, gated))
        part = lambda i: lax.dynamic_slice(out_full, ((c ^ i) * out_rows, 0), (out_rows, channels))
        sets = [[w_out], [out_peer], [part(2)], [part(3)]]
    else:
        sets = [[lax.all_gather(w_out, "context", axis=0, tiled=True)]]

    results = []
    for parts in sets:
        partial = [
            lax.dot_general(
                combined, part, (((1,), (1,)), ((), ())), preferred_element_type=f32
            ).astype(bf16)
            for part in parts
        ]
        combined = after(combined, *partial)

        def block(index, blocks=1):
            index = jnp.clip(index, 0, count - blocks)
            return jnp.concatenate(
                [
                    lax.dynamic_slice(p, (index * length, 0), (blocks * length, p.shape[1]))
                    for p in partial
                ],
                1,
            )

        def plus(*terms):
            total = terms[0].astype(f32)
            for term in terms[1:]:
                total = total + term.astype(f32)
            return total.astype(bf16)

        if count == 4:
            far_pair = block(jnp.where(z < 2, 2, 0), 2)
            got = send(far_pair, {0: 1, 3: 2})
            got = send(plus(far_pair, got), {1: 2, 2: 1})
            low, high = got[:length], got[length:]
            odd = z % 2 == 1
            got_own = jnp.where(odd, high, low)
            got_peer = jnp.where(odd, low, high)
            last = send(plus(block(z ^ 1), got_peer), {0: 1, 1: 0, 2: 3, 3: 2})
            results.append(plus(block(z), got_own, last))
        else:
            up = down = None
            for s in range(1, count):
                rising = block(count + z - s)
                falling = block(z - count + s)
                if up is not None:
                    rising, falling = plus(rising, up), plus(falling, down)
                up, down = to_up(rising), to_down(falling)
            results.append(plus(block(z), up, down))
    if not paired:
        return results[0]
    swap = lambda test, a, b: (jnp.where(test, b, a), jnp.where(test, a, b))
    e0, e1, e2, e3 = results
    odd = c % 2 == 1
    low = jnp.concatenate(swap(odd, e0, e1), 1)
    high = jnp.concatenate(swap(odd, e2, e3), 1)
    return jnp.concatenate(swap(c >= 2, low, high), 1)


def solution(mesh):
    in_specs = (
        P(axes, None),
        P(),
        P("context", None, "tensor"),
        P(None, None, "tensor"),
        P(None, "tensor"),
        P("tensor"),
        P("context", "tensor"),
    )
    return jax.shard_map(
        local, mesh=mesh, in_specs=in_specs, out_specs=P(axes, None), check_vma=False
    )
```

```python
import functools
import jax
import jax.numpy as jnp
import ml_dtypes
import numpy as np
from jax import lax
from jax.experimental import pallas as pl
from jax.experimental.pallas import tpu as pltpu
from jax.sharding import PartitionSpec as P

norm_epsilon = 1e-06
axes = ("groups", "context", "tensor")
edge = 16
f32 = jnp.float32
bf16 = jnp.bfloat16


def split_parts(matrix):
    high = matrix.astype(ml_dtypes.bfloat16)
    low = (matrix - high.astype(np.float64)).astype(ml_dtypes.bfloat16)
    return high, low


def fourier_tables(taps):
    size = 2 * taps
    freq = np.arange(taps)[:, None]
    time = np.arange(size)[None, :]
    angle = 2 * np.pi * ((freq * time) % size) / size
    cosine, sine = np.cos(angle), np.sin(angle)
    sine[0] = 1.0 - 2.0 * (np.arange(size) % 2)
    forward = np.concatenate([cosine, sine], axis=0)
    weight = np.full((2 * taps, 1), 2.0 / size)
    weight[0] = weight[taps] = 1.0 / size
    inverse = (forward * weight)[:, taps:].T
    fh, fl = split_parts(forward[:, :taps])
    ih, il = split_parts(inverse)
    return np.concatenate([fh, fl], axis=1), np.concatenate([ih, ih, il], axis=1)


def short_sum(s, taps_ref, branch, slab):
    total = None
    for lag in range(taps_ref.shape[0]):
        term = taps_ref[lag, branch][None] * s[edge - lag : edge - lag + slab]
        total = term if total is None else total + term
    return total


def norm_kernel(x_ref, gain_ref, out_ref):
    values = x_ref[...].astype(f32)
    mean = jnp.mean(values * values, axis=1, keepdims=True)
    scaled = values * lax.rsqrt(mean + norm_epsilon)
    out_ref[...] = (scaled * gain_ref[...].astype(f32)).astype(bf16)


def norm(tokens, gain):
    length, features = tokens.shape
    rows = min(length, 32)
    return pl.pallas_call(
        norm_kernel,
        grid=(length // rows,),
        in_specs=[
            pl.BlockSpec((rows, features), lambda i: (i, 0)),
            pl.BlockSpec((1, features), lambda i: (0, 0)),
        ],
        out_specs=pl.BlockSpec((rows, features), lambda i: (i, 0)),
        out_shape=jax.ShapeDtypeStruct((length, features), bf16),
        compiler_params=pltpu.CompilerParams(vmem_limit_bytes=8 << 20),
        name="norm",
    )(tokens, gain.reshape(1, features))


in_hbm = pl.BlockSpec(memory_space=pltpu.MemorySpace.HBM)
in_vmem = pl.BlockSpec(memory_space=pltpu.MemorySpace.VMEM)
in_smem = pl.BlockSpec(memory_space=pltpu.MemorySpace.SMEM)


def hold(array):
    return pltpu.with_memory_space_constraint(array, pltpu.MemorySpace.HBM)


def pack_kernel(kinds, at_ref, *rest):
    arrays = rest[: len(kinds)]
    out_ref, sems = rest[-2:]
    copies = []
    for n, ((branch, depth), array) in enumerate(zip(kinds, arrays)):
        source = array if branch is None else array.at[branch]
        rows = pl.ds(pl.multiple_of(at_ref[n], min(depth, 256)), depth)
        copies.append(pltpu.make_async_copy(source, out_ref.at[rows], sems.at[n]))
    for copy in copies:
        copy.start()
    for copy in copies:
        copy.wait()


def pack(pieces, features, base=None):
    channels = pieces[0][0].shape[-1]
    kinds = tuple((branch, array.shape[-2]) for array, branch, _ in pieces)
    at = jnp.stack([jnp.asarray(p[2], jnp.int32) for p in pieces])
    operands = [at] + [hold(p[0]) for p in pieces] + ([] if base is None else [base])
    specs = [in_smem] + [in_hbm] * len(pieces) + ([] if base is None else [in_vmem])
    return pl.pallas_call(
        functools.partial(pack_kernel, kinds),
        in_specs=specs,
        out_specs=in_vmem,
        out_shape=pltpu.VMEM((features, channels), bf16),
        scratch_shapes=[pltpu.SemaphoreType.DMA((len(pieces),))],
        input_output_aliases={} if base is None else {len(operands) - 1: 0},
        compiler_params=pltpu.CompilerParams(vmem_limit_bytes=1 << 20),
        name="pack",
    )(*operands)


def gate_kernel(width, x_ref, one_ref, two_ref, taps_ref, gated_ref, head_ref, halo_ref, full, s, sem):
    slab, channels = gated_ref.shape
    count = halo_ref.shape[0] - 2 * edge
    load = pltpu.make_async_copy(x_ref, full, sem.at[0])
    load.start()
    load.wait()
    for i in range(channels // width):
        columns = slice(i * width, (i + 1) * width)
        taps = taps_ref[:, :, columns]
        feats = []
        for k, weight in enumerate((one_ref, two_ref)):
            s[k, 0:edge] = jnp.zeros((edge, width), f32)
            term = jnp.dot(full[...], weight[:, columns], preferred_element_type=f32)
            s[k, edge : edge + slab] = term.astype(bf16).astype(f32)
            head_ref[k, :, columns] = s[k, edge : 2 * edge].astype(bf16)
            rows = slice(count + k * edge, count + (k + 1) * edge)
            halo_ref[rows, columns] = s[k, slab : slab + edge].astype(bf16)
            feats.append(short_sum(s.at[k], taps, k + 1, slab))
        gated = (feats[0] * feats[1]).astype(bf16)
        gated_ref[:, columns] = gated
        halo_ref[0:count, columns] = gated[slab - count :]


def gate(x, one, two, short_filter, taps, width):
    slab, features = x.shape
    channels = short_filter.shape[-1]
    return pl.pallas_call(
        functools.partial(gate_kernel, width),
        in_specs=[in_hbm, in_vmem, in_vmem, in_vmem],
        out_specs=[in_vmem] * 3,
        out_shape=[
            jax.ShapeDtypeStruct((slab, channels), bf16),
            jax.ShapeDtypeStruct((2, edge, channels), bf16),
            jax.ShapeDtypeStruct((taps + 2 * edge, channels), bf16),
        ],
        scratch_shapes=[
            pltpu.VMEM((slab, features), bf16),
            pltpu.VMEM((2, slab + edge, width), f32),
            pltpu.SemaphoreType.DMA((1,)),
        ],
        compiler_params=pltpu.CompilerParams(vmem_limit_bytes=16 << 20),
        name="gate",
    )(hold(x), one, two, short_filter)


def query_kernel(width, x_ref, before_ref, weight_ref, taps_ref, out_ref, full, s, sem):
    slab, channels = out_ref.shape
    loads = [
        pltpu.make_async_copy(before_ref, full.at[0:edge], sem.at[0]),
        pltpu.make_async_copy(x_ref, full.at[edge : edge + slab], sem.at[1]),
    ]
    for load in loads:
        load.start()
    for load in loads:
        load.wait()
    for i in range(channels // width):
        columns = slice(i * width, (i + 1) * width)
        term = jnp.dot(full[...], weight_ref[:, columns], preferred_element_type=f32)
        s[...] = term.astype(bf16).astype(f32)
        out_ref[:, columns] = short_sum(s, taps_ref[:, :, columns], 0, slab)


def query(x, before, weight, short_filter, width):
    slab, features = x.shape
    channels = short_filter.shape[-1]
    return pl.pallas_call(
        functools.partial(query_kernel, width),
        in_specs=[in_hbm, in_hbm, in_vmem, in_vmem],
        out_specs=in_vmem,
        out_shape=jax.ShapeDtypeStruct((slab, channels), f32),
        scratch_shapes=[
            pltpu.VMEM((slab + edge, features), bf16),
            pltpu.VMEM((slab + edge, width), f32),
            pltpu.SemaphoreType.DMA((2,)),
        ],
        compiler_params=pltpu.CompilerParams(vmem_limit_bytes=16 << 20),
        name="query",
    )(hold(x), hold(before), weight, short_filter)


def transform(fwd_ref, block):
    return jnp.dot(fwd_ref[...], jnp.concatenate([block, block], axis=0), preferred_element_type=f32)


def respond_kernel(filter_ref, decay_ref, fwd_ref, out_ref):
    taps = filter_ref.shape[0]
    lag = lax.broadcasted_iota(jnp.int32, (taps, 1), 0)
    faded = filter_ref[...] * jnp.exp(-decay_ref[...] * lag.astype(f32))
    response = transform(fwd_ref, faded.astype(bf16))
    h_cos, h_sin = response[:taps], response[taps:]
    out_ref[0] = h_cos
    out_ref[1] = jnp.where(lag == 0, 0.0, h_sin)
    out_ref[2] = jnp.where(lag == 0, h_sin, h_cos)


def respond(medium_filter, decay, forward, width):
    taps, channels = medium_filter.shape
    return pl.pallas_call(
        respond_kernel,
        grid=(channels // width,),
        in_specs=[
            pl.BlockSpec((taps, width), lambda i: (0, i)),
            pl.BlockSpec((1, width), lambda i: (0, i)),
            pl.BlockSpec(forward.shape, lambda i: (0, 0)),
        ],
        out_specs=pl.BlockSpec((3, taps, width), lambda i: (0, 0, i)),
        out_shape=jax.ShapeDtypeStruct((3, taps, channels), f32),
        compiler_params=pltpu.CompilerParams(vmem_limit_bytes=8 << 20),
        name="respond",
    )(medium_filter, decay.reshape(1, channels), forward)


def mix_kernel(
    gated_ref, halo_ref, head_ref, short_ref, response_ref, query_ref, fwd_ref, inv_ref, out_ref, s
):
    taps = response_ref.shape[1]
    blocks = gated_ref.shape[0] // taps
    feats = []
    for k in range(2):
        s[0:edge] = halo_ref[taps + k * edge : taps + (k + 1) * edge].astype(f32)
        s[edge : 2 * edge] = head_ref[k].astype(f32)
        total = None
        for lag in range(short_ref.shape[0]):
            term = short_ref[lag, k + 1][None] * s[edge - lag : 2 * edge - lag]
            total = term if total is None else total + term
        feats.append(total)
    first = (feats[0] * feats[1]).astype(bf16)

    row = lax.broadcasted_iota(jnp.int32, (2 * taps, 1), 0)
    sign = jnp.where(row % 2 == 0, 1.0, -1.0).astype(f32)
    h_cos, h_sin, h_low = response_ref[0], response_ref[1], response_ref[2]
    last = transform(fwd_ref, halo_ref[0:taps])
    for b in range(blocks):
        if b == 0:
            block = jnp.concatenate([first, gated_ref[edge:taps]], axis=0)
        else:
            block = gated_ref[b * taps : (b + 1) * taps]
        now = transform(fwd_ref, block)
        x = last + sign * now
        last = now
        x_cos, x_sin = x[:taps], x[taps:]
        y = jnp.concatenate([x_cos * h_cos - x_sin * h_sin, x_sin * h_low + x_cos * h_sin], axis=0)
        high = y.astype(bf16)
        low = (y - high.astype(f32)).astype(bf16)
        mixed = jnp.dot(
            inv_ref[...], jnp.concatenate([high, low, high], axis=0), preferred_element_type=f32
        )
        at = slice(b * taps, (b + 1) * taps)
        out_ref[at] = (query_ref[at] * mixed).astype(bf16)


def mix(gated, halo, head, short_filter, response, query_rows, tables, width):
    slab, channels = gated.shape
    count = response.shape[1]
    forward, inverse = tables
    col = lambda rows: pl.BlockSpec((rows, width), lambda i: (0, i))
    cube = lambda a, b: pl.BlockSpec((a, b, width), lambda i: (0, 0, i))
    return pl.pallas_call(
        mix_kernel,
        grid=(channels // width,),
        in_specs=[
            col(slab),
            col(count + 2 * edge),
            cube(2, edge),
            cube(*short_filter.shape[:2]),
            cube(3, count),
            col(slab),
            pl.BlockSpec(forward.shape, lambda i: (0, 0)),
            pl.BlockSpec(inverse.shape, lambda i: (0, 0)),
        ],
        out_specs=col(slab),
        out_shape=jax.ShapeDtypeStruct((slab, channels), bf16),
        scratch_shapes=[pltpu.VMEM((2 * edge, width), f32)],
        compiler_params=pltpu.CompilerParams(vmem_limit_bytes=16 << 20),
        name="mix",
    )(gated, halo, head, short_filter, response, query_rows, forward, inverse)


def local(tokens, norm_gain, w_in, short_filter, medium_filter, decay, w_out):
    groups, contexts, count = (lax.axis_size(a) for a in axes)
    g, c, z = (lax.axis_index(a) for a in axes)
    length, features = tokens.shape
    rows, branches, channels = w_in.shape
    slab = length * count
    width = min(channels, 256)
    paired = contexts == 4 and groups == 2

    def move(value, target):
        pairs = []
        for i in range(groups):
            for j in range(contexts):
                for k in range(count):
                    to = target(i, j, k)
                    if 0 <= to[1] < contexts and 0 <= to[2] < count:
                        pairs.append(
                            ((i * contexts + j) * count + k, (to[0] * contexts + to[1]) * count + to[2])
                        )
        return lax.ppermute(value, axes, pairs)

    to_chip = lambda v: move(v, lambda i, j, k: (i, j ^ 2, k))
    to_core = lambda v: move(v, lambda i, j, k: (i, j ^ 1, k))
    to_group = lambda v: move(v, lambda i, j, k: (1 - i, j, k))
    to_next = lambda v: move(v, lambda i, j, k: (i, j + 1, k))
    send = lambda v, pairs: move(v, lambda i, j, k: (i, j, pairs.get(k, -1)))
    to_up = lambda v: move(v, lambda i, j, k: (i, j, k + 1))
    to_down = lambda v: move(v, lambda i, j, k: (i, j, k - 1))

    def after(value, *earlier):
        return lax.optimization_barrier((value, *earlier))[0]

    def spread_last(value):
        value = move(
            value, lambda i, j, k: (i, j + 1, k) if k == count - 1 else (i, -1, k)
        )
        held = 1
        while held < count:
            first, last = max(0, count - 2 * held), count - held
            value = value + move(
                value,
                lambda i, j, k: (i, j, k - held) if k - held >= first and k >= last else (i, j, -1),
            )
            held += last - first
        return value

    medium_count = medium_filter.shape[0]
    tables = fourier_tables(medium_count)
    weights = jnp.transpose(w_in, (1, 0, 2))
    half = rows // 2
    out_rows = w_out.shape[0]
    out_half = out_rows // 2
    if paired:
        first_half, other_half = g * half, (1 - g) * half
        peer = to_core(weights)
        near, far, packed = {}, {}, {}
        order = (1, 2, 0)
        for n, b in enumerate(order):
            source = after(weights, normed) if n else weights
            mine = lax.dynamic_slice(source, (b, first_half, 0), (1, half, channels))
            mine = mine.reshape(half, channels)
            if n == 0:
                normed = norm(after(tokens, mine), norm_gain)
                response = respond(medium_filter, decay, tables[0], width)
                before_rows = spread_last(normed[length - edge :])
            else:
                mine = after(mine, near[order[n - 1]])
            near[b] = to_chip(mine)
            if n == 0:
                ready = near[b]
            elif n == 1:
                ready = after(near[b], far[1], response, before_rows)
            else:
                ready = after(near[b], far[2], packed[1])
            far[b] = to_group(ready)
            packed[b] = pack(
                [
                    (weights, b, c * rows),
                    (peer, b, (c ^ 1) * rows),
                    (near[b], None, (c ^ 2) * rows + first_half),
                    (to_core(near[b]), None, (c ^ 3) * rows + first_half),
                ],
                features,
            )
            if b == 1:
                packed[b] = pack(
                    [
                        (far[b], None, (c ^ 2) * rows + other_half),
                        (to_core(far[b]), None, (c ^ 3) * rows + other_half),
                    ],
                    features,
                    packed[b],
                )
        far_two = after(far[2], packed[2])
        packed[2] = pack(
            [
                (far_two, None, (c ^ 2) * rows + other_half),
                (to_core(far_two), None, (c ^ 3) * rows + other_half),
            ],
            features,
            packed[2],
        )
    else:
        normed = norm(tokens, norm_gain)
        response = respond(medium_filter, decay, tables[0], width)
        before_rows = spread_last(normed[length - edge :])
        full = lax.all_gather(weights, "context", axis=1, tiled=True)
        packed = {b: pack([(full, b, 0)], features) for b in range(branches)}

    gathered = lax.all_gather(normed, "tensor", axis=0, tiled=True)
    if paired:
        gate_taps = after(short_filter, response, packed[0])
    else:
        gate_taps = short_filter
    gated, head, edges = gate(gathered, packed[1], packed[2], gate_taps, medium_count, width)
    halo = to_next(edges)
    if paired:
        far_zero = after(far[0], gated)
        packed[0] = pack(
            [
                (far_zero, None, (c ^ 2) * rows + other_half),
                (to_core(far_zero), None, (c ^ 3) * rows + other_half),
            ],
            features,
            packed[0],
        )
    query_rows = query(gathered, before_rows, packed[0], short_filter, width)
    combined = mix(gated, halo, head, short_filter, response, query_rows, tables, width)
    if paired:
        mine = lax.dynamic_slice(w_out, (g * out_half, 0), (out_half, channels))
        chips = [[0, 2], [1, 3]]
        pair = lax.all_gather(
            after(mine, near[1]), "context", axis=0, tiled=True, axis_index_groups=chips
        )
        pair = after(pair, query_rows)
        near_out = lax.dynamic_slice(pair, ((1 - c // 2) * out_half, 0), (out_half, channels))
        far_out = to_group(near_out)
        out_peer = to_core(after(w_out, gated))
        near_core = to_core(near_out)

        def last_parts(earlier):
            late = after(far_out, earlier[1])
            return [late, to_core(late)]

        sets = [
            lambda _: [w_out],
            lambda _: [out_peer],
            lambda _: [near_out, near_core],
            last_parts,
        ]
    else:
        sets = [lambda _: [lax.all_gather(w_out, "context", axis=0, tiled=True)]]

    def plus(*terms):
        total = terms[0].astype(f32)
        for term in terms[1:]:
            total = total + term.astype(f32)
        return total.astype(bf16)

    results, partial, firsts, pending = [], [], [], []
    for make in sets:
        parts = make(firsts)
        partial = [
            lax.dot_general(
                combined, part, (((1,), (1,)), ((), ())), preferred_element_type=f32
            ).astype(bf16)
            for part in parts
        ]
        combined = after(combined, *partial)

        def block(index, blocks=1, partial=partial):
            index = jnp.clip(index, 0, count - blocks)
            return jnp.concatenate(
                [
                    lax.dynamic_slice(p, (index * length, 0), (blocks * length, p.shape[1]))
                    for p in partial
                ],
                1,
            )

        if count == 4:
            far_pair = block(jnp.where(z < 2, 2, 0), 2)
            firsts.append(send(far_pair, {0: 1, 3: 2}))
            pending.append((far_pair, block(z), block(z ^ 1), partial[0]))
        else:
            up = down = None
            for s in range(1, count):
                rising = block(count + z - s)
                falling = block(z - count + s)
                if up is not None:
                    rising, falling = plus(rising, up), plus(falling, down)
                up, down = to_up(rising), to_down(falling)
            results.append(plus(block(z), up, down))
    for n, (far_pair, own, other, _) in enumerate(pending):
        got = plus(far_pair, firsts[n])
        if n + 1 < len(pending) - 1:
            got = after(got, pending[n + 1][3])
        got = send(got, {1: 2, 2: 1})
        low, high = got[:length], got[length:]
        odd = z % 2 == 1
        got_own = jnp.where(odd, high, low)
        got_other = jnp.where(odd, low, high)
        last = send(plus(other, got_other), {0: 1, 1: 0, 2: 3, 3: 2})
        results.append(plus(own, got_own, last))
    if not paired:
        return results[0]
    swap = lambda test, a, b: (jnp.where(test, b, a), jnp.where(test, a, b))
    e0, e1, e2, e3 = results
    e2, e3 = (
        jnp.concatenate(swap(g == 1, e2[:, at], e3[:, at]), 1)
        for at in (slice(0, out_half), slice(out_half, None))
    )
    odd = c % 2 == 1
    low = jnp.concatenate(swap(odd, e0, e1), 1)
    high = jnp.concatenate(swap(odd, e2, e3), 1)
    return jnp.concatenate(swap(c >= 2, low, high), 1)


def solution(mesh):
    in_specs = (
        P(axes, None),
        P(),
        P("context", None, "tensor"),
        P(None, None, "tensor"),
        P(None, "tensor"),
        P("tensor"),
        P("context", "tensor"),
    )
    return jax.shard_map(
        local, mesh=mesh, in_specs=in_specs, out_specs=P(axes, None), check_vma=False
    )
```

```python
import functools
import jax
import jax.numpy as jnp
import ml_dtypes
import numpy as np
from jax import lax
from jax.experimental import pallas as pl
from jax.experimental.pallas import tpu as pltpu
from jax.sharding import PartitionSpec as P

norm_epsilon = 1e-06
axes = ("groups", "context", "tensor")
edge = 16
f32 = jnp.float32
bf16 = jnp.bfloat16


def split_parts(matrix):
    high = matrix.astype(ml_dtypes.bfloat16)
    low = (matrix - high.astype(np.float64)).astype(ml_dtypes.bfloat16)
    return high, low


def fourier_tables(taps):
    size = 2 * taps
    freq = np.arange(taps)[:, None]
    time = np.arange(size)[None, :]
    angle = 2 * np.pi * ((freq * time) % size) / size
    cosine, sine = np.cos(angle), np.sin(angle)
    sine[0] = 1.0 - 2.0 * (np.arange(size) % 2)
    forward = np.concatenate([cosine, sine], axis=0)
    weight = np.full((2 * taps, 1), 2.0 / size)
    weight[0] = weight[taps] = 1.0 / size
    inverse = (forward * weight)[:, taps:].T
    fh, fl = split_parts(forward[:, :taps])
    ih, il = split_parts(inverse)
    return np.concatenate([fh, fl], axis=1), np.concatenate([ih, ih, il], axis=1)


def short_sum(s, taps_ref, branch, slab):
    total = None
    for lag in range(taps_ref.shape[0]):
        term = taps_ref[lag, branch][None] * s[edge - lag : edge - lag + slab]
        total = term if total is None else total + term
    return total


def norm_kernel(x_ref, gain_ref, out_ref):
    values = x_ref[...].astype(f32)
    mean = jnp.mean(values * values, axis=1, keepdims=True)
    scaled = values * lax.rsqrt(mean + norm_epsilon)
    out_ref[...] = (scaled * gain_ref[...].astype(f32)).astype(bf16)


def norm(tokens, gain):
    length, features = tokens.shape
    rows = min(length, 32)
    return pl.pallas_call(
        norm_kernel,
        grid=(length // rows,),
        in_specs=[
            pl.BlockSpec((rows, features), lambda i: (i, 0)),
            pl.BlockSpec((1, features), lambda i: (0, 0)),
        ],
        out_specs=pl.BlockSpec((rows, features), lambda i: (i, 0)),
        out_shape=jax.ShapeDtypeStruct((length, features), bf16),
        compiler_params=pltpu.CompilerParams(vmem_limit_bytes=8 << 20),
        name="norm",
    )(tokens, gain.reshape(1, features))


in_hbm = pl.BlockSpec(memory_space=pltpu.MemorySpace.HBM)
in_vmem = pl.BlockSpec(memory_space=pltpu.MemorySpace.VMEM)
in_smem = pl.BlockSpec(memory_space=pltpu.MemorySpace.SMEM)


def hold(array):
    return pltpu.with_memory_space_constraint(array, pltpu.MemorySpace.HBM)


def kinds_of(pieces):
    return tuple((branch, array.shape[-2]) for array, branch, _ in pieces)


def offsets(pieces):
    return jnp.stack([jnp.asarray(p[2], jnp.int32) for p in pieces])


def spans(kinds):
    start = 0
    for _, depth in kinds:
        yield start, start + depth
        start += depth


def token_copies(kinds, at_ref, x_ref, target, sems):
    copies = []
    for n, (low, high) in enumerate(spans(kinds)):
        columns = pl.ds(pl.multiple_of(at_ref[n], min(high - low, 256)), high - low)
        copies.append(
            pltpu.make_async_copy(x_ref.at[:, columns], target.at[:, low:high], sems.at[n])
        )
    return copies


def weight_copies(kinds, arrays, target, sems):
    copies = []
    for n, (low, high) in enumerate(spans(kinds)):
        branch = kinds[n][0]
        source = arrays[n] if branch is None else arrays[n].at[branch]
        copies.append(pltpu.make_async_copy(source, target.at[low:high], sems.at[n]))
    return copies


def add_up(kinds, width, waits, full, weight, s, first):
    channels = weight.shape[1]
    for n, (low, high) in enumerate(spans(kinds)):
        for copies in waits:
            copies[n].wait()
        for i in range(channels // width):
            columns = slice(i * width, (i + 1) * width)
            term = jnp.dot(
                full[:, low:high], weight[low:high, columns], preferred_element_type=f32
            )
            if n > 0:
                term = s[first:, columns] + term
            if n == len(kinds) - 1:
                term = term.astype(bf16).astype(f32)
            s[first:, columns] = term


def gate_kernel(one, two, width, at_ref, x_ref, taps_ref, *rest):
    arrays = rest[: len(one) + len(two)]
    gated_ref, head_ref, halo_ref, full, weights, s1, feat, s2, sems = rest[len(arrays) :]
    slab, channels = gated_ref.shape
    count = halo_ref.shape[0] - 2 * edge
    x_copies = token_copies(one, at_ref, x_ref, full, sems.at[0])
    copies = [
        weight_copies(one, arrays[: len(one)], weights.at[0], sems.at[1]),
        weight_copies(two, arrays[len(one) :], weights.at[1], sems.at[2]),
    ]
    for x_copy, copy in zip(x_copies, copies[0]):
        x_copy.start()
        copy.start()
    for copy in copies[1]:
        copy.start()
    s1[0:edge] = jnp.zeros((edge, channels), f32)
    add_up(one, width, (x_copies, copies[0]), full, weights.at[0], s1, edge)
    head_ref[0] = s1[edge : 2 * edge].astype(bf16)
    halo_ref[count : count + edge] = s1[slab : slab + edge].astype(bf16)
    feat[...] = short_sum(s1, taps_ref, 1, slab)
    for copy in copies[1]:
        copy.wait()
    s2[0:edge] = jnp.zeros((edge, width), f32)
    for i in range(channels // width):
        columns = slice(i * width, (i + 1) * width)
        term = jnp.dot(full[...], weights[1, :, columns], preferred_element_type=f32)
        s2[edge : edge + slab] = term.astype(bf16).astype(f32)
        head_ref[1, :, columns] = s2[edge : 2 * edge].astype(bf16)
        halo_ref[count + edge :, columns] = s2[slab : slab + edge].astype(bf16)
        gated = feat[:, columns] * short_sum(s2, taps_ref[:, :, columns], 2, slab)
        gated = gated.astype(bf16)
        gated_ref[:, columns] = gated
        halo_ref[0:count, columns] = gated[slab - count :]


def gate(x, one, two, short_filter, taps, width):
    slab, features = x.shape
    channels = short_filter.shape[-1]
    return pl.pallas_call(
        functools.partial(gate_kernel, kinds_of(one), kinds_of(two), width),
        in_specs=[in_smem, in_hbm, in_vmem] + [in_hbm] * (len(one) + len(two)),
        out_specs=[in_vmem] * 3,
        out_shape=[
            jax.ShapeDtypeStruct((slab, channels), bf16),
            jax.ShapeDtypeStruct((2, edge, channels), bf16),
            jax.ShapeDtypeStruct((taps + 2 * edge, channels), bf16),
        ],
        scratch_shapes=[
            pltpu.VMEM((slab, features), bf16),
            pltpu.VMEM((2, features, channels), bf16),
            pltpu.VMEM((slab + edge, channels), f32),
            pltpu.VMEM((slab, channels), f32),
            pltpu.VMEM((slab + edge, width), f32),
            pltpu.SemaphoreType.DMA((3, len(one))),
        ],
        compiler_params=pltpu.CompilerParams(vmem_limit_bytes=40 << 20),
        name="gate",
    )(offsets(one), hold(x), short_filter, *[hold(p[0]) for p in one + two])


def query_kernel(kinds, width, at_ref, x_ref, before_ref, taps_ref, *rest):
    arrays = rest[: len(kinds)]
    out_ref, full, weight, s, sems = rest[len(arrays) :]
    slab, channels = out_ref.shape
    x_copies = token_copies(kinds, at_ref, x_ref, full.at[edge : edge + slab], sems.at[0])
    e_copies = token_copies(kinds, at_ref, before_ref, full.at[0:edge], sems.at[1])
    copies = weight_copies(kinds, arrays, weight, sems.at[2])
    for group in zip(e_copies, x_copies, copies):
        for copy in group:
            copy.start()
    add_up(kinds, width, (e_copies, x_copies, copies), full, weight, s, 0)
    out_ref[...] = short_sum(s, taps_ref, 0, slab)


def query(x, before, pieces, short_filter, width):
    slab, features = x.shape
    channels = short_filter.shape[-1]
    return pl.pallas_call(
        functools.partial(query_kernel, kinds_of(pieces), width),
        in_specs=[in_smem, in_hbm, in_hbm, in_vmem] + [in_hbm] * len(pieces),
        out_specs=in_vmem,
        out_shape=jax.ShapeDtypeStruct((slab, channels), f32),
        scratch_shapes=[
            pltpu.VMEM((slab + edge, features), bf16),
            pltpu.VMEM((features, channels), bf16),
            pltpu.VMEM((slab + edge, channels), f32),
            pltpu.SemaphoreType.DMA((3, len(pieces))),
        ],
        compiler_params=pltpu.CompilerParams(vmem_limit_bytes=32 << 20),
        name="query",
    )(offsets(pieces), hold(x), hold(before), short_filter, *[hold(p[0]) for p in pieces])


def transform(fwd_ref, block):
    return jnp.dot(fwd_ref[...], jnp.concatenate([block, block], axis=0), preferred_element_type=f32)


def respond_kernel(filter_ref, decay_ref, fwd_ref, out_ref):
    taps = filter_ref.shape[0]
    lag = lax.broadcasted_iota(jnp.int32, (taps, 1), 0)
    faded = filter_ref[...] * jnp.exp(-decay_ref[...] * lag.astype(f32))
    response = transform(fwd_ref, faded.astype(bf16))
    h_cos, h_sin = response[:taps], response[taps:]
    out_ref[0] = h_cos
    out_ref[1] = jnp.where(lag == 0, 0.0, h_sin)
    out_ref[2] = jnp.where(lag == 0, h_sin, h_cos)


def respond(medium_filter, decay, forward, width):
    taps, channels = medium_filter.shape
    return pl.pallas_call(
        respond_kernel,
        grid=(channels // width,),
        in_specs=[
            pl.BlockSpec((taps, width), lambda i: (0, i)),
            pl.BlockSpec((1, width), lambda i: (0, i)),
            pl.BlockSpec(forward.shape, lambda i: (0, 0)),
        ],
        out_specs=pl.BlockSpec((3, taps, width), lambda i: (0, 0, i)),
        out_shape=jax.ShapeDtypeStruct((3, taps, channels), f32),
        compiler_params=pltpu.CompilerParams(vmem_limit_bytes=8 << 20),
        name="respond",
    )(medium_filter, decay.reshape(1, channels), forward)


def mix_kernel(
    gated_ref, halo_ref, head_ref, short_ref, response_ref, query_ref, fwd_ref, inv_ref, out_ref, s
):
    taps = response_ref.shape[1]
    blocks = gated_ref.shape[0] // taps
    feats = []
    for k in range(2):
        s[0:edge] = halo_ref[taps + k * edge : taps + (k + 1) * edge].astype(f32)
        s[edge : 2 * edge] = head_ref[k].astype(f32)
        total = None
        for lag in range(short_ref.shape[0]):
            term = short_ref[lag, k + 1][None] * s[edge - lag : 2 * edge - lag]
            total = term if total is None else total + term
        feats.append(total)
    first = (feats[0] * feats[1]).astype(bf16)

    row = lax.broadcasted_iota(jnp.int32, (2 * taps, 1), 0)
    sign = jnp.where(row % 2 == 0, 1.0, -1.0).astype(f32)
    h_cos, h_sin, h_low = response_ref[0], response_ref[1], response_ref[2]
    last = transform(fwd_ref, halo_ref[0:taps])
    for b in range(blocks):
        if b == 0:
            block = jnp.concatenate([first, gated_ref[edge:taps]], axis=0)
        else:
            block = gated_ref[b * taps : (b + 1) * taps]
        now = transform(fwd_ref, block)
        x = last + sign * now
        last = now
        x_cos, x_sin = x[:taps], x[taps:]
        y = jnp.concatenate([x_cos * h_cos - x_sin * h_sin, x_sin * h_low + x_cos * h_sin], axis=0)
        high = y.astype(bf16)
        low = (y - high.astype(f32)).astype(bf16)
        mixed = jnp.dot(
            inv_ref[...], jnp.concatenate([high, low, high], axis=0), preferred_element_type=f32
        )
        at = slice(b * taps, (b + 1) * taps)
        out_ref[at] = (query_ref[at] * mixed).astype(bf16)


def mix(gated, halo, head, short_filter, response, query_rows, tables, width):
    slab, channels = gated.shape
    count = response.shape[1]
    forward, inverse = tables
    col = lambda rows: pl.BlockSpec((rows, width), lambda i: (0, i))
    cube = lambda a, b: pl.BlockSpec((a, b, width), lambda i: (0, 0, i))
    return pl.pallas_call(
        mix_kernel,
        grid=(channels // width,),
        in_specs=[
            col(slab),
            col(count + 2 * edge),
            cube(2, edge),
            cube(*short_filter.shape[:2]),
            cube(3, count),
            col(slab),
            pl.BlockSpec(forward.shape, lambda i: (0, 0)),
            pl.BlockSpec(inverse.shape, lambda i: (0, 0)),
        ],
        out_specs=col(slab),
        out_shape=jax.ShapeDtypeStruct((slab, channels), bf16),
        scratch_shapes=[pltpu.VMEM((2 * edge, width), f32)],
        compiler_params=pltpu.CompilerParams(vmem_limit_bytes=16 << 20),
        name="mix",
    )(gated, halo, head, short_filter, response, query_rows, forward, inverse)


def local(tokens, norm_gain, w_in, short_filter, medium_filter, decay, w_out):
    groups, contexts, count = (lax.axis_size(a) for a in axes)
    g, c, z = (lax.axis_index(a) for a in axes)
    length, features = tokens.shape
    rows, branches, channels = w_in.shape
    slab = length * count
    width = min(channels, 256)
    paired = contexts == 4 and groups == 2

    def move(value, target):
        pairs = []
        for i in range(groups):
            for j in range(contexts):
                for k in range(count):
                    to = target(i, j, k)
                    if 0 <= to[1] < contexts and 0 <= to[2] < count:
                        pairs.append(
                            ((i * contexts + j) * count + k, (to[0] * contexts + to[1]) * count + to[2])
                        )
        return lax.ppermute(value, axes, pairs)

    to_chip = lambda v: move(v, lambda i, j, k: (i, j ^ 2, k))
    to_core = lambda v: move(v, lambda i, j, k: (i, j ^ 1, k))
    to_group = lambda v: move(v, lambda i, j, k: (1 - i, j, k))
    to_next = lambda v: move(v, lambda i, j, k: (i, j + 1, k))
    send = lambda v, pairs: move(v, lambda i, j, k: (i, j, pairs.get(k, -1)))
    to_up = lambda v: move(v, lambda i, j, k: (i, j, k + 1))
    to_down = lambda v: move(v, lambda i, j, k: (i, j, k - 1))

    def after(value, *earlier):
        return lax.optimization_barrier((value, *earlier))[0]

    medium_count = medium_filter.shape[0]
    tables = fourier_tables(medium_count)
    weights = jnp.transpose(w_in, (1, 0, 2))
    half = rows // 2
    out_rows = w_out.shape[0]
    out_half = out_rows // 2
    if paired:
        first_half, other_half = g * half, (1 - g) * half
        peer = to_core(weights)
        near, far, pieces = {}, {}, {}
        order = (1, 2, 0)
        for n, b in enumerate(order):
            source = after(weights, normed) if n else weights
            mine = lax.dynamic_slice(source, (b, first_half, 0), (1, half, channels))
            mine = mine.reshape(half, channels)
            if n == 0:
                normed = norm(after(tokens, mine), norm_gain)
                response = respond(medium_filter, decay, tables[0], width)
            else:
                mine = after(mine, near[order[n - 1]])
            near[b] = to_chip(mine)
            if n == 0:
                ready = near[b]
            elif n == 1:
                ready = after(near[b], far[1], response)
            else:
                ready = after(near[b], far[2])
            far[b] = to_group(ready)
            pieces[b] = [
                (weights, b, c * rows),
                (peer, b, (c ^ 1) * rows),
                (near[b], None, (c ^ 2) * rows + first_half),
                (to_core(near[b]), None, (c ^ 3) * rows + first_half),
                (far[b], None, (c ^ 2) * rows + other_half),
            ]
            if b != 0:
                pieces[b].append((to_core(far[b]), None, (c ^ 3) * rows + other_half))
    else:
        normed = norm(tokens, norm_gain)
        response = respond(medium_filter, decay, tables[0], width)
        full = lax.all_gather(weights, "context", axis=1, tiled=True)
        pieces = {b: [(full, b, 0)] for b in range(branches)}

    gathered = lax.all_gather(normed, "tensor", axis=0, tiled=True)
    gate_taps = after(short_filter, response)
    gated, head, edges = gate(gathered, pieces[1], pieces[2], gate_taps, medium_count, width)
    before_rows = to_next(after(gathered[slab - edge :], gated))
    halo = to_next(after(edges, before_rows))
    if paired:
        far_core = to_core(after(far[0], gated))
        pieces[0].append((far_core, None, (c ^ 3) * rows + other_half))
    query_rows = query(gathered, before_rows, pieces[0], short_filter, width)
    combined = mix(gated, halo, head, short_filter, response, query_rows, tables, width)
    if paired:
        mine = lax.dynamic_slice(w_out, (g * out_half, 0), (out_half, channels))
        chips = [[0, 2], [1, 3]]
        pair = lax.all_gather(
            after(mine, near[1]), "context", axis=0, tiled=True, axis_index_groups=chips
        )
        pair = after(pair, query_rows)
        near_out = lax.dynamic_slice(pair, ((1 - c // 2) * out_half, 0), (out_half, channels))
        far_out = to_group(near_out)
        out_peer = to_core(after(w_out, gated))
        near_core = to_core(near_out)

        def last_parts(earlier):
            late = after(far_out, earlier[1])
            return [late, to_core(late)]

        sets = [
            lambda _: [w_out],
            lambda _: [out_peer],
            lambda _: [near_out, near_core],
            last_parts,
        ]
    else:
        sets = [lambda _: [lax.all_gather(w_out, "context", axis=0, tiled=True)]]

    def plus(*terms):
        total = terms[0].astype(f32)
        for term in terms[1:]:
            total = total + term.astype(f32)
        return total.astype(bf16)

    results, partial, firsts, pending = [], [], [], []
    for make in sets:
        parts = make(firsts)
        partial = [
            lax.dot_general(
                combined, part, (((1,), (1,)), ((), ())), preferred_element_type=f32
            ).astype(bf16)
            for part in parts
        ]
        combined = after(combined, *partial)

        def block(index, blocks=1, partial=partial):
            index = jnp.clip(index, 0, count - blocks)
            return jnp.concatenate(
                [
                    lax.dynamic_slice(p, (index * length, 0), (blocks * length, p.shape[1]))
                    for p in partial
                ],
                1,
            )

        if count == 4:
            far_pair = block(jnp.where(z < 2, 2, 0), 2)
            firsts.append(send(far_pair, {0: 1, 3: 2}))
            pending.append((far_pair, block(z), block(z ^ 1), partial[0]))
        else:
            up = down = None
            for s in range(1, count):
                rising = block(count + z - s)
                falling = block(z - count + s)
                if up is not None:
                    rising, falling = plus(rising, up), plus(falling, down)
                up, down = to_up(rising), to_down(falling)
            results.append(plus(block(z), up, down))
    for n, (far_pair, own, other, _) in enumerate(pending):
        got = plus(far_pair, firsts[n])
        if n + 1 < len(pending) - 1:
            got = after(got, pending[n + 1][3])
        got = send(got, {1: 2, 2: 1})
        low, high = got[:length], got[length:]
        odd = z % 2 == 1
        got_own = jnp.where(odd, high, low)
        got_other = jnp.where(odd, low, high)
        last = send(plus(other, got_other), {0: 1, 1: 0, 2: 3, 3: 2})
        results.append(plus(own, got_own, last))
    if not paired:
        return results[0]
    swap = lambda test, a, b: (jnp.where(test, b, a), jnp.where(test, a, b))
    e0, e1, e2, e3 = results
    e2, e3 = (
        jnp.concatenate(swap(g == 1, e2[:, at], e3[:, at]), 1)
        for at in (slice(0, out_half), slice(out_half, None))
    )
    odd = c % 2 == 1
    low = jnp.concatenate(swap(odd, e0, e1), 1)
    high = jnp.concatenate(swap(odd, e2, e3), 1)
    return jnp.concatenate(swap(c >= 2, low, high), 1)


def solution(mesh):
    in_specs = (
        P(axes, None),
        P(),
        P("context", None, "tensor"),
        P(None, None, "tensor"),
        P(None, "tensor"),
        P("tensor"),
        P("context", "tensor"),
    )
    return jax.shard_map(
        local, mesh=mesh, in_specs=in_specs, out_specs=P(axes, None), check_vma=False
    )
```

```python
import functools
import jax
import jax.numpy as jnp
import ml_dtypes
import numpy as np
from jax import lax
from jax.experimental import pallas as pl
from jax.experimental.pallas import tpu as pltpu
from jax.sharding import PartitionSpec as P

norm_epsilon = 1e-06
axes = ("groups", "context", "tensor")
edge = 16
f32 = jnp.float32
bf16 = jnp.bfloat16


def split_parts(matrix):
    high = matrix.astype(ml_dtypes.bfloat16)
    low = (matrix - high.astype(np.float64)).astype(ml_dtypes.bfloat16)
    return high, low


def fourier_tables(taps):
    size = 2 * taps
    freq = np.arange(taps)[:, None]
    time = np.arange(size)[None, :]
    angle = 2 * np.pi * ((freq * time) % size) / size
    cosine, sine = np.cos(angle), np.sin(angle)
    sine[0] = 1.0 - 2.0 * (np.arange(size) % 2)
    forward = np.concatenate([cosine, sine], axis=0)
    weight = np.full((2 * taps, 1), 2.0 / size)
    weight[0] = weight[taps] = 1.0 / size
    inverse = (forward * weight)[:, taps:].T
    fh, fl = split_parts(forward[:, :taps])
    ih, il = split_parts(inverse)
    return np.concatenate([fh, fl], axis=1), np.concatenate([ih, ih, il], axis=1)


def short_sum(s, taps_ref, branch, slab):
    total = None
    for lag in range(taps_ref.shape[0]):
        term = taps_ref[lag, branch][None] * s[edge - lag : edge - lag + slab]
        total = term if total is None else total + term
    return total


def norm_kernel(x_ref, gain_ref, out_ref):
    values = x_ref[...].astype(f32)
    mean = jnp.mean(values * values, axis=1, keepdims=True)
    scaled = values * lax.rsqrt(mean + norm_epsilon)
    out_ref[...] = (scaled * gain_ref[...].astype(f32)).astype(bf16)


def norm(tokens, gain):
    length, features = tokens.shape
    rows = min(length, 32)
    return pl.pallas_call(
        norm_kernel,
        grid=(length // rows,),
        in_specs=[
            pl.BlockSpec((rows, features), lambda i: (i, 0)),
            pl.BlockSpec((1, features), lambda i: (0, 0)),
        ],
        out_specs=pl.BlockSpec((rows, features), lambda i: (i, 0)),
        out_shape=jax.ShapeDtypeStruct((length, features), bf16),
        compiler_params=pltpu.CompilerParams(vmem_limit_bytes=8 << 20),
        name="norm",
    )(tokens, gain.reshape(1, features))


in_hbm = pl.BlockSpec(memory_space=pltpu.MemorySpace.HBM)
in_vmem = pl.BlockSpec(memory_space=pltpu.MemorySpace.VMEM)
in_smem = pl.BlockSpec(memory_space=pltpu.MemorySpace.SMEM)


def hold(array):
    return pltpu.with_memory_space_constraint(array, pltpu.MemorySpace.HBM)


def kinds_of(pieces):
    return tuple((branch, array.shape[-2]) for array, branch, _ in pieces)


def offsets(pieces):
    return jnp.stack([jnp.asarray(p[2], jnp.int32) for p in pieces])


def spans(kinds):
    start = 0
    for _, depth in kinds:
        yield start, start + depth
        start += depth


def token_copies(kinds, at_ref, x_ref, target, sems):
    copies = []
    for n, (low, high) in enumerate(spans(kinds)):
        columns = pl.ds(pl.multiple_of(at_ref[n], min(high - low, 256)), high - low)
        copies.append(
            pltpu.make_async_copy(x_ref.at[:, columns], target.at[:, low:high], sems.at[n])
        )
    return copies


def weight_copies(kinds, arrays, target, sems):
    copies = []
    for n, (low, high) in enumerate(spans(kinds)):
        branch = kinds[n][0]
        source = arrays[n] if branch is None else arrays[n].at[branch]
        copies.append(pltpu.make_async_copy(source, target.at[low:high], sems.at[n]))
    return copies


def add_up(kinds, width, waits, full, weight, s, first):
    channels = weight.shape[1]
    for n, (low, high) in enumerate(spans(kinds)):
        for copies in waits:
            copies[n].wait()
        for i in range(channels // width):
            columns = slice(i * width, (i + 1) * width)
            term = jnp.dot(
                full[:, low:high], weight[low:high, columns], preferred_element_type=f32
            )
            if n > 0:
                term = s[first:, columns] + term
            if n == len(kinds) - 1:
                term = term.astype(bf16).astype(f32)
            s[first:, columns] = term


def gate_kernel(one, two, width, at_ref, x_ref, taps_ref, *rest):
    arrays = rest[: len(one) + len(two)]
    gated_ref, head_ref, halo_ref, full, weights, s1, feat, s2, sems = rest[len(arrays) :]
    slab, channels = gated_ref.shape
    count = halo_ref.shape[0] - 2 * edge
    x_copies = token_copies(one, at_ref, x_ref, full, sems.at[0])
    copies = [
        weight_copies(one, arrays[: len(one)], weights.at[0], sems.at[1]),
        weight_copies(two, arrays[len(one) :], weights.at[1], sems.at[2]),
    ]
    for x_copy, copy in zip(x_copies, copies[0]):
        x_copy.start()
        copy.start()
    for copy in copies[1]:
        copy.start()
    s1[0:edge] = jnp.zeros((edge, channels), f32)
    add_up(one, width, (x_copies, copies[0]), full, weights.at[0], s1, edge)
    head_ref[0] = s1[edge : 2 * edge].astype(bf16)
    halo_ref[count : count + edge] = s1[slab : slab + edge].astype(bf16)
    feat[...] = short_sum(s1, taps_ref, 1, slab)
    for copy in copies[1]:
        copy.wait()
    s2[0:edge] = jnp.zeros((edge, width), f32)
    for i in range(channels // width):
        columns = slice(i * width, (i + 1) * width)
        term = jnp.dot(full[...], weights[1, :, columns], preferred_element_type=f32)
        s2[edge : edge + slab] = term.astype(bf16).astype(f32)
        head_ref[1, :, columns] = s2[edge : 2 * edge].astype(bf16)
        halo_ref[count + edge :, columns] = s2[slab : slab + edge].astype(bf16)
        gated = feat[:, columns] * short_sum(s2, taps_ref[:, :, columns], 2, slab)
        gated = gated.astype(bf16)
        gated_ref[:, columns] = gated
        halo_ref[0:count, columns] = gated[slab - count :]


def gate(x, one, two, short_filter, taps, width):
    slab, features = x.shape
    channels = short_filter.shape[-1]
    return pl.pallas_call(
        functools.partial(gate_kernel, kinds_of(one), kinds_of(two), width),
        in_specs=[in_smem, in_hbm, in_vmem] + [in_hbm] * (len(one) + len(two)),
        out_specs=[in_vmem] * 3,
        out_shape=[
            pltpu.MemorySpace.HBM((slab, channels), bf16),
            pltpu.MemorySpace.HBM((2, edge, channels), bf16),
            pltpu.MemorySpace.HBM((taps + 2 * edge, channels), bf16),
        ],
        scratch_shapes=[
            pltpu.VMEM((slab, features), bf16),
            pltpu.VMEM((2, features, channels), bf16),
            pltpu.VMEM((slab + edge, channels), f32),
            pltpu.VMEM((slab, channels), f32),
            pltpu.VMEM((slab + edge, width), f32),
            pltpu.SemaphoreType.DMA((3, len(one))),
        ],
        compiler_params=pltpu.CompilerParams(vmem_limit_bytes=40 << 20),
        name="gate",
    )(offsets(one), hold(x), short_filter, *[hold(p[0]) for p in one + two])


def query_kernel(kinds, width, at_ref, x_ref, before_ref, taps_ref, *rest):
    arrays = rest[: len(kinds)]
    out_ref, full, weight, s, sems = rest[len(arrays) :]
    slab, channels = out_ref.shape
    x_copies = token_copies(kinds, at_ref, x_ref, full.at[edge : edge + slab], sems.at[0])
    e_copies = token_copies(kinds, at_ref, before_ref, full.at[0:edge], sems.at[1])
    copies = weight_copies(kinds, arrays, weight, sems.at[2])
    for group in zip(e_copies, x_copies, copies):
        for copy in group:
            copy.start()
    add_up(kinds, width, (e_copies, x_copies, copies), full, weight, s, 0)
    out_ref[...] = short_sum(s, taps_ref, 0, slab)


def query(x, before, pieces, short_filter, width):
    slab, features = x.shape
    channels = short_filter.shape[-1]
    return pl.pallas_call(
        functools.partial(query_kernel, kinds_of(pieces), width),
        in_specs=[in_smem, in_hbm, in_hbm, in_vmem] + [in_hbm] * len(pieces),
        out_specs=in_vmem,
        out_shape=jax.ShapeDtypeStruct((slab, channels), f32),
        scratch_shapes=[
            pltpu.VMEM((slab + edge, features), bf16),
            pltpu.VMEM((features, channels), bf16),
            pltpu.VMEM((slab + edge, channels), f32),
            pltpu.SemaphoreType.DMA((3, len(pieces))),
        ],
        compiler_params=pltpu.CompilerParams(vmem_limit_bytes=32 << 20),
        name="query",
    )(offsets(pieces), hold(x), hold(before), short_filter, *[hold(p[0]) for p in pieces])


def transform(fwd_ref, block):
    return jnp.dot(fwd_ref[...], jnp.concatenate([block, block], axis=0), preferred_element_type=f32)


def respond_kernel(filter_ref, decay_ref, fwd_ref, out_ref):
    taps = filter_ref.shape[0]
    lag = lax.broadcasted_iota(jnp.int32, (taps, 1), 0)
    faded = filter_ref[...] * jnp.exp(-decay_ref[...] * lag.astype(f32))
    response = transform(fwd_ref, faded.astype(bf16))
    h_cos, h_sin = response[:taps], response[taps:]
    out_ref[0] = h_cos
    out_ref[1] = jnp.where(lag == 0, 0.0, h_sin)
    out_ref[2] = jnp.where(lag == 0, h_sin, h_cos)


def respond(medium_filter, decay, forward, width):
    taps, channels = medium_filter.shape
    return pl.pallas_call(
        respond_kernel,
        grid=(channels // width,),
        in_specs=[
            pl.BlockSpec((taps, width), lambda i: (0, i)),
            pl.BlockSpec((1, width), lambda i: (0, i)),
            pl.BlockSpec(forward.shape, lambda i: (0, 0)),
        ],
        out_specs=pl.BlockSpec((3, taps, width), lambda i: (0, 0, i)),
        out_shape=pltpu.MemorySpace.HBM((3, taps, channels), f32),
        compiler_params=pltpu.CompilerParams(vmem_limit_bytes=8 << 20),
        name="respond",
    )(medium_filter, decay.reshape(1, channels), forward)


def mix_kernel(
    gated_ref, halo_ref, head_ref, short_ref, response_ref, query_ref, fwd_ref, inv_ref, out_ref, s
):
    taps = response_ref.shape[1]
    blocks = gated_ref.shape[0] // taps
    feats = []
    for k in range(2):
        s[0:edge] = halo_ref[taps + k * edge : taps + (k + 1) * edge].astype(f32)
        s[edge : 2 * edge] = head_ref[k].astype(f32)
        total = None
        for lag in range(short_ref.shape[0]):
            term = short_ref[lag, k + 1][None] * s[edge - lag : 2 * edge - lag]
            total = term if total is None else total + term
        feats.append(total)
    first = (feats[0] * feats[1]).astype(bf16)

    row = lax.broadcasted_iota(jnp.int32, (2 * taps, 1), 0)
    sign = jnp.where(row % 2 == 0, 1.0, -1.0).astype(f32)
    h_cos, h_sin, h_low = response_ref[0], response_ref[1], response_ref[2]
    last = transform(fwd_ref, halo_ref[0:taps])
    for b in range(blocks):
        if b == 0:
            block = jnp.concatenate([first, gated_ref[edge:taps]], axis=0)
        else:
            block = gated_ref[b * taps : (b + 1) * taps]
        now = transform(fwd_ref, block)
        x = last + sign * now
        last = now
        x_cos, x_sin = x[:taps], x[taps:]
        y = jnp.concatenate([x_cos * h_cos - x_sin * h_sin, x_sin * h_low + x_cos * h_sin], axis=0)
        high = y.astype(bf16)
        low = (y - high.astype(f32)).astype(bf16)
        mixed = jnp.dot(
            inv_ref[...], jnp.concatenate([high, low, high], axis=0), preferred_element_type=f32
        )
        at = slice(b * taps, (b + 1) * taps)
        out_ref[at] = (query_ref[at] * mixed).astype(bf16)


def mix(gated, halo, head, short_filter, response, query_rows, tables, width):
    slab, channels = gated.shape
    count = response.shape[1]
    forward, inverse = tables
    col = lambda rows: pl.BlockSpec((rows, width), lambda i: (0, i))
    cube = lambda a, b: pl.BlockSpec((a, b, width), lambda i: (0, 0, i))
    return pl.pallas_call(
        mix_kernel,
        grid=(channels // width,),
        in_specs=[
            col(slab),
            col(count + 2 * edge),
            cube(2, edge),
            cube(*short_filter.shape[:2]),
            cube(3, count),
            col(slab),
            pl.BlockSpec(forward.shape, lambda i: (0, 0)),
            pl.BlockSpec(inverse.shape, lambda i: (0, 0)),
        ],
        out_specs=col(slab),
        out_shape=jax.ShapeDtypeStruct((slab, channels), bf16),
        scratch_shapes=[pltpu.VMEM((2 * edge, width), f32)],
        compiler_params=pltpu.CompilerParams(vmem_limit_bytes=16 << 20),
        name="mix",
    )(hold(gated), hold(halo), hold(head), short_filter, hold(response), query_rows, forward, inverse)


def local(tokens, norm_gain, w_in, short_filter, medium_filter, decay, w_out):
    groups, contexts, count = (lax.axis_size(a) for a in axes)
    g, c, z = (lax.axis_index(a) for a in axes)
    length, features = tokens.shape
    rows, branches, channels = w_in.shape
    slab = length * count
    width = min(channels, 256)
    paired = contexts == 4 and groups == 2

    def move(value, target):
        pairs = []
        for i in range(groups):
            for j in range(contexts):
                for k in range(count):
                    to = target(i, j, k)
                    if 0 <= to[1] < contexts and 0 <= to[2] < count:
                        pairs.append(
                            ((i * contexts + j) * count + k, (to[0] * contexts + to[1]) * count + to[2])
                        )
        return lax.ppermute(value, axes, pairs)

    to_chip = lambda v: move(v, lambda i, j, k: (i, j ^ 2, k))
    to_core = lambda v: move(v, lambda i, j, k: (i, j ^ 1, k))
    to_group = lambda v: move(v, lambda i, j, k: (1 - i, j, k))
    to_next = lambda v: move(v, lambda i, j, k: (i, j + 1, k))
    send = lambda v, pairs: move(v, lambda i, j, k: (i, j, pairs.get(k, -1)))
    to_up = lambda v: move(v, lambda i, j, k: (i, j, k + 1))
    to_down = lambda v: move(v, lambda i, j, k: (i, j, k - 1))

    def after(value, *earlier):
        return lax.optimization_barrier((value, *earlier))[0]

    medium_count = medium_filter.shape[0]
    tables = fourier_tables(medium_count)
    weights = jnp.transpose(w_in, (1, 0, 2))
    half = rows // 2
    out_rows = w_out.shape[0]
    if paired:
        first_half, other_half = g * half, (1 - g) * half
        peer = to_core(weights)
        near, far, pieces = {}, {}, {}
        def cut(source, b, first, depth):
            part = lax.dynamic_slice(source, (b, first, 0), (1, depth, channels))
            return part.reshape(depth, channels)

        mine = cut(weights, 1, first_half, half)
        normed = norm(after(tokens, mine), norm_gain)
        response = respond(medium_filter, decay, tables[0], width)
        near[1] = to_chip(mine)
        far[1] = to_group(near[1])
        source = after(weights, normed)
        near[2] = to_chip(after(cut(source, 2, first_half, half), near[1]))
        far[2] = to_group(after(near[2], far[1], response, peer))
        near[0] = to_chip(after(cut(source, 0, first_half, half), near[2]))
        far[0] = to_group(after(near[0], far[2]))
        for b in (1, 2, 0):
            pieces[b] = [
                (weights, b, c * rows),
                (peer, b, (c ^ 1) * rows),
                (near[b], None, (c ^ 2) * rows + first_half),
                (to_core(near[b]), None, (c ^ 3) * rows + first_half),
                (far[b], None, (c ^ 2) * rows + other_half),
            ]
            if b != 0:
                late = after(far[2], near[0]) if b == 2 else far[1]
                pieces[b].append((to_core(late), None, (c ^ 3) * rows + other_half))
    else:
        normed = norm(tokens, norm_gain)
        response = respond(medium_filter, decay, tables[0], width)
        full = lax.all_gather(weights, "context", axis=1, tiled=True)
        pieces = {b: [(full, b, 0)] for b in range(branches)}

    gathered = lax.all_gather(normed, "tensor", axis=0, tiled=True)
    gate_taps = after(short_filter, response)
    gated, head, edges = gate(gathered, pieces[1], pieces[2], gate_taps, medium_count, width)
    before_rows = to_next(after(gathered[slab - edge :], gated))
    halo = to_next(after(edges, before_rows))
    if paired:
        last = to_core(after(far[0], before_rows))
        pieces[0].append((last, None, (c ^ 3) * rows + other_half))
    query_rows = query(gathered, before_rows, pieces[0], short_filter, width)
    combined = mix(gated, halo, head, short_filter, response, query_rows, tables, width)
    if paired:
        out_full = lax.all_gather(after(w_out, near[1]), "context", axis=0, tiled=True)
        out_peer = to_core(after(w_out, gated))
        part = lambda i: lax.dynamic_slice(out_full, ((c ^ i) * out_rows, 0), (out_rows, channels))
        sets = [w_out, out_peer, part(2), part(3)]
    else:
        sets = [lax.all_gather(w_out, "context", axis=0, tiled=True)]

    def plus(*terms):
        total = terms[0].astype(f32)
        for term in terms[1:]:
            total = total + term.astype(f32)
        return total.astype(bf16)

    def product(rows_out):
        return lax.dot_general(
            combined, rows_out, (((1,), (1,)), ((), ())), preferred_element_type=f32
        ).astype(bf16)

    results, firsts = [], []
    for rows_out in sets:
        partial = product(rows_out)
        combined = after(combined, partial)

        def block(index, blocks=1, partial=partial):
            index = jnp.clip(index, 0, count - blocks)
            return lax.dynamic_slice(
                partial, (index * length, 0), (blocks * length, partial.shape[1])
            )

        if count == 4:
            far_pair = block(jnp.where(z < 2, 2, 0), 2)
            firsts.append(send(far_pair, {0: 1, 3: 2}))
            got = plus(far_pair, firsts[-1])
            got = send(got, {1: 2, 2: 1})
            low, high = got[:length], got[length:]
            odd = z % 2 == 1
            got_own = jnp.where(odd, high, low)
            got_other = jnp.where(odd, low, high)
            last = send(plus(block(z ^ 1), got_other), {0: 1, 1: 0, 2: 3, 3: 2})
            results.append(plus(block(z), got_own, last))
        else:
            up = down = None
            for s in range(1, count):
                rising = block(count + z - s)
                falling = block(z - count + s)
                if up is not None:
                    rising, falling = plus(rising, up), plus(falling, down)
                up, down = to_up(rising), to_down(falling)
            results.append(plus(block(z), up, down))
    if not paired:
        return results[0]
    swap = lambda test, a, b: (jnp.where(test, b, a), jnp.where(test, a, b))
    e0, e1, e2, e3 = results
    odd = c % 2 == 1
    low = jnp.concatenate(swap(odd, e0, e1), 1)
    high = jnp.concatenate(swap(odd, e2, e3), 1)
    return jnp.concatenate(swap(c >= 2, low, high), 1)


def solution(mesh):
    in_specs = (
        P(axes, None),
        P(),
        P("context", None, "tensor"),
        P(None, None, "tensor"),
        P(None, "tensor"),
        P("tensor"),
        P("context", "tensor"),
    )
    return jax.shard_map(
        local, mesh=mesh, in_specs=in_specs, out_specs=P(axes, None), check_vma=False
    )
```

```python
import functools
import jax
import jax.numpy as jnp
import ml_dtypes
import numpy as np
from jax import lax
from jax.experimental import pallas as pl
from jax.experimental.pallas import tpu as pltpu
from jax.sharding import PartitionSpec as P

norm_epsilon = 1e-06
axes = ("groups", "context", "tensor")
edge = 16
f32 = jnp.float32
bf16 = jnp.bfloat16


def split_parts(matrix):
    high = matrix.astype(ml_dtypes.bfloat16)
    low = (matrix - high.astype(np.float64)).astype(ml_dtypes.bfloat16)
    return high, low


def fourier_tables(taps):
    size = 2 * taps
    freq = np.arange(taps)[:, None]
    time = np.arange(size)[None, :]
    angle = 2 * np.pi * ((freq * time) % size) / size
    cosine, sine = np.cos(angle), np.sin(angle)
    sine[0] = 1.0 - 2.0 * (np.arange(size) % 2)
    forward = np.concatenate([cosine, sine], axis=0)
    weight = np.full((2 * taps, 1), 2.0 / size)
    weight[0] = weight[taps] = 1.0 / size
    inverse = (forward * weight)[:, taps:].T
    fh, fl = split_parts(forward[:, :taps])
    ih, il = split_parts(inverse)
    return np.concatenate([fh, fl], axis=1), np.concatenate([ih, ih, il], axis=1)


def short_sum(s, taps_ref, branch, slab):
    total = None
    for lag in range(taps_ref.shape[0]):
        term = taps_ref[lag, branch][None] * s[edge - lag : edge - lag + slab]
        total = term if total is None else total + term
    return total


def norm_kernel(x_ref, gain_ref, out_ref):
    values = x_ref[...].astype(f32)
    mean = jnp.mean(values * values, axis=1, keepdims=True)
    scaled = values * lax.rsqrt(mean + norm_epsilon)
    out_ref[...] = (scaled * gain_ref[...].astype(f32)).astype(bf16)


def norm(tokens, gain):
    length, features = tokens.shape
    rows = min(length, 32)
    return pl.pallas_call(
        norm_kernel,
        grid=(length // rows,),
        in_specs=[
            pl.BlockSpec((rows, features), lambda i: (i, 0)),
            pl.BlockSpec((1, features), lambda i: (0, 0)),
        ],
        out_specs=pl.BlockSpec((rows, features), lambda i: (i, 0)),
        out_shape=jax.ShapeDtypeStruct((length, features), bf16),
        compiler_params=pltpu.CompilerParams(vmem_limit_bytes=8 << 20),
        name="norm",
    )(tokens, gain.reshape(1, features))


in_hbm = pl.BlockSpec(memory_space=pltpu.MemorySpace.HBM)
in_vmem = pl.BlockSpec(memory_space=pltpu.MemorySpace.VMEM)
in_smem = pl.BlockSpec(memory_space=pltpu.MemorySpace.SMEM)


def hold(array):
    return pltpu.with_memory_space_constraint(array, pltpu.MemorySpace.HBM)


def kinds_of(pieces):
    return tuple((branch, array.shape[-2]) for array, branch, _ in pieces)


def offsets(pieces):
    return jnp.stack([jnp.asarray(p[2], jnp.int32) for p in pieces])


def spans(kinds):
    start = 0
    for _, depth in kinds:
        yield start, start + depth
        start += depth


def token_copies(kinds, at_ref, x_ref, target, sems):
    copies = []
    for n, (low, high) in enumerate(spans(kinds)):
        columns = pl.ds(pl.multiple_of(at_ref[n], min(high - low, 256)), high - low)
        copies.append(
            pltpu.make_async_copy(x_ref.at[:, columns], target.at[:, low:high], sems.at[n])
        )
    return copies


def weight_copies(kinds, arrays, target, sems):
    copies = []
    for n, (low, high) in enumerate(spans(kinds)):
        branch = kinds[n][0]
        source = arrays[n] if branch is None else arrays[n].at[branch]
        copies.append(pltpu.make_async_copy(source, target.at[low:high], sems.at[n]))
    return copies


def add_up(kinds, width, waits, full, weight, s, first):
    rows = slice(first, None)
    channels = weight.shape[1]
    for n, (low, high) in enumerate(spans(kinds)):
        for copies in waits:
            copies[n].wait()
        for i in range(channels // width):
            columns = slice(i * width, (i + 1) * width)
            term = jnp.dot(
                full[:, low:high], weight[low:high, columns], preferred_element_type=f32
            )
            if n > 0:
                term = s[rows, columns] + term
            if n == len(kinds) - 1 and first is not None:
                term = term.astype(bf16).astype(f32)
            s[rows, columns] = term


def gate_kernel(one, two, width, at_ref, x_ref, taps_ref, *rest):
    arrays = rest[: len(one) + len(two)]
    gated_ref, head_ref, halo_ref, full, weights, s1, feat, s2, sems = rest[len(arrays) :]
    slab, channels = gated_ref.shape
    count = halo_ref.shape[0] - 2 * edge
    x_copies = token_copies(one, at_ref, x_ref, full, sems.at[0])
    copies = [
        weight_copies(one, arrays[: len(one)], weights.at[0], sems.at[1]),
        weight_copies(two, arrays[len(one) :], weights.at[1], sems.at[2]),
    ]
    for x_copy, copy in zip(x_copies, copies[0]):
        x_copy.start()
        copy.start()
    for copy in copies[1]:
        copy.start()
    s1[0:edge] = jnp.zeros((edge, channels), f32)
    add_up(one, width, (x_copies, copies[0]), full, weights.at[0], s1, edge)
    head_ref[0] = s1[edge : 2 * edge].astype(bf16)
    halo_ref[count : count + edge] = s1[slab : slab + edge].astype(bf16)
    feat[...] = short_sum(s1, taps_ref, 1, slab)
    for copy in copies[1]:
        copy.wait()
    s2[0:edge] = jnp.zeros((edge, width), f32)
    for i in range(channels // width):
        columns = slice(i * width, (i + 1) * width)
        term = jnp.dot(full[...], weights[1, :, columns], preferred_element_type=f32)
        s2[edge : edge + slab] = term.astype(bf16).astype(f32)
        head_ref[1, :, columns] = s2[edge : 2 * edge].astype(bf16)
        halo_ref[count + edge :, columns] = s2[slab : slab + edge].astype(bf16)
        gated = feat[:, columns] * short_sum(s2, taps_ref[:, :, columns], 2, slab)
        gated = gated.astype(bf16)
        gated_ref[:, columns] = gated
        halo_ref[0:count, columns] = gated[slab - count :]


def gate(x, one, two, short_filter, taps, width):
    slab, features = x.shape
    channels = short_filter.shape[-1]
    return pl.pallas_call(
        functools.partial(gate_kernel, kinds_of(one), kinds_of(two), width),
        in_specs=[in_smem, in_hbm, in_vmem] + [in_hbm] * (len(one) + len(two)),
        out_specs=[in_vmem] * 3,
        out_shape=[
            pltpu.MemorySpace.HBM((slab, channels), bf16),
            pltpu.MemorySpace.HBM((2, edge, channels), bf16),
            pltpu.MemorySpace.HBM((taps + 2 * edge, channels), bf16),
        ],
        scratch_shapes=[
            pltpu.VMEM((slab, features), bf16),
            pltpu.VMEM((2, features, channels), bf16),
            pltpu.VMEM((slab + edge, channels), f32),
            pltpu.VMEM((slab, channels), f32),
            pltpu.VMEM((slab + edge, width), f32),
            pltpu.SemaphoreType.DMA((3, len(one))),
        ],
        compiler_params=pltpu.CompilerParams(vmem_limit_bytes=40 << 20),
        cost_estimate=pl.CostEstimate(
            flops=4 * slab * features * channels,
            transcendentals=0,
            bytes_accessed=2 * features * (slab + 2 * channels),
        ),
        name="gate",
    )(offsets(one), hold(x), short_filter, *[hold(p[0]) for p in one + two])


def query_start_kernel(kinds, width, at_ref, x_ref, before_ref, *rest):
    arrays = rest[: len(kinds)]
    sum_ref, full, weight, sems = rest[len(arrays) :]
    slab = x_ref.shape[0]
    x_copies = token_copies(kinds, at_ref, x_ref, full.at[edge : edge + slab], sems.at[0])
    e_copies = token_copies(kinds, at_ref, before_ref, full.at[0:edge], sems.at[1])
    copies = weight_copies(kinds, arrays, weight, sems.at[2])
    for group in zip(e_copies, x_copies, copies):
        for copy in group:
            copy.start()
    add_up(kinds, width, (e_copies, x_copies, copies), full, weight, sum_ref, None)


def query_end_kernel(kinds, width, at_ref, x_ref, before_ref, sum_ref, taps_ref, *rest):
    arrays = rest[: len(kinds)]
    out_ref, full, weight, s, sems = rest[len(arrays) :]
    slab, channels = out_ref.shape
    x_copies = token_copies(kinds, at_ref, x_ref, full.at[edge : edge + slab], sems.at[0])
    e_copies = token_copies(kinds, at_ref, before_ref, full.at[0:edge], sems.at[1])
    copies = weight_copies(kinds, arrays, weight, sems.at[2])
    for group in zip(e_copies, x_copies, copies):
        for copy in group:
            copy.start()
    for group in zip(e_copies, x_copies, copies):
        for copy in group:
            copy.wait()
    for i in range(channels // width):
        columns = slice(i * width, (i + 1) * width)
        term = jnp.dot(full[...], weight[:, columns], preferred_element_type=f32)
        s[...] = (sum_ref[:, columns] + term).astype(bf16).astype(f32)
        out_ref[:, columns] = short_sum(s, taps_ref[:, :, columns], 0, slab)


def query_start(x, before, pieces, width):
    slab, features = x.shape
    channels = pieces[0][0].shape[-1]
    kinds = kinds_of(pieces)
    depth = sum(k[1] for k in kinds)
    return pl.pallas_call(
        functools.partial(query_start_kernel, kinds, width),
        in_specs=[in_smem, in_hbm, in_hbm] + [in_hbm] * len(pieces),
        out_specs=in_vmem,
        out_shape=jax.ShapeDtypeStruct((slab + edge, channels), f32),
        scratch_shapes=[
            pltpu.VMEM((slab + edge, depth), bf16),
            pltpu.VMEM((depth, channels), bf16),
            pltpu.SemaphoreType.DMA((3, len(pieces))),
        ],
        compiler_params=pltpu.CompilerParams(vmem_limit_bytes=24 << 20),
        cost_estimate=pl.CostEstimate(
            flops=2 * slab * depth * channels,
            transcendentals=0,
            bytes_accessed=2 * depth * (slab + channels),
        ),
        name="query_start",
    )(offsets(pieces), hold(x), hold(before), *[hold(p[0]) for p in pieces])


def query_end(x, before, pieces, total, short_filter, width):
    slab, features = x.shape
    channels = short_filter.shape[-1]
    kinds = kinds_of(pieces)
    depth = sum(k[1] for k in kinds)
    return pl.pallas_call(
        functools.partial(query_end_kernel, kinds, width),
        in_specs=[in_smem, in_hbm, in_hbm, in_vmem, in_vmem] + [in_hbm] * len(pieces),
        out_specs=in_vmem,
        out_shape=jax.ShapeDtypeStruct((slab, channels), f32),
        scratch_shapes=[
            pltpu.VMEM((slab + edge, depth), bf16),
            pltpu.VMEM((depth, channels), bf16),
            pltpu.VMEM((slab + edge, width), f32),
            pltpu.SemaphoreType.DMA((3, len(pieces))),
        ],
        compiler_params=pltpu.CompilerParams(vmem_limit_bytes=24 << 20),
        cost_estimate=pl.CostEstimate(
            flops=2 * slab * depth * channels,
            transcendentals=0,
            bytes_accessed=2 * depth * (slab + channels),
        ),
        name="query_end",
    )(offsets(pieces), hold(x), hold(before), total, short_filter, *[hold(p[0]) for p in pieces])


def transform(fwd_ref, block):
    return jnp.dot(fwd_ref[...], jnp.concatenate([block, block], axis=0), preferred_element_type=f32)


def respond_kernel(filter_ref, decay_ref, fwd_ref, out_ref):
    taps = filter_ref.shape[0]
    lag = lax.broadcasted_iota(jnp.int32, (taps, 1), 0)
    faded = filter_ref[...] * jnp.exp(-decay_ref[...] * lag.astype(f32))
    response = transform(fwd_ref, faded.astype(bf16))
    h_cos, h_sin = response[:taps], response[taps:]
    out_ref[0] = h_cos
    out_ref[1] = jnp.where(lag == 0, 0.0, h_sin)
    out_ref[2] = jnp.where(lag == 0, h_sin, h_cos)


def respond(medium_filter, decay, forward, width):
    taps, channels = medium_filter.shape
    return pl.pallas_call(
        respond_kernel,
        grid=(channels // width,),
        in_specs=[
            pl.BlockSpec((taps, width), lambda i: (0, i)),
            pl.BlockSpec((1, width), lambda i: (0, i)),
            pl.BlockSpec(forward.shape, lambda i: (0, 0)),
        ],
        out_specs=pl.BlockSpec((3, taps, width), lambda i: (0, 0, i)),
        out_shape=pltpu.MemorySpace.HBM((3, taps, channels), f32),
        compiler_params=pltpu.CompilerParams(vmem_limit_bytes=8 << 20),
        name="respond",
    )(medium_filter, decay.reshape(1, channels), forward)


def mix_kernel(
    gated_ref, halo_ref, head_ref, short_ref, response_ref, query_ref, fwd_ref, inv_ref, out_ref, s
):
    taps = response_ref.shape[1]
    blocks = gated_ref.shape[0] // taps
    feats = []
    for k in range(2):
        s[0:edge] = halo_ref[taps + k * edge : taps + (k + 1) * edge].astype(f32)
        s[edge : 2 * edge] = head_ref[k].astype(f32)
        total = None
        for lag in range(short_ref.shape[0]):
            term = short_ref[lag, k + 1][None] * s[edge - lag : 2 * edge - lag]
            total = term if total is None else total + term
        feats.append(total)
    first = (feats[0] * feats[1]).astype(bf16)

    row = lax.broadcasted_iota(jnp.int32, (2 * taps, 1), 0)
    sign = jnp.where(row % 2 == 0, 1.0, -1.0).astype(f32)
    h_cos, h_sin, h_low = response_ref[0], response_ref[1], response_ref[2]
    last = transform(fwd_ref, halo_ref[0:taps])
    for b in range(blocks):
        if b == 0:
            block = jnp.concatenate([first, gated_ref[edge:taps]], axis=0)
        else:
            block = gated_ref[b * taps : (b + 1) * taps]
        now = transform(fwd_ref, block)
        x = last + sign * now
        last = now
        x_cos, x_sin = x[:taps], x[taps:]
        y = jnp.concatenate([x_cos * h_cos - x_sin * h_sin, x_sin * h_low + x_cos * h_sin], axis=0)
        high = y.astype(bf16)
        low = (y - high.astype(f32)).astype(bf16)
        mixed = jnp.dot(
            inv_ref[...], jnp.concatenate([high, low, high], axis=0), preferred_element_type=f32
        )
        at = slice(b * taps, (b + 1) * taps)
        out_ref[at] = (query_ref[at] * mixed).astype(bf16)


def mix(gated, halo, head, short_filter, response, query_rows, tables, width):
    slab, channels = gated.shape
    count = response.shape[1]
    forward, inverse = tables
    col = lambda rows: pl.BlockSpec((rows, width), lambda i: (0, i))
    cube = lambda a, b: pl.BlockSpec((a, b, width), lambda i: (0, 0, i))
    return pl.pallas_call(
        mix_kernel,
        grid=(channels // width,),
        in_specs=[
            col(slab),
            col(count + 2 * edge),
            cube(2, edge),
            cube(*short_filter.shape[:2]),
            cube(3, count),
            col(slab),
            pl.BlockSpec(forward.shape, lambda i: (0, 0)),
            pl.BlockSpec(inverse.shape, lambda i: (0, 0)),
        ],
        out_specs=col(slab),
        out_shape=jax.ShapeDtypeStruct((slab, channels), bf16),
        scratch_shapes=[pltpu.VMEM((2 * edge, width), f32)],
        compiler_params=pltpu.CompilerParams(vmem_limit_bytes=16 << 20),
        name="mix",
    )(hold(gated), hold(halo), hold(head), short_filter, hold(response), query_rows, forward, inverse)


def local(tokens, norm_gain, w_in, short_filter, medium_filter, decay, w_out):
    groups, contexts, count = (lax.axis_size(a) for a in axes)
    g, c, z = (lax.axis_index(a) for a in axes)
    length, features = tokens.shape
    rows, branches, channels = w_in.shape
    slab = length * count
    width = min(channels, 256)
    paired = contexts == 4 and groups == 2

    def move(value, target):
        pairs = []
        for i in range(groups):
            for j in range(contexts):
                for k in range(count):
                    to = target(i, j, k)
                    if 0 <= to[1] < contexts and 0 <= to[2] < count:
                        pairs.append(
                            ((i * contexts + j) * count + k, (to[0] * contexts + to[1]) * count + to[2])
                        )
        return lax.ppermute(value, axes, pairs)

    to_chip = lambda v: move(v, lambda i, j, k: (i, j ^ 2, k))
    to_core = lambda v: move(v, lambda i, j, k: (i, j ^ 1, k))
    to_group = lambda v: move(v, lambda i, j, k: (1 - i, j, k))
    to_next = lambda v: move(v, lambda i, j, k: (i, j + 1, k))
    send = lambda v, pairs: move(v, lambda i, j, k: (i, j, pairs.get(k, -1)))
    to_up = lambda v: move(v, lambda i, j, k: (i, j, k + 1))
    to_down = lambda v: move(v, lambda i, j, k: (i, j, k - 1))

    def after(value, *earlier):
        return lax.optimization_barrier((value, *earlier))[0]

    def hop(value, held):
        first, last = max(0, count - 2 * held), count - held
        return value + move(
            value,
            lambda i, j, k: (i, j, k - held) if k - held >= first and k >= last else (i, j, -1),
        )

    def from_last_slab(value):
        return move(value, lambda i, j, k: (i, j + 1, k) if k == count - 1 else (i, -1, k))

    medium_count = medium_filter.shape[0]
    tables = fourier_tables(medium_count)
    weights = jnp.transpose(w_in, (1, 0, 2))
    half = rows // 2
    out_rows = w_out.shape[0]
    if paired:
        first_half, other_half = g * half, (1 - g) * half
        peer = to_core(weights)
        near, far, pieces = {}, {}, {}
        def cut(source, b, first, depth):
            part = lax.dynamic_slice(source, (b, first, 0), (1, depth, channels))
            return part.reshape(depth, channels)

        mine = cut(weights, 1, first_half, half)
        normed = norm(after(tokens, mine), norm_gain)
        response = respond(medium_filter, decay, tables[0], width)
        near[1] = to_chip(mine)
        far[1] = to_group(near[1])
        source = after(weights, normed)
        near[2] = to_chip(after(cut(source, 2, first_half, half), near[1]))
        before_rows = hop(after(from_last_slab(normed[length - edge :]), near[1]), 1)
        far[2] = to_group(after(near[2], far[1], response, peer, before_rows))
        before_rows = hop(after(before_rows, near[2]), 2)
        near[0] = to_chip(after(cut(source, 0, first_half, half), near[2]))
        far[0] = to_group(after(near[0], far[2]))
        for b in (1, 2, 0):
            pieces[b] = [
                (weights, b, c * rows),
                (peer, b, (c ^ 1) * rows),
                (near[b], None, (c ^ 2) * rows + first_half),
                (to_core(near[b]), None, (c ^ 3) * rows + first_half),
                (far[b], None, (c ^ 2) * rows + other_half),
            ]
            if b != 0:
                late = after(far[2], near[0], before_rows) if b == 2 else far[1]
                pieces[b].append((to_core(late), None, (c ^ 3) * rows + other_half))
    else:
        normed = norm(tokens, norm_gain)
        response = respond(medium_filter, decay, tables[0], width)
        full = lax.all_gather(weights, "context", axis=1, tiled=True)
        pieces = {b: [(full, b, 0)] for b in (1, 2)}
        middle = features // 2
        pieces[0] = [(full[0, :middle], None, 0), (full[0, middle:], None, middle)]
        before_rows = from_last_slab(normed[length - edge :])
        held = 1
        while held < count:
            before_rows = hop(before_rows, held)
            held *= 2

    gathered = lax.all_gather(normed, "tensor", axis=0, tiled=True)
    gate_taps = after(short_filter, response)
    gated, head, edges = gate(gathered, pieces[1], pieces[2], gate_taps, medium_count, width)
    halo = to_next(edges)
    early = len(pieces[0]) - 1
    before_rows = after(before_rows, gated)
    total = query_start(gathered, before_rows, pieces[0][:early], width)
    if paired:
        last = to_core(after(far[0], gated))
        pieces[0].append((last, None, (c ^ 3) * rows + other_half))
    query_rows = query_end(gathered, before_rows, pieces[0][early:], total, short_filter, width)
    combined = mix(gated, halo, head, short_filter, response, query_rows, tables, width)
    if paired:
        out_full = lax.all_gather(after(w_out, near[1]), "context", axis=0, tiled=True)
        out_peer = to_core(after(w_out, total))
        part = lambda i: lax.dynamic_slice(out_full, ((c ^ i) * out_rows, 0), (out_rows, channels))
        sets = [w_out, out_peer, part(2), part(3)]
    else:
        sets = [lax.all_gather(w_out, "context", axis=0, tiled=True)]

    def plus(*terms):
        total = terms[0].astype(f32)
        for term in terms[1:]:
            total = total + term.astype(f32)
        return total.astype(bf16)

    def product(rows_out):
        return lax.dot_general(
            combined, rows_out, (((1,), (1,)), ((), ())), preferred_element_type=f32
        ).astype(bf16)

    results, firsts, seconds = [], [], []
    for n, rows_out in enumerate(sets):
        if paired and n == 2:
            combined = after(combined, firsts[1])
        if paired and n == 3:
            combined = after(combined, seconds[0])
        partial = product(rows_out)
        combined = after(combined, partial)

        def block(index, blocks=1, partial=partial):
            index = jnp.clip(index, 0, count - blocks)
            return lax.dynamic_slice(
                partial, (index * length, 0), (blocks * length, partial.shape[1])
            )

        if count == 4:
            far_pair = block(jnp.where(z < 2, 2, 0), 2)
            firsts.append(send(far_pair, {0: 1, 3: 2}))
            got = plus(far_pair, firsts[-1])
            got = send(got, {1: 2, 2: 1})
            seconds.append(got)
            low, high = got[:length], got[length:]
            odd = z % 2 == 1
            got_own = jnp.where(odd, high, low)
            got_other = jnp.where(odd, low, high)
            last = send(plus(block(z ^ 1), got_other), {0: 1, 1: 0, 2: 3, 3: 2})
            results.append(plus(block(z), got_own, last))
        else:
            up = down = None
            for s in range(1, count):
                rising = block(count + z - s)
                falling = block(z - count + s)
                if up is not None:
                    rising, falling = plus(rising, up), plus(falling, down)
                up, down = to_up(rising), to_down(falling)
            results.append(plus(block(z), up, down))
    if not paired:
        return results[0]
    swap = lambda test, a, b: (jnp.where(test, b, a), jnp.where(test, a, b))
    e0, e1, e2, e3 = results
    odd = c % 2 == 1
    low = jnp.concatenate(swap(odd, e0, e1), 1)
    high = jnp.concatenate(swap(odd, e2, e3), 1)
    return jnp.concatenate(swap(c >= 2, low, high), 1)


def solution(mesh):
    in_specs = (
        P(axes, None),
        P(),
        P("context", None, "tensor"),
        P(None, None, "tensor"),
        P(None, "tensor"),
        P("tensor"),
        P("context", "tensor"),
    )
    return jax.shard_map(
        local, mesh=mesh, in_specs=in_specs, out_specs=P(axes, None), check_vma=False
    )
```

```python
import functools
import jax
import jax.numpy as jnp
import ml_dtypes
import numpy as np
from jax import lax
from jax.experimental import pallas as pl
from jax.experimental.pallas import tpu as pltpu
from jax.sharding import PartitionSpec as P

norm_epsilon = 1e-06
axes = ("groups", "context", "tensor")
edge = 16
f32 = jnp.float32
bf16 = jnp.bfloat16


def split_parts(matrix):
    high = matrix.astype(ml_dtypes.bfloat16)
    low = (matrix - high.astype(np.float64)).astype(ml_dtypes.bfloat16)
    return high, low


def fourier_tables(taps):
    size = 2 * taps
    freq = np.arange(taps)[:, None]
    time = np.arange(size)[None, :]
    angle = 2 * np.pi * ((freq * time) % size) / size
    cosine, sine = np.cos(angle), np.sin(angle)
    sine[0] = 1.0 - 2.0 * (np.arange(size) % 2)
    forward = np.concatenate([cosine, sine], axis=0)
    weight = np.full((2 * taps, 1), 2.0 / size)
    weight[0] = weight[taps] = 1.0 / size
    inverse = (forward * weight)[:, taps:].T
    fh, fl = split_parts(forward[:, :taps])
    ih, il = split_parts(inverse)
    return np.concatenate([fh, fl], axis=1), np.concatenate([ih, ih, il], axis=1)


def short_sum(s, taps_ref, branch, slab):
    total = None
    for lag in range(taps_ref.shape[0]):
        term = taps_ref[lag, branch][None] * s[edge - lag : edge - lag + slab]
        total = term if total is None else total + term
    return total


def norm_kernel(x_ref, gain_ref, out_ref):
    values = x_ref[...].astype(f32)
    mean = jnp.mean(values * values, axis=1, keepdims=True)
    scaled = values * lax.rsqrt(mean + norm_epsilon)
    out_ref[...] = (scaled * gain_ref[...].astype(f32)).astype(bf16)


def norm(tokens, gain):
    length, features = tokens.shape
    rows = min(length, 32)
    return pl.pallas_call(
        norm_kernel,
        grid=(length // rows,),
        in_specs=[
            pl.BlockSpec((rows, features), lambda i: (i, 0)),
            pl.BlockSpec((1, features), lambda i: (0, 0)),
        ],
        out_specs=pl.BlockSpec((rows, features), lambda i: (i, 0)),
        out_shape=jax.ShapeDtypeStruct((length, features), bf16),
        compiler_params=pltpu.CompilerParams(vmem_limit_bytes=8 << 20),
        name="norm",
    )(tokens, gain.reshape(1, features))


in_hbm = pl.BlockSpec(memory_space=pltpu.MemorySpace.HBM)
in_vmem = pl.BlockSpec(memory_space=pltpu.MemorySpace.VMEM)
in_smem = pl.BlockSpec(memory_space=pltpu.MemorySpace.SMEM)


def hold(array):
    return pltpu.with_memory_space_constraint(array, pltpu.MemorySpace.HBM)


def kinds_of(pieces):
    return tuple((branch, array.shape[-2]) for array, branch, _ in pieces)


def offsets(pieces):
    return jnp.stack([jnp.asarray(p[2], jnp.int32) for p in pieces])


def spans(kinds):
    start = 0
    for _, depth in kinds:
        yield start, start + depth
        start += depth


def token_copies(kinds, at_ref, x_ref, target, sems):
    copies = []
    for n, (low, high) in enumerate(spans(kinds)):
        columns = pl.ds(pl.multiple_of(at_ref[n], min(high - low, 256)), high - low)
        copies.append(
            pltpu.make_async_copy(x_ref.at[:, columns], target.at[:, low:high], sems.at[n])
        )
    return copies


def weight_copies(kinds, arrays, target, sems):
    copies = []
    for n, (low, high) in enumerate(spans(kinds)):
        branch = kinds[n][0]
        source = arrays[n] if branch is None else arrays[n].at[branch]
        copies.append(pltpu.make_async_copy(source, target.at[low:high], sems.at[n]))
    return copies


def add_up(kinds, width, waits, full, weight, s, first):
    rows = slice(first, None)
    channels = weight.shape[1]
    for n, (low, high) in enumerate(spans(kinds)):
        for copies in waits:
            copies[n].wait()
        for i in range(channels // width):
            columns = slice(i * width, (i + 1) * width)
            term = jnp.dot(
                full[:, low:high], weight[low:high, columns], preferred_element_type=f32
            )
            if n > 0:
                term = s[rows, columns] + term
            if n == len(kinds) - 1 and first is not None:
                term = term.astype(bf16).astype(f32)
            s[rows, columns] = term


def gate_kernel(one, two, three, width, at_ref, x_ref, taps_ref, *rest):
    arrays = rest[: len(one) + len(two) + len(three)]
    gated_ref, head_ref, halo_ref, sum_ref, full, weights, s1, feat, s2, sems = rest[len(arrays) :]
    slab, channels = gated_ref.shape
    count = halo_ref.shape[0] - 2 * edge
    x_copies = token_copies(one, at_ref, x_ref, full, sems.at[0])
    copies = [
        weight_copies(one, arrays[: len(one)], weights.at[0], sems.at[1]),
        weight_copies(two, arrays[len(one) : -len(three)], weights.at[1], sems.at[2]),
        weight_copies(three, arrays[-len(three) :], weights.at[2], sems.at[3]),
    ]
    for x_copy, copy in zip(x_copies, copies[0]):
        x_copy.start()
        copy.start()
    for copy in copies[1] + copies[2]:
        copy.start()
    s1[0:edge] = jnp.zeros((edge, channels), f32)
    add_up(one, width, (x_copies, copies[0]), full, weights.at[0], s1, edge)
    head_ref[0] = s1[edge : 2 * edge].astype(bf16)
    halo_ref[count : count + edge] = s1[slab : slab + edge].astype(bf16)
    feat[...] = short_sum(s1, taps_ref, 1, slab)
    for copy in copies[1]:
        copy.wait()
    s2[0:edge] = jnp.zeros((edge, width), f32)
    for i in range(channels // width):
        columns = slice(i * width, (i + 1) * width)
        term = jnp.dot(full[...], weights[1, :, columns], preferred_element_type=f32)
        s2[edge : edge + slab] = term.astype(bf16).astype(f32)
        head_ref[1, :, columns] = s2[edge : 2 * edge].astype(bf16)
        halo_ref[count + edge :, columns] = s2[slab : slab + edge].astype(bf16)
        gated = feat[:, columns] * short_sum(s2, taps_ref[:, :, columns], 2, slab)
        gated = gated.astype(bf16)
        gated_ref[:, columns] = gated
        halo_ref[0:count, columns] = gated[slab - count :]
    for copy in copies[2]:
        copy.wait()
    depth = list(spans(three))[-1][1]
    for i in range(channels // width):
        columns = slice(i * width, (i + 1) * width)
        sum_ref[:, columns] = jnp.dot(
            full[:, 0:depth], weights[2, 0:depth, columns], preferred_element_type=f32
        )


def gate(x, one, two, three, short_filter, taps, width):
    slab, features = x.shape
    channels = short_filter.shape[-1]
    return pl.pallas_call(
        functools.partial(gate_kernel, kinds_of(one), kinds_of(two), kinds_of(three), width),
        in_specs=[in_smem, in_hbm, in_vmem] + [in_hbm] * (len(one) + len(two) + len(three)),
        out_specs=[in_vmem] * 4,
        out_shape=[
            pltpu.MemorySpace.HBM((slab, channels), bf16),
            pltpu.MemorySpace.HBM((2, edge, channels), bf16),
            pltpu.MemorySpace.HBM((taps + 2 * edge, channels), bf16),
            jax.ShapeDtypeStruct((slab, channels), f32),
        ],
        scratch_shapes=[
            pltpu.VMEM((slab, features), bf16),
            pltpu.VMEM((3, features, channels), bf16),
            pltpu.VMEM((slab + edge, channels), f32),
            pltpu.VMEM((slab, channels), f32),
            pltpu.VMEM((slab + edge, width), f32),
            pltpu.SemaphoreType.DMA((4, len(one))),
        ],
        compiler_params=pltpu.CompilerParams(vmem_limit_bytes=48 << 20),
        name="gate",
    )(offsets(one), hold(x), short_filter, *[hold(p[0]) for p in one + two + three])


def query_kernel(kinds, width, at_ref, x_ref, sum_ref, *rest):
    arrays = rest[: len(kinds)]
    out_ref, tail_ref, full, weight, sems = rest[len(arrays) :]
    slab, channels = out_ref.shape
    x_copies = token_copies(kinds, at_ref, x_ref, full, sems.at[0])
    copies = weight_copies(kinds, arrays, weight, sems.at[1])
    for copy in x_copies + copies:
        copy.start()
    for copy in x_copies + copies:
        copy.wait()
    for i in range(channels // width):
        columns = slice(i * width, (i + 1) * width)
        term = jnp.dot(full[...], weight[:, columns], preferred_element_type=f32)
        out_ref[:, columns] = (sum_ref[:, columns] + term).astype(bf16)
    tail_ref[...] = out_ref[slab - edge :]


def query(x, pieces, total, width):
    slab, channels = total.shape
    kinds = kinds_of(pieces)
    depth = sum(k[1] for k in kinds)
    return pl.pallas_call(
        functools.partial(query_kernel, kinds, width),
        in_specs=[in_smem, in_hbm, in_vmem] + [in_hbm] * len(pieces),
        out_specs=[in_vmem] * 2,
        out_shape=[
            jax.ShapeDtypeStruct((slab, channels), bf16),
            pltpu.MemorySpace.HBM((edge, channels), bf16),
        ],
        scratch_shapes=[
            pltpu.VMEM((slab, depth), bf16),
            pltpu.VMEM((depth, channels), bf16),
            pltpu.SemaphoreType.DMA((2, len(pieces))),
        ],
        compiler_params=pltpu.CompilerParams(vmem_limit_bytes=16 << 20),
        name="query",
    )(offsets(pieces), hold(x), total, *[hold(p[0]) for p in pieces])


def combine_kernel(projected_ref, before_ref, taps_ref, mixed_ref, out_ref, s):
    slab = out_ref.shape[0]
    s[0:edge] = before_ref[...].astype(f32)
    s[edge : edge + slab] = projected_ref[...].astype(f32)
    out_ref[...] = (short_sum(s, taps_ref, 0, slab) * mixed_ref[...]).astype(bf16)


def combine(projected, before, short_filter, mixed, width):
    slab, channels = mixed.shape
    col = lambda rows: pl.BlockSpec((rows, width), lambda i: (0, i))
    return pl.pallas_call(
        combine_kernel,
        grid=(channels // width,),
        in_specs=[
            col(slab),
            col(edge),
            pl.BlockSpec(short_filter.shape[:2] + (width,), lambda i: (0, 0, i)),
            col(slab),
        ],
        out_specs=col(slab),
        out_shape=jax.ShapeDtypeStruct((slab, channels), bf16),
        scratch_shapes=[pltpu.VMEM((slab + edge, width), f32)],
        compiler_params=pltpu.CompilerParams(vmem_limit_bytes=16 << 20),
        name="combine",
    )(projected, before, short_filter, mixed)


def transform(fwd_ref, block):
    return jnp.dot(fwd_ref[...], jnp.concatenate([block, block], axis=0), preferred_element_type=f32)


def respond_kernel(filter_ref, decay_ref, fwd_ref, out_ref):
    taps = filter_ref.shape[0]
    lag = lax.broadcasted_iota(jnp.int32, (taps, 1), 0)
    faded = filter_ref[...] * jnp.exp(-decay_ref[...] * lag.astype(f32))
    response = transform(fwd_ref, faded.astype(bf16))
    h_cos, h_sin = response[:taps], response[taps:]
    out_ref[0] = h_cos
    out_ref[1] = jnp.where(lag == 0, 0.0, h_sin)
    out_ref[2] = jnp.where(lag == 0, h_sin, h_cos)


def respond(medium_filter, decay, forward, width):
    taps, channels = medium_filter.shape
    return pl.pallas_call(
        respond_kernel,
        grid=(channels // width,),
        in_specs=[
            pl.BlockSpec((taps, width), lambda i: (0, i)),
            pl.BlockSpec((1, width), lambda i: (0, i)),
            pl.BlockSpec(forward.shape, lambda i: (0, 0)),
        ],
        out_specs=pl.BlockSpec((3, taps, width), lambda i: (0, 0, i)),
        out_shape=pltpu.MemorySpace.HBM((3, taps, channels), f32),
        compiler_params=pltpu.CompilerParams(vmem_limit_bytes=8 << 20),
        name="respond",
    )(medium_filter, decay.reshape(1, channels), forward)


def mix_kernel(
    gated_ref, halo_ref, head_ref, short_ref, response_ref, fwd_ref, inv_ref, out_ref, s
):
    taps = response_ref.shape[1]
    blocks = gated_ref.shape[0] // taps
    feats = []
    for k in range(2):
        s[0:edge] = halo_ref[taps + k * edge : taps + (k + 1) * edge].astype(f32)
        s[edge : 2 * edge] = head_ref[k].astype(f32)
        total = None
        for lag in range(short_ref.shape[0]):
            term = short_ref[lag, k + 1][None] * s[edge - lag : 2 * edge - lag]
            total = term if total is None else total + term
        feats.append(total)
    first = (feats[0] * feats[1]).astype(bf16)

    row = lax.broadcasted_iota(jnp.int32, (2 * taps, 1), 0)
    sign = jnp.where(row % 2 == 0, 1.0, -1.0).astype(f32)
    h_cos, h_sin, h_low = response_ref[0], response_ref[1], response_ref[2]
    last = transform(fwd_ref, halo_ref[0:taps])
    for b in range(blocks):
        if b == 0:
            block = jnp.concatenate([first, gated_ref[edge:taps]], axis=0)
        else:
            block = gated_ref[b * taps : (b + 1) * taps]
        now = transform(fwd_ref, block)
        x = last + sign * now
        last = now
        x_cos, x_sin = x[:taps], x[taps:]
        y = jnp.concatenate([x_cos * h_cos - x_sin * h_sin, x_sin * h_low + x_cos * h_sin], axis=0)
        high = y.astype(bf16)
        low = (y - high.astype(f32)).astype(bf16)
        out_ref[b * taps : (b + 1) * taps] = jnp.dot(
            inv_ref[...], jnp.concatenate([high, low, high], axis=0), preferred_element_type=f32
        )


def mix(gated, halo, head, short_filter, response, tables, width):
    slab, channels = gated.shape
    count = response.shape[1]
    forward, inverse = tables
    col = lambda rows: pl.BlockSpec((rows, width), lambda i: (0, i))
    cube = lambda a, b: pl.BlockSpec((a, b, width), lambda i: (0, 0, i))
    return pl.pallas_call(
        mix_kernel,
        grid=(channels // width,),
        in_specs=[
            col(slab),
            col(count + 2 * edge),
            cube(2, edge),
            cube(*short_filter.shape[:2]),
            cube(3, count),
            pl.BlockSpec(forward.shape, lambda i: (0, 0)),
            pl.BlockSpec(inverse.shape, lambda i: (0, 0)),
        ],
        out_specs=col(slab),
        out_shape=jax.ShapeDtypeStruct((slab, channels), f32),
        scratch_shapes=[pltpu.VMEM((2 * edge, width), f32)],
        compiler_params=pltpu.CompilerParams(vmem_limit_bytes=16 << 20),
        name="mix",
    )(hold(gated), hold(halo), hold(head), short_filter, hold(response), forward, inverse)


def local(tokens, norm_gain, w_in, short_filter, medium_filter, decay, w_out):
    groups, contexts, count = (lax.axis_size(a) for a in axes)
    g, c, z = (lax.axis_index(a) for a in axes)
    length, features = tokens.shape
    rows, branches, channels = w_in.shape
    slab = length * count
    width = min(channels, 256)
    paired = contexts == 4 and groups == 2

    def move(value, target):
        pairs = []
        for i in range(groups):
            for j in range(contexts):
                for k in range(count):
                    to = target(i, j, k)
                    if 0 <= to[1] < contexts and 0 <= to[2] < count:
                        pairs.append(
                            ((i * contexts + j) * count + k, (to[0] * contexts + to[1]) * count + to[2])
                        )
        return lax.ppermute(value, axes, pairs)

    to_chip = lambda v: move(v, lambda i, j, k: (i, j ^ 2, k))
    to_core = lambda v: move(v, lambda i, j, k: (i, j ^ 1, k))
    to_group = lambda v: move(v, lambda i, j, k: (1 - i, j, k))
    to_next = lambda v: move(v, lambda i, j, k: (i, j + 1, k))
    send = lambda v, pairs: move(v, lambda i, j, k: (i, j, pairs.get(k, -1)))
    to_up = lambda v: move(v, lambda i, j, k: (i, j, k + 1))
    to_down = lambda v: move(v, lambda i, j, k: (i, j, k - 1))

    def after(value, *earlier):
        return lax.optimization_barrier((value, *earlier))[0]

    medium_count = medium_filter.shape[0]
    tables = fourier_tables(medium_count)
    weights = jnp.transpose(w_in, (1, 0, 2))
    half = rows // 2
    out_rows = w_out.shape[0]
    if paired:
        first_half, other_half = g * half, (1 - g) * half
        peer = to_core(weights)
        near, far, pieces = {}, {}, {}
        def cut(source, b, first, depth):
            part = lax.dynamic_slice(source, (b, first, 0), (1, depth, channels))
            return part.reshape(depth, channels)

        mine = cut(weights, 1, first_half, half)
        normed = norm(after(tokens, mine), norm_gain)
        response = respond(medium_filter, decay, tables[0], width)
        near[1] = to_chip(mine)
        far[1] = to_group(near[1])
        source = after(weights, normed)
        near[2] = to_chip(after(cut(source, 2, first_half, half), near[1]))
        far[2] = to_group(after(near[2], far[1], response, peer))
        near[0] = to_chip(after(cut(source, 0, first_half, half), near[2]))
        far[0] = to_group(after(near[0], far[2]))
        for b in (1, 2, 0):
            pieces[b] = [
                (weights, b, c * rows),
                (peer, b, (c ^ 1) * rows),
                (near[b], None, (c ^ 2) * rows + first_half),
                (to_core(near[b]), None, (c ^ 3) * rows + first_half),
                (far[b], None, (c ^ 2) * rows + other_half),
            ]
            if b != 0:
                late = after(far[2], near[0]) if b == 2 else far[1]
                pieces[b].append((to_core(late), None, (c ^ 3) * rows + other_half))
    else:
        normed = norm(tokens, norm_gain)
        response = respond(medium_filter, decay, tables[0], width)
        full = lax.all_gather(weights, "context", axis=1, tiled=True)
        pieces = {b: [(full, b, 0)] for b in (1, 2)}
        middle = features // 2
        pieces[0] = [(full[0, :middle], None, 0), (full[0, middle:], None, middle)]

    gathered = lax.all_gather(normed, "tensor", axis=0, tiled=True)
    gate_taps = after(short_filter, response)
    gated, head, edges, total = gate(
        gathered, pieces[1], pieces[2], pieces[0][:-1], gate_taps, medium_count, width
    )
    halo = to_next(edges)
    late = pieces[0][-1:]
    if paired:
        late.append((to_core(after(far[0], gated)), None, (c ^ 3) * rows + other_half))
    projected, tail = query(gathered, late, after(total, halo), width)
    before = to_next(tail)
    mixed = mix(gated, halo, head, short_filter, response, tables, width)
    combined = combine(projected, before, short_filter, mixed, width)
    if paired:
        out_full = lax.all_gather(after(w_out, near[1]), "context", axis=0, tiled=True)
        out_peer = to_core(after(w_out, tail))
        part = lambda i: lax.dynamic_slice(out_full, ((c ^ i) * out_rows, 0), (out_rows, channels))
        sets = [w_out, out_peer, part(2), part(3)]
    else:
        sets = [lax.all_gather(w_out, "context", axis=0, tiled=True)]

    def plus(*terms):
        total = terms[0].astype(f32)
        for term in terms[1:]:
            total = total + term.astype(f32)
        return total.astype(bf16)

    def product(rows_out):
        return lax.dot_general(
            combined, rows_out, (((1,), (1,)), ((), ())), preferred_element_type=f32
        ).astype(bf16)

    results, firsts, seconds = [], [], []
    for n, rows_out in enumerate(sets):
        if paired and n == 2:
            combined = after(combined, firsts[1])
        partial = product(rows_out)
        combined = after(combined, partial)

        def block(index, blocks=1, partial=partial):
            index = jnp.clip(index, 0, count - blocks)
            return lax.dynamic_slice(
                partial, (index * length, 0), (blocks * length, partial.shape[1])
            )

        if count == 4:
            far_pair = block(jnp.where(z < 2, 2, 0), 2)
            firsts.append(send(far_pair, {0: 1, 3: 2}))
            got = plus(far_pair, firsts[-1])
            if n >= 2:
                got = after(got, seconds[n - 2])
            got = send(got, {1: 2, 2: 1})
            seconds.append(got)
            low, high = got[:length], got[length:]
            odd = z % 2 == 1
            got_own = jnp.where(odd, high, low)
            got_other = jnp.where(odd, low, high)
            last = send(plus(block(z ^ 1), got_other), {0: 1, 1: 0, 2: 3, 3: 2})
            results.append(plus(block(z), got_own, last))
        else:
            up = down = None
            for s in range(1, count):
                rising = block(count + z - s)
                falling = block(z - count + s)
                if up is not None:
                    rising, falling = plus(rising, up), plus(falling, down)
                up, down = to_up(rising), to_down(falling)
            results.append(plus(block(z), up, down))
    if not paired:
        return results[0]
    swap = lambda test, a, b: (jnp.where(test, b, a), jnp.where(test, a, b))
    e0, e1, e2, e3 = results
    odd = c % 2 == 1
    low = jnp.concatenate(swap(odd, e0, e1), 1)
    high = jnp.concatenate(swap(odd, e2, e3), 1)
    return jnp.concatenate(swap(c >= 2, low, high), 1)


def solution(mesh):
    in_specs = (
        P(axes, None),
        P(),
        P("context", None, "tensor"),
        P(None, None, "tensor"),
        P(None, "tensor"),
        P("tensor"),
        P("context", "tensor"),
    )
    return jax.shard_map(
        local, mesh=mesh, in_specs=in_specs, out_specs=P(axes, None), check_vma=False
    )
```

```python
import functools
import jax
import jax.numpy as jnp
import ml_dtypes
import numpy as np
from jax import lax
from jax.experimental import pallas as pl
from jax.experimental.pallas import tpu as pltpu
from jax.sharding import PartitionSpec as P

norm_epsilon = 1e-06
axes = ("groups", "context", "tensor")
edge = 16
f32 = jnp.float32
bf16 = jnp.bfloat16


def split_parts(matrix):
    high = matrix.astype(ml_dtypes.bfloat16)
    low = (matrix - high.astype(np.float64)).astype(ml_dtypes.bfloat16)
    return high, low


def fourier_tables(taps):
    size = 2 * taps
    freq = np.arange(taps)[:, None]
    time = np.arange(size)[None, :]
    angle = 2 * np.pi * ((freq * time) % size) / size
    cosine, sine = np.cos(angle), np.sin(angle)
    sine[0] = 1.0 - 2.0 * (np.arange(size) % 2)
    forward = np.concatenate([cosine, sine], axis=0)
    weight = np.full((2 * taps, 1), 2.0 / size)
    weight[0] = weight[taps] = 1.0 / size
    inverse = (forward * weight)[:, taps:].T
    fh, fl = split_parts(forward[:, :taps])
    ih, il = split_parts(inverse)
    return np.concatenate([fh, fl], axis=1), np.concatenate([ih, ih, il], axis=1)


def short_sum(s, taps_ref, branch, slab):
    total = None
    for lag in range(taps_ref.shape[0]):
        term = taps_ref[lag, branch][None] * s[edge - lag : edge - lag + slab]
        total = term if total is None else total + term
    return total


def norm_kernel(x_ref, gain_ref, out_ref):
    values = x_ref[...].astype(f32)
    mean = jnp.mean(values * values, axis=1, keepdims=True)
    scaled = values * lax.rsqrt(mean + norm_epsilon)
    out_ref[...] = (scaled * gain_ref[...].astype(f32)).astype(bf16)


def norm(tokens, gain):
    length, features = tokens.shape
    rows = min(length, 32)
    return pl.pallas_call(
        norm_kernel,
        grid=(length // rows,),
        in_specs=[
            pl.BlockSpec((rows, features), lambda i: (i, 0)),
            pl.BlockSpec((1, features), lambda i: (0, 0)),
        ],
        out_specs=pl.BlockSpec((rows, features), lambda i: (i, 0)),
        out_shape=jax.ShapeDtypeStruct((length, features), bf16),
        compiler_params=pltpu.CompilerParams(vmem_limit_bytes=8 << 20),
        name="norm",
    )(tokens, gain.reshape(1, features))


in_hbm = pl.BlockSpec(memory_space=pltpu.MemorySpace.HBM)
in_vmem = pl.BlockSpec(memory_space=pltpu.MemorySpace.VMEM)
in_smem = pl.BlockSpec(memory_space=pltpu.MemorySpace.SMEM)


def hold(array):
    return pltpu.with_memory_space_constraint(array, pltpu.MemorySpace.HBM)


def kinds_of(pieces):
    return tuple((branch, array.shape[-2]) for array, branch, _ in pieces)


def offsets(pieces):
    return jnp.stack([jnp.asarray(p[2], jnp.int32) for p in pieces])


def spans(kinds):
    start = 0
    for _, depth in kinds:
        yield start, start + depth
        start += depth


def token_copies(kinds, at_ref, x_ref, target, sems):
    copies = []
    for n, (low, high) in enumerate(spans(kinds)):
        columns = pl.ds(pl.multiple_of(at_ref[n], min(high - low, 256)), high - low)
        copies.append(
            pltpu.make_async_copy(x_ref.at[:, columns], target.at[:, low:high], sems.at[n])
        )
    return copies


def weight_copies(kinds, arrays, target, sems):
    copies = []
    for n, (low, high) in enumerate(spans(kinds)):
        branch = kinds[n][0]
        source = arrays[n] if branch is None else arrays[n].at[branch]
        copies.append(pltpu.make_async_copy(source, target.at[low:high], sems.at[n]))
    return copies


def add_up(kinds, width, waits, full, weight, s, first):
    rows = slice(first, None)
    channels = weight.shape[1]
    for n, (low, high) in enumerate(spans(kinds)):
        for copies in waits:
            copies[n].wait()
        for i in range(channels // width):
            columns = slice(i * width, (i + 1) * width)
            term = jnp.dot(
                full[:, low:high], weight[low:high, columns], preferred_element_type=f32
            )
            if n > 0:
                term = s[rows, columns] + term
            if n == len(kinds) - 1 and first is not None:
                term = term.astype(bf16).astype(f32)
            s[rows, columns] = term


def gate_kernel(one, two, three, width, at_ref, x_ref, taps_ref, *rest):
    arrays = rest[: len(one) + len(two) + len(three)]
    gated_ref, head_ref, halo_ref, sum_ref, full, weights, s1, feat, s2, sems = rest[len(arrays) :]
    slab, channels = gated_ref.shape
    count = halo_ref.shape[0] - 2 * edge
    x_copies = token_copies(one, at_ref, x_ref, full, sems.at[0])
    copies = [
        weight_copies(one, arrays[: len(one)], weights.at[0], sems.at[1]),
        weight_copies(two, arrays[len(one) : -len(three)], weights.at[1], sems.at[2]),
        weight_copies(three, arrays[-len(three) :], weights.at[2], sems.at[3]),
    ]
    for x_copy, copy in zip(x_copies, copies[0]):
        x_copy.start()
        copy.start()
    for copy in copies[1] + copies[2]:
        copy.start()
    s1[0:edge] = jnp.zeros((edge, channels), f32)
    add_up(one, width, (x_copies, copies[0]), full, weights.at[0], s1, edge)
    head_ref[0] = s1[edge : 2 * edge].astype(bf16)
    halo_ref[count : count + edge] = s1[slab : slab + edge].astype(bf16)
    feat[...] = short_sum(s1, taps_ref, 1, slab)
    for copy in copies[1]:
        copy.wait()
    s2[0:edge] = jnp.zeros((edge, width), f32)
    for i in range(channels // width):
        columns = slice(i * width, (i + 1) * width)
        term = jnp.dot(full[...], weights[1, :, columns], preferred_element_type=f32)
        s2[edge : edge + slab] = term.astype(bf16).astype(f32)
        head_ref[1, :, columns] = s2[edge : 2 * edge].astype(bf16)
        halo_ref[count + edge :, columns] = s2[slab : slab + edge].astype(bf16)
        gated = feat[:, columns] * short_sum(s2, taps_ref[:, :, columns], 2, slab)
        gated = gated.astype(bf16)
        gated_ref[:, columns] = gated
        halo_ref[0:count, columns] = gated[slab - count :]
    for copy in copies[2]:
        copy.wait()
    depth = list(spans(three))[-1][1]
    for i in range(channels // width):
        columns = slice(i * width, (i + 1) * width)
        sum_ref[:, columns] = jnp.dot(
            full[:, 0:depth], weights[2, 0:depth, columns], preferred_element_type=f32
        )


def gate(x, one, two, three, short_filter, taps, width):
    slab, features = x.shape
    channels = short_filter.shape[-1]
    return pl.pallas_call(
        functools.partial(gate_kernel, kinds_of(one), kinds_of(two), kinds_of(three), width),
        in_specs=[in_smem, in_hbm, in_vmem] + [in_hbm] * (len(one) + len(two) + len(three)),
        out_specs=[in_vmem] * 4,
        out_shape=[
            pltpu.MemorySpace.HBM((slab, channels), bf16),
            pltpu.MemorySpace.HBM((2, edge, channels), bf16),
            pltpu.MemorySpace.HBM((taps + 2 * edge, channels), bf16),
            jax.ShapeDtypeStruct((slab, channels), f32),
        ],
        scratch_shapes=[
            pltpu.VMEM((slab, features), bf16),
            pltpu.VMEM((3, features, channels), bf16),
            pltpu.VMEM((slab + edge, channels), f32),
            pltpu.VMEM((slab, channels), f32),
            pltpu.VMEM((slab + edge, width), f32),
            pltpu.SemaphoreType.DMA((4, len(one))),
        ],
        compiler_params=pltpu.CompilerParams(vmem_limit_bytes=48 << 20),
        name="gate",
    )(offsets(one), hold(x), short_filter, *[hold(p[0]) for p in one + two + three])


def query_kernel(kinds, width, at_ref, x_ref, sum_ref, *rest):
    arrays = rest[: len(kinds)]
    out_ref, tail_ref, full, weight, sems = rest[len(arrays) :]
    slab, channels = out_ref.shape
    x_copies = token_copies(kinds, at_ref, x_ref, full, sems.at[0])
    copies = weight_copies(kinds, arrays, weight, sems.at[1])
    for copy in x_copies + copies:
        copy.start()
    for copy in x_copies + copies:
        copy.wait()
    for i in range(channels // width):
        columns = slice(i * width, (i + 1) * width)
        term = jnp.dot(full[...], weight[:, columns], preferred_element_type=f32)
        out_ref[:, columns] = (sum_ref[:, columns] + term).astype(bf16)
    tail_ref[...] = out_ref[slab - edge :]


def query(x, pieces, total, width):
    slab, channels = total.shape
    kinds = kinds_of(pieces)
    depth = sum(k[1] for k in kinds)
    return pl.pallas_call(
        functools.partial(query_kernel, kinds, width),
        in_specs=[in_smem, in_hbm, in_vmem] + [in_hbm] * len(pieces),
        out_specs=[in_vmem] * 2,
        out_shape=[
            jax.ShapeDtypeStruct((slab, channels), bf16),
            pltpu.MemorySpace.HBM((edge, channels), bf16),
        ],
        scratch_shapes=[
            pltpu.VMEM((slab, depth), bf16),
            pltpu.VMEM((depth, channels), bf16),
            pltpu.SemaphoreType.DMA((2, len(pieces))),
        ],
        compiler_params=pltpu.CompilerParams(vmem_limit_bytes=16 << 20),
        name="query",
    )(offsets(pieces), hold(x), total, *[hold(p[0]) for p in pieces])


def combine_kernel(projected_ref, before_ref, taps_ref, mixed_ref, out_ref, s):
    slab = out_ref.shape[0]
    s[0:edge] = before_ref[...].astype(f32)
    s[edge : edge + slab] = projected_ref[...].astype(f32)
    out_ref[...] = (short_sum(s, taps_ref, 0, slab) * mixed_ref[...]).astype(bf16)


def combine(projected, before, short_filter, mixed, width):
    slab, channels = mixed.shape
    col = lambda rows: pl.BlockSpec((rows, width), lambda i: (0, i))
    return pl.pallas_call(
        combine_kernel,
        grid=(channels // width,),
        in_specs=[
            col(slab),
            col(edge),
            pl.BlockSpec(short_filter.shape[:2] + (width,), lambda i: (0, 0, i)),
            col(slab),
        ],
        out_specs=col(slab),
        out_shape=jax.ShapeDtypeStruct((slab, channels), bf16),
        scratch_shapes=[pltpu.VMEM((slab + edge, width), f32)],
        compiler_params=pltpu.CompilerParams(vmem_limit_bytes=16 << 20),
        name="combine",
    )(projected, before, short_filter, mixed)


def transform(fwd_ref, block):
    return jnp.dot(fwd_ref[...], jnp.concatenate([block, block], axis=0), preferred_element_type=f32)


def respond_kernel(filter_ref, decay_ref, fwd_ref, out_ref):
    taps = filter_ref.shape[0]
    lag = lax.broadcasted_iota(jnp.int32, (taps, 1), 0)
    faded = filter_ref[...] * jnp.exp(-decay_ref[...] * lag.astype(f32))
    response = transform(fwd_ref, faded.astype(bf16))
    h_cos, h_sin = response[:taps], response[taps:]
    out_ref[0] = h_cos
    out_ref[1] = jnp.where(lag == 0, 0.0, h_sin)
    out_ref[2] = jnp.where(lag == 0, h_sin, h_cos)


def respond(medium_filter, decay, forward, width):
    taps, channels = medium_filter.shape
    return pl.pallas_call(
        respond_kernel,
        grid=(channels // width,),
        in_specs=[
            pl.BlockSpec((taps, width), lambda i: (0, i)),
            pl.BlockSpec((1, width), lambda i: (0, i)),
            pl.BlockSpec(forward.shape, lambda i: (0, 0)),
        ],
        out_specs=pl.BlockSpec((3, taps, width), lambda i: (0, 0, i)),
        out_shape=pltpu.MemorySpace.HBM((3, taps, channels), f32),
        compiler_params=pltpu.CompilerParams(vmem_limit_bytes=8 << 20),
        name="respond",
    )(medium_filter, decay.reshape(1, channels), forward)


def mix_kernel(
    gated_ref, halo_ref, head_ref, short_ref, response_ref, fwd_ref, inv_ref, out_ref, s
):
    taps = response_ref.shape[1]
    blocks = gated_ref.shape[0] // taps
    feats = []
    for k in range(2):
        s[0:edge] = halo_ref[taps + k * edge : taps + (k + 1) * edge].astype(f32)
        s[edge : 2 * edge] = head_ref[k].astype(f32)
        total = None
        for lag in range(short_ref.shape[0]):
            term = short_ref[lag, k + 1][None] * s[edge - lag : 2 * edge - lag]
            total = term if total is None else total + term
        feats.append(total)
    first = (feats[0] * feats[1]).astype(bf16)

    row = lax.broadcasted_iota(jnp.int32, (2 * taps, 1), 0)
    sign = jnp.where(row % 2 == 0, 1.0, -1.0).astype(f32)
    h_cos, h_sin, h_low = response_ref[0], response_ref[1], response_ref[2]
    last = transform(fwd_ref, halo_ref[0:taps])
    for b in range(blocks):
        if b == 0:
            block = jnp.concatenate([first, gated_ref[edge:taps]], axis=0)
        else:
            block = gated_ref[b * taps : (b + 1) * taps]
        now = transform(fwd_ref, block)
        x = last + sign * now
        last = now
        x_cos, x_sin = x[:taps], x[taps:]
        y = jnp.concatenate([x_cos * h_cos - x_sin * h_sin, x_sin * h_low + x_cos * h_sin], axis=0)
        high = y.astype(bf16)
        low = (y - high.astype(f32)).astype(bf16)
        out_ref[b * taps : (b + 1) * taps] = jnp.dot(
            inv_ref[...], jnp.concatenate([high, low, high], axis=0), preferred_element_type=f32
        )


def mix(gated, halo, head, short_filter, response, tables, width):
    slab, channels = gated.shape
    count = response.shape[1]
    forward, inverse = tables
    col = lambda rows: pl.BlockSpec((rows, width), lambda i: (0, i))
    cube = lambda a, b: pl.BlockSpec((a, b, width), lambda i: (0, 0, i))
    return pl.pallas_call(
        mix_kernel,
        grid=(channels // width,),
        in_specs=[
            col(slab),
            col(count + 2 * edge),
            cube(2, edge),
            cube(*short_filter.shape[:2]),
            cube(3, count),
            pl.BlockSpec(forward.shape, lambda i: (0, 0)),
            pl.BlockSpec(inverse.shape, lambda i: (0, 0)),
        ],
        out_specs=col(slab),
        out_shape=jax.ShapeDtypeStruct((slab, channels), f32),
        scratch_shapes=[pltpu.VMEM((2 * edge, width), f32)],
        compiler_params=pltpu.CompilerParams(vmem_limit_bytes=16 << 20),
        name="mix",
    )(hold(gated), hold(halo), hold(head), short_filter, hold(response), forward, inverse)


def local(tokens, norm_gain, w_in, short_filter, medium_filter, decay, w_out):
    groups, contexts, count = (lax.axis_size(a) for a in axes)
    g, c, z = (lax.axis_index(a) for a in axes)
    length, features = tokens.shape
    rows, branches, channels = w_in.shape
    slab = length * count
    width = min(channels, 256)
    paired = contexts == 4 and groups == 2

    def move(value, target):
        pairs = []
        for i in range(groups):
            for j in range(contexts):
                for k in range(count):
                    to = target(i, j, k)
                    if 0 <= to[1] < contexts and 0 <= to[2] < count:
                        pairs.append(
                            ((i * contexts + j) * count + k, (to[0] * contexts + to[1]) * count + to[2])
                        )
        return lax.ppermute(value, axes, pairs)

    to_chip = lambda v: move(v, lambda i, j, k: (i, j ^ 2, k))
    to_core = lambda v: move(v, lambda i, j, k: (i, j ^ 1, k))
    to_group = lambda v: move(v, lambda i, j, k: (1 - i, j, k))
    to_next = lambda v: move(v, lambda i, j, k: (i, j + 1, k))
    send = lambda v, pairs: move(v, lambda i, j, k: (i, j, pairs.get(k, -1)))
    to_up = lambda v: move(v, lambda i, j, k: (i, j, k + 1))
    to_down = lambda v: move(v, lambda i, j, k: (i, j, k - 1))

    def after(value, *earlier):
        return lax.optimization_barrier((value, *earlier))[0]

    medium_count = medium_filter.shape[0]
    tables = fourier_tables(medium_count)
    weights = jnp.transpose(w_in, (1, 0, 2))
    half = rows // 2
    out_rows = w_out.shape[0]
    if paired:
        first_half, other_half = g * half, (1 - g) * half
        peer = to_core(weights)
        near, far, pieces = {}, {}, {}
        def cut(source, b, first, depth):
            part = lax.dynamic_slice(source, (b, first, 0), (1, depth, channels))
            return part.reshape(depth, channels)

        mine = cut(weights, 1, first_half, half)
        normed = norm(after(tokens, mine), norm_gain)
        response = respond(medium_filter, decay, tables[0], width)
        near[1] = to_chip(mine)
        far[1] = to_group(near[1])
        source = after(weights, normed)
        near[2] = to_chip(after(cut(source, 2, first_half, half), near[1]))
        far[2] = to_group(after(near[2], far[1], response, peer))
        near[0] = to_chip(after(cut(source, 0, first_half, half), near[2]))
        far[0] = to_group(after(near[0], far[2]))
        out_half = out_rows // 2
        mine = lax.dynamic_slice(w_out, (g * out_half, 0), (out_half, channels))
        near_out = to_chip(after(mine, near[0]))
        for b in (1, 2, 0):
            pieces[b] = [
                (weights, b, c * rows),
                (peer, b, (c ^ 1) * rows),
                (near[b], None, (c ^ 2) * rows + first_half),
                (to_core(near[b]), None, (c ^ 3) * rows + first_half),
                (far[b], None, (c ^ 2) * rows + other_half),
            ]
            if b != 0:
                late = after(far[2], near[0]) if b == 2 else far[1]
                pieces[b].append((to_core(late), None, (c ^ 3) * rows + other_half))
    else:
        normed = norm(tokens, norm_gain)
        response = respond(medium_filter, decay, tables[0], width)
        full = lax.all_gather(weights, "context", axis=1, tiled=True)
        pieces = {b: [(full, b, 0)] for b in (1, 2)}
        middle = features // 2
        pieces[0] = [(full[0, :middle], None, 0), (full[0, middle:], None, middle)]

    gathered = lax.all_gather(normed, "tensor", axis=0, tiled=True)
    gate_taps = after(short_filter, response)
    gated, head, edges, total = gate(
        gathered, pieces[1], pieces[2], pieces[0][:-1], gate_taps, medium_count, width
    )
    halo = to_next(edges)
    late = pieces[0][-1:]
    if paired:
        late.append((to_core(after(far[0], near_out, halo)), None, (c ^ 3) * rows + other_half))
    projected, tail = query(gathered, late, total, width)
    before = to_next(tail)
    mixed = mix(gated, halo, head, short_filter, response, tables, width)
    combined = combine(projected, before, short_filter, mixed, width)
    if paired:
        out_other = lax.all_gather(after(near_out, gated), "groups", axis=0, tiled=True)
        out_peer = to_core(after(w_out, tail))
        sets = [w_out, out_peer, out_other, None]
    else:
        sets = [lax.all_gather(w_out, "context", axis=0, tiled=True)]

    def plus(*terms):
        total = terms[0].astype(f32)
        for term in terms[1:]:
            total = total + term.astype(f32)
        return total.astype(bf16)

    def product(rows_out):
        return lax.dot_general(
            combined, rows_out, (((1,), (1,)), ((), ())), preferred_element_type=f32
        ).astype(bf16)

    results, firsts, seconds = [], [], []
    for n in range(len(sets)):
        if n == 2:
            sets[2] = after(sets[2], combined, *firsts[:1])
            sets[3] = to_core(sets[2])
        rows_out = sets[n]
        partial = product(rows_out)
        combined = after(combined, partial)

        def block(index, blocks=1, partial=partial):
            index = jnp.clip(index, 0, count - blocks)
            return lax.dynamic_slice(
                partial, (index * length, 0), (blocks * length, partial.shape[1])
            )

        if count == 4:
            far_pair = block(jnp.where(z < 2, 2, 0), 2)
            firsts.append(send(far_pair, {0: 1, 3: 2}))
            got = plus(far_pair, firsts[-1])
            got = send(got, {1: 2, 2: 1})
            seconds.append(got)
            low, high = got[:length], got[length:]
            odd = z % 2 == 1
            got_own = jnp.where(odd, high, low)
            got_other = jnp.where(odd, low, high)
            last = send(plus(block(z ^ 1), got_other), {0: 1, 1: 0, 2: 3, 3: 2})
            results.append(plus(block(z), got_own, last))
        else:
            up = down = None
            for s in range(1, count):
                rising = block(count + z - s)
                falling = block(z - count + s)
                if up is not None:
                    rising, falling = plus(rising, up), plus(falling, down)
                up, down = to_up(rising), to_down(falling)
            results.append(plus(block(z), up, down))
    if not paired:
        return results[0]
    swap = lambda test, a, b: (jnp.where(test, b, a), jnp.where(test, a, b))
    e0, e1, e2, e3 = results
    odd = c % 2 == 1
    low = jnp.concatenate(swap(odd, e0, e1), 1)
    high = jnp.concatenate(swap(odd, e2, e3), 1)
    return jnp.concatenate(swap(c >= 2, low, high), 1)


def solution(mesh):
    in_specs = (
        P(axes, None),
        P(),
        P("context", None, "tensor"),
        P(None, None, "tensor"),
        P(None, "tensor"),
        P("tensor"),
        P("context", "tensor"),
    )
    return jax.shard_map(
        local, mesh=mesh, in_specs=in_specs, out_specs=P(axes, None), check_vma=False
    )
```

```python
import functools
import jax
import jax.numpy as jnp
import ml_dtypes
import numpy as np
from jax import lax
from jax.experimental import pallas as pl
from jax.experimental.pallas import tpu as pltpu
from jax.sharding import PartitionSpec as P

norm_epsilon = 1e-06
axes = ("groups", "context", "tensor")
edge = 16
f32 = jnp.float32
bf16 = jnp.bfloat16


def split_parts(matrix):
    high = matrix.astype(ml_dtypes.bfloat16)
    low = (matrix - high.astype(np.float64)).astype(ml_dtypes.bfloat16)
    return high, low


def fourier_tables(taps):
    size = 2 * taps
    freq = np.arange(taps)[:, None]
    time = np.arange(size)[None, :]
    angle = 2 * np.pi * ((freq * time) % size) / size
    cosine, sine = np.cos(angle), np.sin(angle)
    sine[0] = 1.0 - 2.0 * (np.arange(size) % 2)
    forward = np.concatenate([cosine, sine], axis=0)
    weight = np.full((2 * taps, 1), 2.0 / size)
    weight[0] = weight[taps] = 1.0 / size
    inverse = (forward * weight)[:, taps:].T
    fh, fl = split_parts(forward[:, :taps])
    ih, il = split_parts(inverse)
    return np.concatenate([fh, fl], axis=1), np.concatenate([ih, ih, il], axis=1)


def short_sum(s, taps_ref, branch, slab):
    total = None
    for lag in range(taps_ref.shape[0]):
        term = taps_ref[lag, branch][None] * s[edge - lag : edge - lag + slab]
        total = term if total is None else total + term
    return total


def norm_kernel(x_ref, gain_ref, out_ref):
    values = x_ref[...].astype(f32)
    mean = jnp.mean(values * values, axis=1, keepdims=True)
    scaled = values * lax.rsqrt(mean + norm_epsilon)
    out_ref[...] = (scaled * gain_ref[...].astype(f32)).astype(bf16)


def norm(tokens, gain):
    length, features = tokens.shape
    rows = min(length, 32)
    return pl.pallas_call(
        norm_kernel,
        grid=(length // rows,),
        in_specs=[
            pl.BlockSpec((rows, features), lambda i: (i, 0)),
            pl.BlockSpec((1, features), lambda i: (0, 0)),
        ],
        out_specs=pl.BlockSpec((rows, features), lambda i: (i, 0)),
        out_shape=jax.ShapeDtypeStruct((length, features), bf16),
        compiler_params=pltpu.CompilerParams(vmem_limit_bytes=8 << 20),
        name="norm",
    )(tokens, gain.reshape(1, features))


in_hbm = pl.BlockSpec(memory_space=pltpu.MemorySpace.HBM)
in_vmem = pl.BlockSpec(memory_space=pltpu.MemorySpace.VMEM)
in_smem = pl.BlockSpec(memory_space=pltpu.MemorySpace.SMEM)


def hold(array):
    return pltpu.with_memory_space_constraint(array, pltpu.MemorySpace.HBM)


def kinds_of(pieces):
    return tuple((branch, array.shape[-2]) for array, branch, _ in pieces)


def offsets(pieces):
    return jnp.stack([jnp.asarray(p[2], jnp.int32) for p in pieces])


def spans(kinds):
    start = 0
    for _, depth in kinds:
        yield start, start + depth
        start += depth


def token_copies(kinds, at_ref, x_ref, target, sems):
    copies = []
    for n, (low, high) in enumerate(spans(kinds)):
        columns = pl.ds(pl.multiple_of(at_ref[n], min(high - low, 256)), high - low)
        copies.append(
            pltpu.make_async_copy(x_ref.at[:, columns], target.at[:, low:high], sems.at[n])
        )
    return copies


def weight_copies(kinds, arrays, target, sems):
    copies = []
    for n, (low, high) in enumerate(spans(kinds)):
        branch = kinds[n][0]
        source = arrays[n] if branch is None else arrays[n].at[branch]
        copies.append(pltpu.make_async_copy(source, target.at[low:high], sems.at[n]))
    return copies


def add_up(kinds, width, waits, full, weight, s, first):
    rows = slice(first, None)
    channels = weight.shape[1]
    for n, (low, high) in enumerate(spans(kinds)):
        for copies in waits:
            copies[n].wait()
        for i in range(channels // width):
            columns = slice(i * width, (i + 1) * width)
            term = jnp.dot(
                full[:, low:high], weight[low:high, columns], preferred_element_type=f32
            )
            if n > 0:
                term = s[rows, columns] + term
            if n == len(kinds) - 1 and first is not None:
                term = term.astype(bf16).astype(f32)
            s[rows, columns] = term


def gate_kernel(one, two, three, width, at_ref, x_ref, taps_ref, *rest):
    arrays = rest[: len(one) + len(two) + len(three)]
    gated_ref, head_ref, halo_ref, sum_ref, full, weights, s1, feat, s2, sems = rest[len(arrays) :]
    slab, channels = gated_ref.shape
    count = halo_ref.shape[0] - 2 * edge
    x_copies = token_copies(one, at_ref, x_ref, full, sems.at[0])
    copies = [
        weight_copies(one, arrays[: len(one)], weights.at[0], sems.at[1]),
        weight_copies(two, arrays[len(one) : -len(three)], weights.at[1], sems.at[2]),
        weight_copies(three, arrays[-len(three) :], weights.at[2], sems.at[3]),
    ]
    for x_copy, copy in zip(x_copies, copies[0]):
        x_copy.start()
        copy.start()
    for copy in copies[1] + copies[2]:
        copy.start()
    s1[0:edge] = jnp.zeros((edge, channels), f32)
    add_up(one, width, (x_copies, copies[0]), full, weights.at[0], s1, edge)
    head_ref[0] = s1[edge : 2 * edge].astype(bf16)
    halo_ref[count : count + edge] = s1[slab : slab + edge].astype(bf16)
    feat[...] = short_sum(s1, taps_ref, 1, slab)
    for copy in copies[1]:
        copy.wait()
    s2[0:edge] = jnp.zeros((edge, width), f32)
    for i in range(channels // width):
        columns = slice(i * width, (i + 1) * width)
        term = jnp.dot(full[...], weights[1, :, columns], preferred_element_type=f32)
        s2[edge : edge + slab] = term.astype(bf16).astype(f32)
        head_ref[1, :, columns] = s2[edge : 2 * edge].astype(bf16)
        halo_ref[count + edge :, columns] = s2[slab : slab + edge].astype(bf16)
        gated = feat[:, columns] * short_sum(s2, taps_ref[:, :, columns], 2, slab)
        gated = gated.astype(bf16)
        gated_ref[:, columns] = gated
        halo_ref[0:count, columns] = gated[slab - count :]
    for copy in copies[2]:
        copy.wait()
    depth = list(spans(three))[-1][1]
    for i in range(channels // width):
        columns = slice(i * width, (i + 1) * width)
        sum_ref[:, columns] = jnp.dot(
            full[:, 0:depth], weights[2, 0:depth, columns], preferred_element_type=f32
        )


def gate(x, one, two, three, short_filter, taps, width):
    slab, features = x.shape
    channels = short_filter.shape[-1]
    return pl.pallas_call(
        functools.partial(gate_kernel, kinds_of(one), kinds_of(two), kinds_of(three), width),
        in_specs=[in_smem, in_hbm, in_vmem] + [in_hbm] * (len(one) + len(two) + len(three)),
        out_specs=[in_vmem] * 4,
        out_shape=[
            pltpu.MemorySpace.HBM((slab, channels), bf16),
            pltpu.MemorySpace.HBM((2, edge, channels), bf16),
            pltpu.MemorySpace.HBM((taps + 2 * edge, channels), bf16),
            jax.ShapeDtypeStruct((slab, channels), f32),
        ],
        scratch_shapes=[
            pltpu.VMEM((slab, features), bf16),
            pltpu.VMEM((3, features, channels), bf16),
            pltpu.VMEM((slab + edge, channels), f32),
            pltpu.VMEM((slab, channels), f32),
            pltpu.VMEM((slab + edge, width), f32),
            pltpu.SemaphoreType.DMA((4, len(one))),
        ],
        compiler_params=pltpu.CompilerParams(vmem_limit_bytes=48 << 20),
        name="gate",
    )(offsets(one), hold(x), short_filter, *[hold(p[0]) for p in one + two + three])


def query_kernel(kinds, width, at_ref, x_ref, sum_ref, *rest):
    arrays = rest[: len(kinds)]
    out_ref, tail_ref, full, weight, sems = rest[len(arrays) :]
    slab, channels = out_ref.shape
    x_copies = token_copies(kinds, at_ref, x_ref, full, sems.at[0])
    copies = weight_copies(kinds, arrays, weight, sems.at[1])
    for copy in x_copies + copies:
        copy.start()
    for copy in x_copies + copies:
        copy.wait()
    for i in range(channels // width):
        columns = slice(i * width, (i + 1) * width)
        term = jnp.dot(full[...], weight[:, columns], preferred_element_type=f32)
        out_ref[:, columns] = (sum_ref[:, columns] + term).astype(bf16)
    tail_ref[...] = out_ref[slab - edge :]


def query(x, pieces, total, width):
    slab, channels = total.shape
    kinds = kinds_of(pieces)
    depth = sum(k[1] for k in kinds)
    return pl.pallas_call(
        functools.partial(query_kernel, kinds, width),
        in_specs=[in_smem, in_hbm, in_vmem] + [in_hbm] * len(pieces),
        out_specs=[in_vmem] * 2,
        out_shape=[
            jax.ShapeDtypeStruct((slab, channels), bf16),
            pltpu.MemorySpace.HBM((edge, channels), bf16),
        ],
        scratch_shapes=[
            pltpu.VMEM((slab, depth), bf16),
            pltpu.VMEM((depth, channels), bf16),
            pltpu.SemaphoreType.DMA((2, len(pieces))),
        ],
        compiler_params=pltpu.CompilerParams(vmem_limit_bytes=16 << 20),
        name="query",
    )(offsets(pieces), hold(x), total, *[hold(p[0]) for p in pieces])


def combine_kernel(projected_ref, before_ref, taps_ref, mixed_ref, out_ref, s):
    slab = out_ref.shape[0]
    s[0:edge] = before_ref[...].astype(f32)
    s[edge : edge + slab] = projected_ref[...].astype(f32)
    out_ref[...] = (short_sum(s, taps_ref, 0, slab) * mixed_ref[...]).astype(bf16)


def combine(projected, before, short_filter, mixed, width):
    slab, channels = mixed.shape
    col = lambda rows: pl.BlockSpec((rows, width), lambda i: (0, i))
    return pl.pallas_call(
        combine_kernel,
        grid=(channels // width,),
        in_specs=[
            col(slab),
            col(edge),
            pl.BlockSpec(short_filter.shape[:2] + (width,), lambda i: (0, 0, i)),
            col(slab),
        ],
        out_specs=col(slab),
        out_shape=jax.ShapeDtypeStruct((slab, channels), bf16),
        scratch_shapes=[pltpu.VMEM((slab + edge, width), f32)],
        compiler_params=pltpu.CompilerParams(vmem_limit_bytes=16 << 20),
        name="combine",
    )(projected, before, short_filter, mixed)


def transform(fwd_ref, block):
    return jnp.dot(fwd_ref[...], jnp.concatenate([block, block], axis=0), preferred_element_type=f32)


def respond_kernel(filter_ref, decay_ref, fwd_ref, out_ref):
    taps = filter_ref.shape[0]
    lag = lax.broadcasted_iota(jnp.int32, (taps, 1), 0)
    faded = filter_ref[...] * jnp.exp(-decay_ref[...] * lag.astype(f32))
    response = transform(fwd_ref, faded.astype(bf16))
    h_cos, h_sin = response[:taps], response[taps:]
    out_ref[0] = h_cos
    out_ref[1] = jnp.where(lag == 0, 0.0, h_sin)
    out_ref[2] = jnp.where(lag == 0, h_sin, h_cos)


def respond(medium_filter, decay, forward, width):
    taps, channels = medium_filter.shape
    return pl.pallas_call(
        respond_kernel,
        grid=(channels // width,),
        in_specs=[
            pl.BlockSpec((taps, width), lambda i: (0, i)),
            pl.BlockSpec((1, width), lambda i: (0, i)),
            pl.BlockSpec(forward.shape, lambda i: (0, 0)),
        ],
        out_specs=pl.BlockSpec((3, taps, width), lambda i: (0, 0, i)),
        out_shape=pltpu.MemorySpace.HBM((3, taps, channels), f32),
        compiler_params=pltpu.CompilerParams(vmem_limit_bytes=8 << 20),
        name="respond",
    )(medium_filter, decay.reshape(1, channels), forward)


def mix_kernel(
    gated_ref, halo_ref, head_ref, short_ref, response_ref, fwd_ref, inv_ref, out_ref, s
):
    taps = response_ref.shape[1]
    blocks = gated_ref.shape[0] // taps
    feats = []
    for k in range(2):
        s[0:edge] = halo_ref[taps + k * edge : taps + (k + 1) * edge].astype(f32)
        s[edge : 2 * edge] = head_ref[k].astype(f32)
        total = None
        for lag in range(short_ref.shape[0]):
            term = short_ref[lag, k + 1][None] * s[edge - lag : 2 * edge - lag]
            total = term if total is None else total + term
        feats.append(total)
    first = (feats[0] * feats[1]).astype(bf16)

    row = lax.broadcasted_iota(jnp.int32, (2 * taps, 1), 0)
    sign = jnp.where(row % 2 == 0, 1.0, -1.0).astype(f32)
    h_cos, h_sin, h_low = response_ref[0], response_ref[1], response_ref[2]
    last = transform(fwd_ref, halo_ref[0:taps])
    for b in range(blocks):
        if b == 0:
            block = jnp.concatenate([first, gated_ref[edge:taps]], axis=0)
        else:
            block = gated_ref[b * taps : (b + 1) * taps]
        now = transform(fwd_ref, block)
        x = last + sign * now
        last = now
        x_cos, x_sin = x[:taps], x[taps:]
        y = jnp.concatenate([x_cos * h_cos - x_sin * h_sin, x_sin * h_low + x_cos * h_sin], axis=0)
        high = y.astype(bf16)
        low = (y - high.astype(f32)).astype(bf16)
        out_ref[b * taps : (b + 1) * taps] = jnp.dot(
            inv_ref[...], jnp.concatenate([high, low, high], axis=0), preferred_element_type=f32
        )


def mix(gated, halo, head, short_filter, response, tables, width):
    slab, channels = gated.shape
    count = response.shape[1]
    forward, inverse = tables
    col = lambda rows: pl.BlockSpec((rows, width), lambda i: (0, i))
    cube = lambda a, b: pl.BlockSpec((a, b, width), lambda i: (0, 0, i))
    return pl.pallas_call(
        mix_kernel,
        grid=(channels // width,),
        in_specs=[
            col(slab),
            col(count + 2 * edge),
            cube(2, edge),
            cube(*short_filter.shape[:2]),
            cube(3, count),
            pl.BlockSpec(forward.shape, lambda i: (0, 0)),
            pl.BlockSpec(inverse.shape, lambda i: (0, 0)),
        ],
        out_specs=col(slab),
        out_shape=jax.ShapeDtypeStruct((slab, channels), f32),
        scratch_shapes=[pltpu.VMEM((2 * edge, width), f32)],
        compiler_params=pltpu.CompilerParams(vmem_limit_bytes=16 << 20),
        name="mix",
    )(hold(gated), hold(halo), hold(head), short_filter, hold(response), forward, inverse)


def local(tokens, norm_gain, w_in, short_filter, medium_filter, decay, w_out):
    groups, contexts, count = (lax.axis_size(a) for a in axes)
    g, c, z = (lax.axis_index(a) for a in axes)
    length, features = tokens.shape
    rows, branches, channels = w_in.shape
    slab = length * count
    width = min(channels, 256)
    paired = contexts == 4 and groups == 2

    def move(value, target):
        pairs = []
        for i in range(groups):
            for j in range(contexts):
                for k in range(count):
                    to = target(i, j, k)
                    if 0 <= to[1] < contexts and 0 <= to[2] < count:
                        pairs.append(
                            ((i * contexts + j) * count + k, (to[0] * contexts + to[1]) * count + to[2])
                        )
        return lax.ppermute(value, axes, pairs)

    to_chip = lambda v: move(v, lambda i, j, k: (i, j ^ 2, k))
    to_core = lambda v: move(v, lambda i, j, k: (i, j ^ 1, k))
    to_group = lambda v: move(v, lambda i, j, k: (1 - i, j, k))
    to_next = lambda v: move(v, lambda i, j, k: (i, j + 1, k))
    send = lambda v, pairs: move(v, lambda i, j, k: (i, j, pairs.get(k, -1)))
    to_up = lambda v: move(v, lambda i, j, k: (i, j, k + 1))
    to_down = lambda v: move(v, lambda i, j, k: (i, j, k - 1))

    def after(value, *earlier):
        return lax.optimization_barrier((value, *earlier))[0]

    medium_count = medium_filter.shape[0]
    tables = fourier_tables(medium_count)
    weights = jnp.transpose(w_in, (1, 0, 2))
    half = rows // 2
    out_rows = w_out.shape[0]
    if paired:
        first_half, other_half = g * half, (1 - g) * half
        peer = to_core(weights)
        near, far, pieces = {}, {}, {}
        def cut(source, b, first, depth):
            part = lax.dynamic_slice(source, (b, first, 0), (1, depth, channels))
            return part.reshape(depth, channels)

        mine = cut(weights, 1, first_half, half)
        normed = norm(after(tokens, mine), norm_gain)
        response = respond(medium_filter, decay, tables[0], width)
        near[1] = to_chip(mine)
        far[1] = to_group(near[1])
        source = after(weights, normed)
        near[2] = to_chip(after(cut(source, 2, first_half, half), near[1]))
        far[2] = to_group(after(near[2], far[1], response, peer))
        near[0] = to_chip(after(cut(source, 0, first_half, half), near[2]))
        far[0] = to_group(after(near[0], far[2]))
        out_half = out_rows // 2
        mine = lax.dynamic_slice(w_out, (g * out_half, 0), (out_half, channels))
        near_out = to_chip(after(mine, near[0]))
        for b in (1, 2, 0):
            pieces[b] = [
                (weights, b, c * rows),
                (peer, b, (c ^ 1) * rows),
                (near[b], None, (c ^ 2) * rows + first_half),
                (to_core(near[b]), None, (c ^ 3) * rows + first_half),
                (far[b], None, (c ^ 2) * rows + other_half),
            ]
            if b != 0:
                late = after(far[2], near[0]) if b == 2 else far[1]
                pieces[b].append((to_core(late), None, (c ^ 3) * rows + other_half))
    else:
        normed = norm(tokens, norm_gain)
        response = respond(medium_filter, decay, tables[0], width)
        full = lax.all_gather(weights, "context", axis=1, tiled=True)
        pieces = {b: [(full, b, 0)] for b in (1, 2)}
        middle = features // 2
        pieces[0] = [(full[0, :middle], None, 0), (full[0, middle:], None, middle)]

    gathered = lax.all_gather(normed, "tensor", axis=0, tiled=True)
    gate_taps = after(short_filter, response)
    gated, head, edges, total = gate(
        gathered, pieces[1], pieces[2], pieces[0][:-1], gate_taps, medium_count, width
    )
    halo = to_next(edges)
    late = pieces[0][-1:]
    if paired:
        late.append((to_core(after(far[0], near_out, halo)), None, (c ^ 3) * rows + other_half))
    projected, tail = query(gathered, late, total, width)
    before = to_next(tail)
    mixed = mix(gated, halo, head, short_filter, response, tables, width)
    combined = combine(projected, before, short_filter, mixed, width)
    if paired:
        out_other = lax.all_gather(after(near_out, gated), "groups", axis=0, tiled=True)
        out_peer = to_core(after(w_out, tail))
        sets = [w_out, out_peer, out_other, None]
    else:
        sets = [lax.all_gather(w_out, "context", axis=0, tiled=True)]

    def plus(*terms):
        total = terms[0].astype(f32)
        for term in terms[1:]:
            total = total + term.astype(f32)
        return total.astype(bf16)

    def product(rows_out):
        return lax.dot_general(
            combined, rows_out, (((1,), (1,)), ((), ())), preferred_element_type=f32
        ).astype(bf16)

    results, firsts, seconds = [], [], []
    for n in range(len(sets)):
        if n == 2:
            sets[2] = after(sets[2], firsts[1])
            sets[3] = to_core(after(sets[2], seconds[0]))
        rows_out = sets[n]
        partial = product(rows_out)
        combined = after(combined, partial)

        def block(index, blocks=1, partial=partial):
            index = jnp.clip(index, 0, count - blocks)
            return lax.dynamic_slice(
                partial, (index * length, 0), (blocks * length, partial.shape[1])
            )

        if count == 4:
            far_pair = block(jnp.where(z < 2, 2, 0), 2)
            firsts.append(send(far_pair, {0: 1, 3: 2}))
            got = plus(far_pair, firsts[-1])
            got = send(got, {1: 2, 2: 1})
            seconds.append(got)
            low, high = got[:length], got[length:]
            odd = z % 2 == 1
            got_own = jnp.where(odd, high, low)
            got_other = jnp.where(odd, low, high)
            last = send(plus(block(z ^ 1), got_other), {0: 1, 1: 0, 2: 3, 3: 2})
            results.append(plus(block(z), got_own, last))
        else:
            up = down = None
            for s in range(1, count):
                rising = block(count + z - s)
                falling = block(z - count + s)
                if up is not None:
                    rising, falling = plus(rising, up), plus(falling, down)
                up, down = to_up(rising), to_down(falling)
            results.append(plus(block(z), up, down))
    if not paired:
        return results[0]
    swap = lambda test, a, b: (jnp.where(test, b, a), jnp.where(test, a, b))
    e0, e1, e2, e3 = results
    odd = c % 2 == 1
    low = jnp.concatenate(swap(odd, e0, e1), 1)
    high = jnp.concatenate(swap(odd, e2, e3), 1)
    return jnp.concatenate(swap(c >= 2, low, high), 1)


def solution(mesh):
    in_specs = (
        P(axes, None),
        P(),
        P("context", None, "tensor"),
        P(None, None, "tensor"),
        P(None, "tensor"),
        P("tensor"),
        P("context", "tensor"),
    )
    return jax.shard_map(
        local, mesh=mesh, in_specs=in_specs, out_specs=P(axes, None), check_vma=False
    )
```

```python
import functools
import jax
import jax.numpy as jnp
import ml_dtypes
import numpy as np
from jax import lax
from jax.experimental import pallas as pl
from jax.experimental.pallas import tpu as pltpu
from jax.sharding import PartitionSpec as P

norm_epsilon = 1e-06
axes = ("groups", "context", "tensor")
edge = 16
f32 = jnp.float32
bf16 = jnp.bfloat16


def split_parts(matrix):
    high = matrix.astype(ml_dtypes.bfloat16)
    low = (matrix - high.astype(np.float64)).astype(ml_dtypes.bfloat16)
    return high, low


def fourier_tables(taps):
    size = 2 * taps
    freq = np.arange(taps)[:, None]
    time = np.arange(size)[None, :]
    angle = 2 * np.pi * ((freq * time) % size) / size
    cosine, sine = np.cos(angle), np.sin(angle)
    sine[0] = 1.0 - 2.0 * (np.arange(size) % 2)
    forward = np.concatenate([cosine, sine], axis=0)
    weight = np.full((2 * taps, 1), 2.0 / size)
    weight[0] = weight[taps] = 1.0 / size
    inverse = (forward * weight)[:, taps:].T
    fh, fl = split_parts(forward[:, :taps])
    ih, il = split_parts(inverse)
    return np.concatenate([fh, fl], axis=1), np.concatenate([ih, ih, il], axis=1)


def short_sum(s, taps_ref, branch, slab):
    total = None
    for lag in range(taps_ref.shape[0]):
        term = taps_ref[lag, branch][None] * s[edge - lag : edge - lag + slab]
        total = term if total is None else total + term
    return total


def norm_kernel(x_ref, gain_ref, out_ref):
    values = x_ref[...].astype(f32)
    mean = jnp.mean(values * values, axis=1, keepdims=True)
    scaled = values * lax.rsqrt(mean + norm_epsilon)
    out_ref[...] = (scaled * gain_ref[...].astype(f32)).astype(bf16)


def norm(tokens, gain):
    length, features = tokens.shape
    rows = min(length, 32)
    return pl.pallas_call(
        norm_kernel,
        grid=(length // rows,),
        in_specs=[
            pl.BlockSpec((rows, features), lambda i: (i, 0)),
            pl.BlockSpec((1, features), lambda i: (0, 0)),
        ],
        out_specs=pl.BlockSpec((rows, features), lambda i: (i, 0)),
        out_shape=jax.ShapeDtypeStruct((length, features), bf16),
        compiler_params=pltpu.CompilerParams(vmem_limit_bytes=8 << 20),
        name="norm",
    )(tokens, gain.reshape(1, features))


in_hbm = pl.BlockSpec(memory_space=pltpu.MemorySpace.HBM)
in_vmem = pl.BlockSpec(memory_space=pltpu.MemorySpace.VMEM)
in_smem = pl.BlockSpec(memory_space=pltpu.MemorySpace.SMEM)


def hold(array):
    return pltpu.with_memory_space_constraint(array, pltpu.MemorySpace.HBM)


def kinds_of(pieces):
    return tuple((branch, array.shape[-2]) for array, branch, _ in pieces)


def offsets(pieces):
    return jnp.stack([jnp.asarray(p[2], jnp.int32) for p in pieces])


def spans(kinds):
    start = 0
    for _, depth in kinds:
        yield start, start + depth
        start += depth


def token_copies(kinds, at_ref, x_ref, target, sems):
    copies = []
    for n, (low, high) in enumerate(spans(kinds)):
        columns = pl.ds(pl.multiple_of(at_ref[n], min(high - low, 256)), high - low)
        copies.append(
            pltpu.make_async_copy(x_ref.at[:, columns], target.at[:, low:high], sems.at[n])
        )
    return copies


def weight_copies(kinds, arrays, target, sems):
    copies = []
    for n, (low, high) in enumerate(spans(kinds)):
        branch = kinds[n][0]
        source = arrays[n] if branch is None else arrays[n].at[branch]
        copies.append(pltpu.make_async_copy(source, target.at[low:high], sems.at[n]))
    return copies


def add_up(kinds, width, waits, full, weight, s, first):
    rows = slice(first, None)
    channels = weight.shape[1]
    for n, (low, high) in enumerate(spans(kinds)):
        for copies in waits:
            copies[n].wait()
        for i in range(channels // width):
            columns = slice(i * width, (i + 1) * width)
            term = jnp.dot(
                full[:, low:high], weight[low:high, columns], preferred_element_type=f32
            )
            if n > 0:
                term = s[rows, columns] + term
            if n == len(kinds) - 1 and first is not None:
                term = term.astype(bf16).astype(f32)
            s[rows, columns] = term


def gate_kernel(one, two, three, width, at_ref, x_ref, taps_ref, *rest):
    arrays = rest[: len(one) + len(two) + len(three)]
    gated_ref, head_ref, halo_ref, sum_ref, full, weights, s1, feat, s2, sems = rest[len(arrays) :]
    slab, channels = gated_ref.shape
    count = halo_ref.shape[0] - 2 * edge
    x_copies = token_copies(one, at_ref, x_ref, full, sems.at[0])
    copies = [
        weight_copies(one, arrays[: len(one)], weights.at[0], sems.at[1]),
        weight_copies(two, arrays[len(one) : -len(three)], weights.at[1], sems.at[2]),
        weight_copies(three, arrays[-len(three) :], weights.at[2], sems.at[3]),
    ]
    for x_copy, copy in zip(x_copies, copies[0]):
        x_copy.start()
        copy.start()
    for copy in copies[1] + copies[2]:
        copy.start()
    s1[0:edge] = jnp.zeros((edge, channels), f32)
    add_up(one, width, (x_copies, copies[0]), full, weights.at[0], s1, edge)
    head_ref[0] = s1[edge : 2 * edge].astype(bf16)
    halo_ref[count : count + edge] = s1[slab : slab + edge].astype(bf16)
    feat[...] = short_sum(s1, taps_ref, 1, slab)
    for copy in copies[1]:
        copy.wait()
    s2[0:edge] = jnp.zeros((edge, width), f32)
    for i in range(channels // width):
        columns = slice(i * width, (i + 1) * width)
        term = jnp.dot(full[...], weights[1, :, columns], preferred_element_type=f32)
        s2[edge : edge + slab] = term.astype(bf16).astype(f32)
        head_ref[1, :, columns] = s2[edge : 2 * edge].astype(bf16)
        halo_ref[count + edge :, columns] = s2[slab : slab + edge].astype(bf16)
        gated = feat[:, columns] * short_sum(s2, taps_ref[:, :, columns], 2, slab)
        gated = gated.astype(bf16)
        gated_ref[:, columns] = gated
        halo_ref[0:count, columns] = gated[slab - count :]
    for copy in copies[2]:
        copy.wait()
    depth = list(spans(three))[-1][1]
    for i in range(channels // width):
        columns = slice(i * width, (i + 1) * width)
        sum_ref[:, columns] = jnp.dot(
            full[:, 0:depth], weights[2, 0:depth, columns], preferred_element_type=f32
        )


def gate(x, one, two, three, short_filter, taps, width):
    slab, features = x.shape
    channels = short_filter.shape[-1]
    return pl.pallas_call(
        functools.partial(gate_kernel, kinds_of(one), kinds_of(two), kinds_of(three), width),
        in_specs=[in_smem, in_hbm, in_vmem] + [in_hbm] * (len(one) + len(two) + len(three)),
        out_specs=[in_vmem] * 4,
        out_shape=[
            pltpu.MemorySpace.HBM((slab, channels), bf16),
            pltpu.MemorySpace.HBM((2, edge, channels), bf16),
            pltpu.MemorySpace.HBM((taps + 2 * edge, channels), bf16),
            jax.ShapeDtypeStruct((slab, channels), f32),
        ],
        scratch_shapes=[
            pltpu.VMEM((slab, features), bf16),
            pltpu.VMEM((3, features, channels), bf16),
            pltpu.VMEM((slab + edge, channels), f32),
            pltpu.VMEM((slab, channels), f32),
            pltpu.VMEM((slab + edge, width), f32),
            pltpu.SemaphoreType.DMA((4, len(one))),
        ],
        compiler_params=pltpu.CompilerParams(vmem_limit_bytes=48 << 20),
        name="gate",
    )(offsets(one), hold(x), short_filter, *[hold(p[0]) for p in one + two + three])


def query_kernel(kinds, width, at_ref, x_ref, sum_ref, *rest):
    arrays = rest[: len(kinds)]
    out_ref, tail_ref, full, weight, sems = rest[len(arrays) :]
    slab, channels = out_ref.shape
    x_copies = token_copies(kinds, at_ref, x_ref, full, sems.at[0])
    copies = weight_copies(kinds, arrays, weight, sems.at[1])
    for copy in x_copies + copies:
        copy.start()
    for copy in x_copies + copies:
        copy.wait()
    for i in range(channels // width):
        columns = slice(i * width, (i + 1) * width)
        term = jnp.dot(full[...], weight[:, columns], preferred_element_type=f32)
        out_ref[:, columns] = (sum_ref[:, columns] + term).astype(bf16)
    tail_ref[...] = out_ref[slab - edge :]


def query(x, pieces, total, width):
    slab, channels = total.shape
    kinds = kinds_of(pieces)
    depth = sum(k[1] for k in kinds)
    return pl.pallas_call(
        functools.partial(query_kernel, kinds, width),
        in_specs=[in_smem, in_hbm, in_vmem] + [in_hbm] * len(pieces),
        out_specs=[in_vmem] * 2,
        out_shape=[
            jax.ShapeDtypeStruct((slab, channels), bf16),
            pltpu.MemorySpace.HBM((edge, channels), bf16),
        ],
        scratch_shapes=[
            pltpu.VMEM((slab, depth), bf16),
            pltpu.VMEM((depth, channels), bf16),
            pltpu.SemaphoreType.DMA((2, len(pieces))),
        ],
        compiler_params=pltpu.CompilerParams(vmem_limit_bytes=16 << 20),
        name="query",
    )(offsets(pieces), hold(x), total, *[hold(p[0]) for p in pieces])


def combine_kernel(projected_ref, before_ref, taps_ref, mixed_ref, out_ref, s):
    slab = out_ref.shape[0]
    s[0:edge] = before_ref[...].astype(f32)
    s[edge : edge + slab] = projected_ref[...].astype(f32)
    out_ref[...] = (short_sum(s, taps_ref, 0, slab) * mixed_ref[...]).astype(bf16)


def combine(projected, before, short_filter, mixed, width):
    slab, channels = mixed.shape
    col = lambda rows: pl.BlockSpec((rows, width), lambda i: (0, i))
    return pl.pallas_call(
        combine_kernel,
        grid=(channels // width,),
        in_specs=[
            col(slab),
            col(edge),
            pl.BlockSpec(short_filter.shape[:2] + (width,), lambda i: (0, 0, i)),
            col(slab),
        ],
        out_specs=col(slab),
        out_shape=jax.ShapeDtypeStruct((slab, channels), bf16),
        scratch_shapes=[pltpu.VMEM((slab + edge, width), f32)],
        compiler_params=pltpu.CompilerParams(vmem_limit_bytes=16 << 20),
        name="combine",
    )(projected, before, short_filter, mixed)


def transform(fwd_ref, block):
    return jnp.dot(fwd_ref[...], jnp.concatenate([block, block], axis=0), preferred_element_type=f32)


def respond_kernel(filter_ref, decay_ref, fwd_ref, out_ref):
    taps = filter_ref.shape[0]
    lag = lax.broadcasted_iota(jnp.int32, (taps, 1), 0)
    faded = filter_ref[...] * jnp.exp(-decay_ref[...] * lag.astype(f32))
    response = transform(fwd_ref, faded.astype(bf16))
    h_cos, h_sin = response[:taps], response[taps:]
    out_ref[0] = h_cos
    out_ref[1] = jnp.where(lag == 0, 0.0, h_sin)
    out_ref[2] = jnp.where(lag == 0, h_sin, h_cos)


def respond(medium_filter, decay, forward, width):
    taps, channels = medium_filter.shape
    return pl.pallas_call(
        respond_kernel,
        grid=(channels // width,),
        in_specs=[
            pl.BlockSpec((taps, width), lambda i: (0, i)),
            pl.BlockSpec((1, width), lambda i: (0, i)),
            pl.BlockSpec(forward.shape, lambda i: (0, 0)),
        ],
        out_specs=pl.BlockSpec((3, taps, width), lambda i: (0, 0, i)),
        out_shape=pltpu.MemorySpace.HBM((3, taps, channels), f32),
        compiler_params=pltpu.CompilerParams(vmem_limit_bytes=8 << 20),
        name="respond",
    )(medium_filter, decay.reshape(1, channels), forward)


def mix_kernel(
    gated_ref, halo_ref, head_ref, short_ref, response_ref, fwd_ref, inv_ref, out_ref, s
):
    taps = response_ref.shape[1]
    blocks = gated_ref.shape[0] // taps
    feats = []
    for k in range(2):
        s[0:edge] = halo_ref[taps + k * edge : taps + (k + 1) * edge].astype(f32)
        s[edge : 2 * edge] = head_ref[k].astype(f32)
        total = None
        for lag in range(short_ref.shape[0]):
            term = short_ref[lag, k + 1][None] * s[edge - lag : 2 * edge - lag]
            total = term if total is None else total + term
        feats.append(total)
    first = (feats[0] * feats[1]).astype(bf16)

    row = lax.broadcasted_iota(jnp.int32, (2 * taps, 1), 0)
    sign = jnp.where(row % 2 == 0, 1.0, -1.0).astype(f32)
    h_cos, h_sin, h_low = response_ref[0], response_ref[1], response_ref[2]
    last = transform(fwd_ref, halo_ref[0:taps])
    for b in range(blocks):
        if b == 0:
            block = jnp.concatenate([first, gated_ref[edge:taps]], axis=0)
        else:
            block = gated_ref[b * taps : (b + 1) * taps]
        now = transform(fwd_ref, block)
        x = last + sign * now
        last = now
        x_cos, x_sin = x[:taps], x[taps:]
        y = jnp.concatenate([x_cos * h_cos - x_sin * h_sin, x_sin * h_low + x_cos * h_sin], axis=0)
        high = y.astype(bf16)
        low = (y - high.astype(f32)).astype(bf16)
        out_ref[b * taps : (b + 1) * taps] = jnp.dot(
            inv_ref[...], jnp.concatenate([high, low, high], axis=0), preferred_element_type=f32
        )


def mix(gated, halo, head, short_filter, response, tables, width):
    slab, channels = gated.shape
    count = response.shape[1]
    forward, inverse = tables
    col = lambda rows: pl.BlockSpec((rows, width), lambda i: (0, i))
    cube = lambda a, b: pl.BlockSpec((a, b, width), lambda i: (0, 0, i))
    return pl.pallas_call(
        mix_kernel,
        grid=(channels // width,),
        in_specs=[
            col(slab),
            col(count + 2 * edge),
            cube(2, edge),
            cube(*short_filter.shape[:2]),
            cube(3, count),
            pl.BlockSpec(forward.shape, lambda i: (0, 0)),
            pl.BlockSpec(inverse.shape, lambda i: (0, 0)),
        ],
        out_specs=col(slab),
        out_shape=jax.ShapeDtypeStruct((slab, channels), f32),
        scratch_shapes=[pltpu.VMEM((2 * edge, width), f32)],
        compiler_params=pltpu.CompilerParams(vmem_limit_bytes=16 << 20),
        name="mix",
    )(hold(gated), hold(halo), hold(head), short_filter, hold(response), forward, inverse)


def local(tokens, norm_gain, w_in, short_filter, medium_filter, decay, w_out):
    groups, contexts, count = (lax.axis_size(a) for a in axes)
    g, c, z = (lax.axis_index(a) for a in axes)
    length, features = tokens.shape
    rows, branches, channels = w_in.shape
    slab = length * count
    width = min(channels, 256)
    paired = contexts == 4 and groups == 2

    def move(value, target):
        pairs = []
        for i in range(groups):
            for j in range(contexts):
                for k in range(count):
                    to = target(i, j, k)
                    if 0 <= to[1] < contexts and 0 <= to[2] < count:
                        pairs.append(
                            ((i * contexts + j) * count + k, (to[0] * contexts + to[1]) * count + to[2])
                        )
        return lax.ppermute(value, axes, pairs)

    to_chip = lambda v: move(v, lambda i, j, k: (i, j ^ 2, k))
    to_core = lambda v: move(v, lambda i, j, k: (i, j ^ 1, k))
    to_group = lambda v: move(v, lambda i, j, k: (1 - i, j, k))
    to_next = lambda v: move(v, lambda i, j, k: (i, j + 1, k))
    send = lambda v, pairs: move(v, lambda i, j, k: (i, j, pairs.get(k, -1)))
    to_up = lambda v: move(v, lambda i, j, k: (i, j, k + 1))
    to_down = lambda v: move(v, lambda i, j, k: (i, j, k - 1))

    def after(value, *earlier):
        return lax.optimization_barrier((value, *earlier))[0]

    medium_count = medium_filter.shape[0]
    tables = fourier_tables(medium_count)
    weights = jnp.transpose(w_in, (1, 0, 2))
    half = rows // 2
    out_rows = w_out.shape[0]
    if paired:
        first_half, other_half = g * half, (1 - g) * half
        peer = to_core(weights)
        near, far, pieces = {}, {}, {}
        def cut(source, b, first, depth):
            part = lax.dynamic_slice(source, (b, first, 0), (1, depth, channels))
            return part.reshape(depth, channels)

        mine = cut(weights, 1, first_half, half)
        normed = norm(after(tokens, mine), norm_gain)
        response = respond(medium_filter, decay, tables[0], width)
        near[1] = to_chip(mine)
        far[1] = to_group(near[1])
        source = after(weights, normed)
        near[2] = to_chip(after(cut(source, 2, first_half, half), near[1]))
        far[2] = to_group(after(near[2], far[1], response, peer))
        near[0] = to_chip(after(cut(source, 0, first_half, half), near[2]))
        far[0] = to_group(after(near[0], far[2]))
        for b in (1, 2, 0):
            pieces[b] = [
                (weights, b, c * rows),
                (peer, b, (c ^ 1) * rows),
                (near[b], None, (c ^ 2) * rows + first_half),
                (to_core(near[b]), None, (c ^ 3) * rows + first_half),
                (far[b], None, (c ^ 2) * rows + other_half),
            ]
            if b != 0:
                late = after(far[2], near[0]) if b == 2 else far[1]
                pieces[b].append((to_core(late), None, (c ^ 3) * rows + other_half))
    else:
        normed = norm(tokens, norm_gain)
        response = respond(medium_filter, decay, tables[0], width)
        full = lax.all_gather(weights, "context", axis=1, tiled=True)
        pieces = {b: [(full, b, 0)] for b in (1, 2)}
        middle = features // 2
        pieces[0] = [(full[0, :middle], None, 0), (full[0, middle:], None, middle)]

    gathered = lax.all_gather(normed, "tensor", axis=0, tiled=True)
    gate_taps = after(short_filter, response)
    gated, head, edges, total = gate(
        gathered, pieces[1], pieces[2], pieces[0][:-1], gate_taps, medium_count, width
    )
    halo = to_next(edges)
    late = pieces[0][-1:]
    if paired:
        late.append((to_core(after(far[0], halo)), None, (c ^ 3) * rows + other_half))
    projected, tail = query(gathered, late, total, width)
    before = to_next(tail)
    mixed = mix(gated, halo, head, short_filter, response, tables, width)
    combined = combine(projected, before, short_filter, mixed, width)
    if paired:
        out_full = lax.all_gather(after(w_out, near[1]), "context", axis=0, tiled=True)
        out_peer = to_core(after(w_out, tail))
        part = lambda i: lax.dynamic_slice(out_full, ((c ^ i) * out_rows, 0), (out_rows, channels))
        sets = [w_out, out_peer, part(2), part(3)]
    else:
        sets = [lax.all_gather(w_out, "context", axis=0, tiled=True)]

    def plus(*terms):
        total = terms[0].astype(f32)
        for term in terms[1:]:
            total = total + term.astype(f32)
        return total.astype(bf16)

    def product(rows_out):
        return lax.dot_general(
            combined, rows_out, (((1,), (1,)), ((), ())), preferred_element_type=f32
        ).astype(bf16)

    results = []
    for rows_out in sets:
        partial = product(rows_out)
        combined = after(combined, partial)

        def block(index, blocks=1, partial=partial):
            index = jnp.clip(index, 0, count - blocks)
            return lax.dynamic_slice(
                partial, (index * length, 0), (blocks * length, partial.shape[1])
            )

        if count == 4:
            far_pair = block(jnp.where(z < 2, 2, 0), 2)
            got = plus(far_pair, send(far_pair, {0: 1, 3: 2}))
            got = send(got, {1: 2, 2: 1})
            low, high = got[:length], got[length:]
            odd = z % 2 == 1
            got_own = jnp.where(odd, high, low)
            got_other = jnp.where(odd, low, high)
            last = send(plus(block(z ^ 1), got_other), {0: 1, 1: 0, 2: 3, 3: 2})
            results.append(plus(block(z), got_own, last))
        else:
            up = down = None
            for s in range(1, count):
                rising = block(count + z - s)
                falling = block(z - count + s)
                if up is not None:
                    rising, falling = plus(rising, up), plus(falling, down)
                up, down = to_up(rising), to_down(falling)
            results.append(plus(block(z), up, down))
    if not paired:
        return results[0]
    swap = lambda test, a, b: (jnp.where(test, b, a), jnp.where(test, a, b))
    e0, e1, e2, e3 = results
    odd = c % 2 == 1
    low = jnp.concatenate(swap(odd, e0, e1), 1)
    high = jnp.concatenate(swap(odd, e2, e3), 1)
    return jnp.concatenate(swap(c >= 2, low, high), 1)


def solution(mesh):
    in_specs = (
        P(axes, None),
        P(),
        P("context", None, "tensor"),
        P(None, None, "tensor"),
        P(None, "tensor"),
        P("tensor"),
        P("context", "tensor"),
    )
    return jax.shard_map(
        local, mesh=mesh, in_specs=in_specs, out_specs=P(axes, None), check_vma=False
    )
```

```python
import functools
import jax
import jax.numpy as jnp
import ml_dtypes
import numpy as np
from jax import lax
from jax.experimental import pallas as pl
from jax.experimental.pallas import tpu as pltpu
from jax.sharding import PartitionSpec as P

norm_epsilon = 1e-06
axes = ("groups", "context", "tensor")
edge = 16
f32 = jnp.float32
bf16 = jnp.bfloat16


def split_parts(matrix):
    high = matrix.astype(ml_dtypes.bfloat16)
    low = (matrix - high.astype(np.float64)).astype(ml_dtypes.bfloat16)
    return high, low


def fourier_tables(taps):
    size = 2 * taps
    freq = np.arange(taps)[:, None]
    time = np.arange(size)[None, :]
    angle = 2 * np.pi * ((freq * time) % size) / size
    cosine, sine = np.cos(angle), np.sin(angle)
    sine[0] = 1.0 - 2.0 * (np.arange(size) % 2)
    forward = np.concatenate([cosine, sine], axis=0)
    weight = np.full((2 * taps, 1), 2.0 / size)
    weight[0] = weight[taps] = 1.0 / size
    inverse = (forward * weight)[:, taps:].T
    fh, fl = split_parts(forward[:, :taps])
    ih, il = split_parts(inverse)
    return np.concatenate([fh, fl], axis=1), np.concatenate([ih, ih, il], axis=1)


def short_sum(s, taps_ref, branch, slab):
    total = None
    for lag in range(taps_ref.shape[0]):
        term = taps_ref[lag, branch][None] * s[edge - lag : edge - lag + slab]
        total = term if total is None else total + term
    return total


def norm_kernel(x_ref, gain_ref, out_ref):
    values = x_ref[...].astype(f32)
    mean = jnp.mean(values * values, axis=1, keepdims=True)
    scaled = values * lax.rsqrt(mean + norm_epsilon)
    out_ref[...] = (scaled * gain_ref[...].astype(f32)).astype(bf16)


def norm(tokens, gain):
    length, features = tokens.shape
    rows = min(length, 32)
    return pl.pallas_call(
        norm_kernel,
        grid=(length // rows,),
        in_specs=[
            pl.BlockSpec((rows, features), lambda i: (i, 0)),
            pl.BlockSpec((1, features), lambda i: (0, 0)),
        ],
        out_specs=pl.BlockSpec((rows, features), lambda i: (i, 0)),
        out_shape=jax.ShapeDtypeStruct((length, features), bf16),
        compiler_params=pltpu.CompilerParams(vmem_limit_bytes=8 << 20),
        name="norm",
    )(tokens, gain.reshape(1, features))


in_hbm = pl.BlockSpec(memory_space=pltpu.MemorySpace.HBM)
in_vmem = pl.BlockSpec(memory_space=pltpu.MemorySpace.VMEM)
in_smem = pl.BlockSpec(memory_space=pltpu.MemorySpace.SMEM)


def hold(array):
    return pltpu.with_memory_space_constraint(array, pltpu.MemorySpace.HBM)


def kinds_of(pieces):
    return tuple((branch, array.shape[-2]) for array, branch, _ in pieces)


def offsets(pieces):
    return jnp.stack([jnp.asarray(p[2], jnp.int32) for p in pieces])


def spans(kinds):
    start = 0
    for _, depth in kinds:
        yield start, start + depth
        start += depth


def token_copies(kinds, at_ref, x_ref, target, sems):
    copies = []
    for n, (low, high) in enumerate(spans(kinds)):
        columns = pl.ds(pl.multiple_of(at_ref[n], min(high - low, 256)), high - low)
        copies.append(
            pltpu.make_async_copy(x_ref.at[:, columns], target.at[:, low:high], sems.at[n])
        )
    return copies


def weight_copies(kinds, arrays, target, sems):
    copies = []
    for n, (low, high) in enumerate(spans(kinds)):
        branch = kinds[n][0]
        source = arrays[n] if branch is None else arrays[n].at[branch]
        copies.append(pltpu.make_async_copy(source, target.at[low:high], sems.at[n]))
    return copies


def add_up(kinds, width, waits, full, weight, s, first):
    channels = weight.shape[1]
    for n, (low, high) in enumerate(spans(kinds)):
        for copies in waits:
            copies[n].wait()
        for i in range(channels // width):
            columns = slice(i * width, (i + 1) * width)
            term = jnp.dot(
                full[:, low:high], weight[low:high, columns], preferred_element_type=f32
            )
            if n > 0:
                term = s[first:, columns] + term
            if n == len(kinds) - 1:
                term = term.astype(bf16).astype(f32)
            s[first:, columns] = term


def gate_kernel(one, two, width, at_ref, x_ref, taps_ref, *rest):
    arrays = rest[: len(one) + len(two)]
    gated_ref, head_ref, halo_ref, full, weights, s1, feat, s2, sems = rest[len(arrays) :]
    slab, channels = gated_ref.shape
    count = halo_ref.shape[0] - 2 * edge
    x_copies = token_copies(one, at_ref, x_ref, full, sems.at[0])
    copies = [
        weight_copies(one, arrays[: len(one)], weights.at[0], sems.at[1]),
        weight_copies(two, arrays[len(one) :], weights.at[1], sems.at[2]),
    ]
    for x_copy, copy in zip(x_copies, copies[0]):
        x_copy.start()
        copy.start()
    for copy in copies[1]:
        copy.start()
    s1[0:edge] = jnp.zeros((edge, channels), f32)
    add_up(one, width, (x_copies, copies[0]), full, weights.at[0], s1, edge)
    head_ref[0] = s1[edge : 2 * edge].astype(bf16)
    halo_ref[count : count + edge] = s1[slab : slab + edge].astype(bf16)
    feat[...] = short_sum(s1, taps_ref, 1, slab)
    for copy in copies[1]:
        copy.wait()
    s2[0:edge] = jnp.zeros((edge, width), f32)
    for i in range(channels // width):
        columns = slice(i * width, (i + 1) * width)
        term = jnp.dot(full[...], weights[1, :, columns], preferred_element_type=f32)
        s2[edge : edge + slab] = term.astype(bf16).astype(f32)
        head_ref[1, :, columns] = s2[edge : 2 * edge].astype(bf16)
        halo_ref[count + edge :, columns] = s2[slab : slab + edge].astype(bf16)
        gated = feat[:, columns] * short_sum(s2, taps_ref[:, :, columns], 2, slab)
        gated = gated.astype(bf16)
        gated_ref[:, columns] = gated
        halo_ref[0:count, columns] = gated[slab - count :]


def gate(x, one, two, short_filter, taps, width):
    slab, features = x.shape
    channels = short_filter.shape[-1]
    return pl.pallas_call(
        functools.partial(gate_kernel, kinds_of(one), kinds_of(two), width),
        in_specs=[in_smem, in_hbm, in_vmem] + [in_hbm] * (len(one) + len(two)),
        out_specs=[in_vmem] * 3,
        out_shape=[
            pltpu.MemorySpace.HBM((slab, channels), bf16),
            pltpu.MemorySpace.HBM((2, edge, channels), bf16),
            pltpu.MemorySpace.HBM((taps + 2 * edge, channels), bf16),
        ],
        scratch_shapes=[
            pltpu.VMEM((slab, features), bf16),
            pltpu.VMEM((2, features, channels), bf16),
            pltpu.VMEM((slab + edge, channels), f32),
            pltpu.VMEM((slab, channels), f32),
            pltpu.VMEM((slab + edge, width), f32),
            pltpu.SemaphoreType.DMA((3, len(one))),
        ],
        compiler_params=pltpu.CompilerParams(vmem_limit_bytes=40 << 20),
        name="gate",
    )(offsets(one), hold(x), short_filter, *[hold(p[0]) for p in one + two])


def query_kernel(kinds, width, at_ref, x_ref, before_ref, taps_ref, *rest):
    arrays = rest[: len(kinds)]
    out_ref, full, weight, s, sems = rest[len(arrays) :]
    slab, channels = out_ref.shape
    x_copies = token_copies(kinds, at_ref, x_ref, full.at[edge : edge + slab], sems.at[0])
    e_copies = token_copies(kinds, at_ref, before_ref, full.at[0:edge], sems.at[1])
    copies = weight_copies(kinds, arrays, weight, sems.at[2])
    for group in zip(e_copies, x_copies, copies):
        for copy in group:
            copy.start()
    add_up(kinds, width, (e_copies, x_copies, copies), full, weight, s, 0)
    out_ref[...] = short_sum(s, taps_ref, 0, slab)


def query(x, before, pieces, short_filter, width):
    slab, features = x.shape
    channels = short_filter.shape[-1]
    return pl.pallas_call(
        functools.partial(query_kernel, kinds_of(pieces), width),
        in_specs=[in_smem, in_hbm, in_hbm, in_vmem] + [in_hbm] * len(pieces),
        out_specs=in_vmem,
        out_shape=jax.ShapeDtypeStruct((slab, channels), f32),
        scratch_shapes=[
            pltpu.VMEM((slab + edge, features), bf16),
            pltpu.VMEM((features, channels), bf16),
            pltpu.VMEM((slab + edge, channels), f32),
            pltpu.SemaphoreType.DMA((3, len(pieces))),
        ],
        compiler_params=pltpu.CompilerParams(vmem_limit_bytes=32 << 20),
        name="query",
    )(offsets(pieces), hold(x), hold(before), short_filter, *[hold(p[0]) for p in pieces])


def transform(fwd_ref, block):
    return jnp.dot(fwd_ref[...], jnp.concatenate([block, block], axis=0), preferred_element_type=f32)


def respond_kernel(filter_ref, decay_ref, fwd_ref, out_ref):
    taps = filter_ref.shape[0]
    lag = lax.broadcasted_iota(jnp.int32, (taps, 1), 0)
    faded = filter_ref[...] * jnp.exp(-decay_ref[...] * lag.astype(f32))
    response = transform(fwd_ref, faded.astype(bf16))
    h_cos, h_sin = response[:taps], response[taps:]
    out_ref[0] = h_cos
    out_ref[1] = jnp.where(lag == 0, 0.0, h_sin)
    out_ref[2] = jnp.where(lag == 0, h_sin, h_cos)


def respond(medium_filter, decay, forward, width):
    taps, channels = medium_filter.shape
    return pl.pallas_call(
        respond_kernel,
        grid=(channels // width,),
        in_specs=[
            pl.BlockSpec((taps, width), lambda i: (0, i)),
            pl.BlockSpec((1, width), lambda i: (0, i)),
            pl.BlockSpec(forward.shape, lambda i: (0, 0)),
        ],
        out_specs=pl.BlockSpec((3, taps, width), lambda i: (0, 0, i)),
        out_shape=pltpu.MemorySpace.HBM((3, taps, channels), f32),
        compiler_params=pltpu.CompilerParams(vmem_limit_bytes=8 << 20),
        name="respond",
    )(medium_filter, decay.reshape(1, channels), forward)


def mix_kernel(
    gated_ref, halo_ref, head_ref, short_ref, response_ref, query_ref, fwd_ref, inv_ref, out_ref, s
):
    taps = response_ref.shape[1]
    blocks = gated_ref.shape[0] // taps
    feats = []
    for k in range(2):
        s[0:edge] = halo_ref[taps + k * edge : taps + (k + 1) * edge].astype(f32)
        s[edge : 2 * edge] = head_ref[k].astype(f32)
        total = None
        for lag in range(short_ref.shape[0]):
            term = short_ref[lag, k + 1][None] * s[edge - lag : 2 * edge - lag]
            total = term if total is None else total + term
        feats.append(total)
    first = (feats[0] * feats[1]).astype(bf16)

    row = lax.broadcasted_iota(jnp.int32, (2 * taps, 1), 0)
    sign = jnp.where(row % 2 == 0, 1.0, -1.0).astype(f32)
    h_cos, h_sin, h_low = response_ref[0], response_ref[1], response_ref[2]
    last = transform(fwd_ref, halo_ref[0:taps])
    for b in range(blocks):
        if b == 0:
            block = jnp.concatenate([first, gated_ref[edge:taps]], axis=0)
        else:
            block = gated_ref[b * taps : (b + 1) * taps]
        now = transform(fwd_ref, block)
        x = last + sign * now
        last = now
        x_cos, x_sin = x[:taps], x[taps:]
        y = jnp.concatenate([x_cos * h_cos - x_sin * h_sin, x_sin * h_low + x_cos * h_sin], axis=0)
        high = y.astype(bf16)
        low = (y - high.astype(f32)).astype(bf16)
        mixed = jnp.dot(
            inv_ref[...], jnp.concatenate([high, low, high], axis=0), preferred_element_type=f32
        )
        at = slice(b * taps, (b + 1) * taps)
        out_ref[at] = (query_ref[at] * mixed).astype(bf16)


def mix(gated, halo, head, short_filter, response, query_rows, tables, width):
    slab, channels = gated.shape
    count = response.shape[1]
    forward, inverse = tables
    col = lambda rows: pl.BlockSpec((rows, width), lambda i: (0, i))
    cube = lambda a, b: pl.BlockSpec((a, b, width), lambda i: (0, 0, i))
    return pl.pallas_call(
        mix_kernel,
        grid=(channels // width,),
        in_specs=[
            col(slab),
            col(count + 2 * edge),
            cube(2, edge),
            cube(*short_filter.shape[:2]),
            cube(3, count),
            col(slab),
            pl.BlockSpec(forward.shape, lambda i: (0, 0)),
            pl.BlockSpec(inverse.shape, lambda i: (0, 0)),
        ],
        out_specs=col(slab),
        out_shape=jax.ShapeDtypeStruct((slab, channels), bf16),
        scratch_shapes=[pltpu.VMEM((2 * edge, width), f32)],
        compiler_params=pltpu.CompilerParams(vmem_limit_bytes=16 << 20),
        name="mix",
    )(hold(gated), hold(halo), hold(head), short_filter, hold(response), query_rows, forward, inverse)


def local(tokens, norm_gain, w_in, short_filter, medium_filter, decay, w_out):
    groups, contexts, count = (lax.axis_size(a) for a in axes)
    g, c, z = (lax.axis_index(a) for a in axes)
    length, features = tokens.shape
    rows, branches, channels = w_in.shape
    slab = length * count
    width = min(channels, 256)
    paired = contexts == 4 and groups == 2

    def move(value, target):
        pairs = []
        for i in range(groups):
            for j in range(contexts):
                for k in range(count):
                    to = target(i, j, k)
                    if 0 <= to[1] < contexts and 0 <= to[2] < count:
                        pairs.append(
                            ((i * contexts + j) * count + k, (to[0] * contexts + to[1]) * count + to[2])
                        )
        return lax.ppermute(value, axes, pairs)

    to_chip = lambda v: move(v, lambda i, j, k: (i, j ^ 2, k))
    to_core = lambda v: move(v, lambda i, j, k: (i, j ^ 1, k))
    to_group = lambda v: move(v, lambda i, j, k: (1 - i, j, k))
    to_next = lambda v: move(v, lambda i, j, k: (i, j + 1, k))
    send = lambda v, pairs: move(v, lambda i, j, k: (i, j, pairs.get(k, -1)))
    to_up = lambda v: move(v, lambda i, j, k: (i, j, k + 1))
    to_down = lambda v: move(v, lambda i, j, k: (i, j, k - 1))

    def after(value, *earlier):
        return lax.optimization_barrier((value, *earlier))[0]

    medium_count = medium_filter.shape[0]
    tables = fourier_tables(medium_count)
    weights = jnp.transpose(w_in, (1, 0, 2))
    half = rows // 2
    out_rows = w_out.shape[0]
    if paired:
        first_half, other_half = g * half, (1 - g) * half
        peer = to_core(weights)
        near, far, pieces = {}, {}, {}
        def cut(source, b, first, depth):
            part = lax.dynamic_slice(source, (b, first, 0), (1, depth, channels))
            return part.reshape(depth, channels)

        mine = cut(weights, 1, first_half, half)
        normed = norm(after(tokens, mine), norm_gain)
        response = respond(medium_filter, decay, tables[0], width)
        near[1] = to_chip(mine)
        far[1] = to_group(near[1])
        source = after(weights, normed)
        near[2] = to_chip(after(cut(source, 2, first_half, half), near[1]))
        far[2] = to_group(after(near[2], far[1], response, peer))
        near[0] = to_chip(after(cut(source, 0, first_half, half), near[2]))
        far[0] = to_group(after(near[0], far[2]))
        for b in (1, 2, 0):
            pieces[b] = [
                (weights, b, c * rows),
                (peer, b, (c ^ 1) * rows),
                (near[b], None, (c ^ 2) * rows + first_half),
                (to_core(near[b]), None, (c ^ 3) * rows + first_half),
                (far[b], None, (c ^ 2) * rows + other_half),
            ]
            if b != 0:
                late = after(far[2], near[0]) if b == 2 else far[1]
                pieces[b].append((to_core(late), None, (c ^ 3) * rows + other_half))
    else:
        normed = norm(tokens, norm_gain)
        response = respond(medium_filter, decay, tables[0], width)
        full = lax.all_gather(weights, "context", axis=1, tiled=True)
        pieces = {b: [(full, b, 0)] for b in range(branches)}

    gathered = lax.all_gather(normed, "tensor", axis=0, tiled=True)
    gate_taps = after(short_filter, response)
    gated, head, edges = gate(gathered, pieces[1], pieces[2], gate_taps, medium_count, width)
    before_rows = to_next(after(gathered[slab - edge :], gated))
    halo = to_next(after(edges, before_rows))
    if paired:
        last = to_core(after(far[0], before_rows))
        pieces[0].append((last, None, (c ^ 3) * rows + other_half))
    query_rows = query(gathered, before_rows, pieces[0], short_filter, width)
    combined = mix(gated, halo, head, short_filter, response, query_rows, tables, width)
    if paired:
        out_full = lax.all_gather(after(w_out, near[1]), "context", axis=0, tiled=True)
        out_peer = to_core(after(w_out, gated))
        part = lambda i: lax.dynamic_slice(out_full, ((c ^ i) * out_rows, 0), (out_rows, channels))
        sets = [w_out, out_peer, part(2), part(3)]
    else:
        sets = [lax.all_gather(w_out, "context", axis=0, tiled=True)]

    def plus(*terms):
        total = terms[0].astype(f32)
        for term in terms[1:]:
            total = total + term.astype(f32)
        return total.astype(bf16)

    def product(rows_out):
        return lax.dot_general(
            combined, rows_out, (((1,), (1,)), ((), ())), preferred_element_type=f32
        ).astype(bf16)

    results, firsts, seconds = [], [], []
    for n, rows_out in enumerate(sets):
        if paired and n == 2:
            combined = after(combined, firsts[0])
        partial = product(rows_out)
        combined = after(combined, partial)

        def block(index, blocks=1, partial=partial):
            index = jnp.clip(index, 0, count - blocks)
            return lax.dynamic_slice(
                partial, (index * length, 0), (blocks * length, partial.shape[1])
            )

        if count == 4:
            far_pair = block(jnp.where(z < 2, 2, 0), 2)
            firsts.append(send(far_pair, {0: 1, 3: 2}))
            got = plus(far_pair, firsts[-1])
            if n >= 2:
                got = after(got, seconds[n - 2])
            got = send(got, {1: 2, 2: 1})
            seconds.append(got)
            low, high = got[:length], got[length:]
            odd = z % 2 == 1
            got_own = jnp.where(odd, high, low)
            got_other = jnp.where(odd, low, high)
            last = send(plus(block(z ^ 1), got_other), {0: 1, 1: 0, 2: 3, 3: 2})
            results.append(plus(block(z), got_own, last))
        else:
            up = down = None
            for s in range(1, count):
                rising = block(count + z - s)
                falling = block(z - count + s)
                if up is not None:
                    rising, falling = plus(rising, up), plus(falling, down)
                up, down = to_up(rising), to_down(falling)
            results.append(plus(block(z), up, down))
    if not paired:
        return results[0]
    swap = lambda test, a, b: (jnp.where(test, b, a), jnp.where(test, a, b))
    e0, e1, e2, e3 = results
    odd = c % 2 == 1
    low = jnp.concatenate(swap(odd, e0, e1), 1)
    high = jnp.concatenate(swap(odd, e2, e3), 1)
    return jnp.concatenate(swap(c >= 2, low, high), 1)


def solution(mesh):
    in_specs = (
        P(axes, None),
        P(),
        P("context", None, "tensor"),
        P(None, None, "tensor"),
        P(None, "tensor"),
        P("tensor"),
        P("context", "tensor"),
    )
    return jax.shard_map(
        local, mesh=mesh, in_specs=in_specs, out_specs=P(axes, None), check_vma=False
    )
```
